128 devices in a mesh: win: 16 (over y, x_hi, core), tile: 8 (over x_lo, z).
Axes of the slice: x: 4 (x_hi: 2, x_lo: 2; x = x_hi * 2 + x_lo), y: 4, z: 4, core: 2. Of those that a mesh axis runs over, the one named last changes fastest.
Arguments:
- flux: bfloat16 [3840, 65536], P('win', 'tile'), may hold values from -6 to 6
- prior_std: float32 [3840, 65536], P('win', 'tile'), may hold values from 0.3 to 3
- footprint: bfloat16 [16384, 128, 128], P('win', 'tile'), may hold values from 0.0099487305 to 1
- obs_value: float32 [16384], P('win'), may hold values from -180 to 180
- obs_weight: float32 [16384], P('win'), may hold values from 0.002 to 0.02
- obs_hour: int32 [16384], P('win'), may hold values from 0 to 239
- hour_offset: int32 [16384, 128], P('win', 'tile'), may hold values from 0 to 239
- block_cell: int32 [16384, 128], P('win', 'tile'), may hold values from 0 to 63
Outputs:
- gradient: float32 [3840, 65536], P('win', 'tile')
The draws below stay inside these ranges and needn't reach their ends.
Inputs may be any that keep to these rules, and one draw needn't show every extreme that they name: `block_cell`: index of a block of 128 cells within the tile.
All inputs are finite; a program needn't handle non-finite values.
Results may differ from the reference program's by a relative error of at most 0.0003.
Values may be sent and summed in bfloat16 or wider, within the bound.
A program may use at most 128 MiB of HBM per device.

```python
import math
import jax
import jax.numpy as jnp
from jax import lax

HB = 240
BS = 128
NBT = 16
KH = 24
CD = 8192
OBS_DEV = 1024
BPT = 64
NH = 3840
CELLS = 65536
OBS = 16384
NB = 128
N_WIN = 16
N_TILE = 8


def plant(entries, stream_key, low, high):
    longest = entries.shape.index(max(entries.shape))
    spots = []
    for shift in (0, 1):
        where = [jax.random.randint(jax.random.fold_in(stream_key, axis), (), 0, length) for axis, length in enumerate(entries.shape)]
        where[longest] = (where[longest] + shift) % entries.shape[longest]
        spots.append(tuple(where))
    return entries.at[spots[0]].set(low).at[spots[1]].set(high)


def block_levels(key, dims, split, low, largest):
    level, own = 1.0, jax.random.fold_in(key, 6)
    for axis_at, blocks in split:
        steps = jnp.exp(jax.random.uniform(jax.random.fold_in(own, axis_at), (blocks,), jnp.float32, low / len(split), largest / len(split)))
        level = level * jnp.repeat(steps, dims[axis_at] // blocks).reshape([-1 if axis == axis_at else 1 for axis in range(len(dims))])
    return level


def scatter_about(rng, shape, width, bound, cuts=(), kind=jnp.bfloat16):
    result = jax.random.normal(rng, shape, jnp.float32) * width
    if len(cuts) > 0:
        result = block_levels(rng, shape, cuts, -0.22, 0.18) * result
    return jnp.clip(result, min=-bound, max=bound).astype(kind)


def setup_inputs(seed: int = 0) -> dict:
    splits = jax.random.split(jax.random.key(seed), 9)
    return {
        "flux": scatter_about(splits[0], (NH, CELLS), 1.0, 6.0, ((0, 16), (1, 8))),
        "prior_std": jnp.clip(jnp.exp(math.log(3.0) - 2.3025851 * jax.random.uniform(splits[1], (NH, CELLS), jnp.float32) ** block_levels(splits[1], (NH, CELLS), ((0, 16), (1, 8)), -0.2, 0.2)), 0.3, 3.0),
        "footprint": jnp.clip(jnp.exp(math.log(1.0) - 4.61031033 * jax.random.uniform(splits[2], (OBS, NB, BS), jnp.float32) ** block_levels(splits[2], (OBS, NB, BS), ((0, 16), (1, 8)), -0.2, 0.2)), 0.0099487305, 1.0).astype(jnp.bfloat16),
        "obs_value": scatter_about(splits[3], (OBS,), 30.0, 180.0, ((0, 16),), jnp.float32),
        "obs_weight": jnp.clip(jnp.exp(math.log(0.02) - 2.30258502 * jax.random.uniform(splits[4], (OBS,), jnp.float32) ** block_levels(splits[4], (OBS,), ((0, 16),), -0.2, 0.2)), 0.002, 0.02),
        "obs_hour": plant(jax.random.randint(splits[5], (OBS,), 0, HB), jax.random.fold_in(splits[5], 1), 0, HB - 1).astype(jnp.int32),
        "hour_offset": plant(jax.random.randint(splits[6], (OBS, NB), 0, HB), jax.random.fold_in(splits[6], 1), 0, HB - 1).astype(jnp.int32),
        "block_cell": plant(jax.random.randint(splits[7], (OBS, NB), 0, CD // BS), jax.random.fold_in(splits[7], 1), 0, (CD // BS) - 1).astype(jnp.int32),
    }


def reference(flux, prior_std, footprint, obs_value, obs_weight, obs_hour, hour_offset, block_cell):
    nblk = N_TILE * BPT
    padded = jnp.concatenate([jnp.zeros((HB, CELLS), jnp.bfloat16), flux], axis=0)
    blocks = padded.reshape((NH + HB) * nblk, BS)
    window = (jnp.arange(OBS, dtype=jnp.int32) // OBS_DEV).astype(jnp.int32)
    tile_of = (jnp.arange(NB, dtype=jnp.int32) // NBT).astype(jnp.int32)
    hour_pad = (window[:, None] + 1) * HB + obs_hour[:, None] - hour_offset
    flat = (hour_pad * nblk + tile_of[None, :] * BPT + block_cell).astype(jnp.int32)
    foot_w = footprint.reshape(N_WIN, OBS_DEV, NB, BS)
    flat_w = flat.reshape(N_WIN, OBS_DEV, NB)

    def predict(item):
        foot, index = item
        picked = blocks[index].astype(jnp.float32)
        return jnp.einsum("onc,onc->o", foot.astype(jnp.float32), picked)

    predicted = lax.map(predict, (foot_w, flat_w)).reshape(OBS)
    weighted = (predicted - obs_value) * obs_weight
    weighted_w = weighted.reshape(N_WIN, OBS_DEV)

    def accumulate(total, item):
        foot, index, scale = item
        contrib = scale[:, None, None] * foot.astype(jnp.float32)
        return total.at[index.reshape(-1)].add(contrib.reshape(-1, BS)), None

    total0 = jnp.zeros(((NH + HB) * nblk, BS), jnp.float32)
    total, unused = lax.scan(accumulate, total0, (foot_w, flat_w, weighted_w))
    adjoint = total.reshape(NH + HB, CELLS)[HB:]
    scaled = prior_std * adjoint
    spread = jnp.pad(scaled, ((KH, KH), (0, 0)))
    smoothed = jnp.zeros((NH, CELLS), jnp.float32)
    for shift_k in range(-KH, KH + 1):
        factor = jnp.exp(jnp.float32(-2.0 * abs(shift_k) / KH))
        smoothed = smoothed + factor * spread[KH + shift_k:KH + shift_k + NH]
    return prior_std * smoothed
```

```python
import functools
import jax
import jax.numpy as jnp
import numpy as np
from jax import lax
from jax.experimental import pallas as pl
from jax.experimental.pallas import tpu as pltpu
from jax.sharding import PartitionSpec as P

LANES = 128
NBIN = 128
CELLS = 64
HEAD = 41 * 128
META = 56
F32, BF16, I32 = jnp.float32, jnp.bfloat16, jnp.int32
NT = (((1,), (1,)), ((), ()))


def iota(shape, dim):
    return lax.broadcasted_iota(I32, shape, dim)


def dot(a, b):
    return jnp.dot(a, b, preferred_element_type=F32)


def capacity(n):
    return n + CELLS * 16 + LANES


def sort_body(nobs, which, hb, oh_ref, off_ref, cell_ref, fp_ref, own_ref, neg_ref, ometa_ref, nmeta_ref,
              fpv, stage, rows, outv, keyv, hourv, posv, poss, metav, tabs, tabv, sems):
    nblk = off_ref.shape[0]
    n = nobs * nblk
    per = nobs // LANES
    lines = nblk * per
    cap = capacity(n)
    span = HEAD // LANES - 1
    top = META - 8
    fetch = pltpu.make_async_copy(fp_ref.at[pl.ds(which * n, n)], fpv, sems.at[0])
    fetch.start()
    bins = iota((NBIN, LANES), 0)
    lanes = iota((NBIN, LANES), 1)
    upper = (bins < lanes).astype(BF16)
    ones = jnp.ones((LANES, LANES), BF16)
    same = (bins // CELLS) == (lanes // CELLS)
    below = jnp.where(same & (lanes < bins), 1.0, 0.0).astype(BF16)
    before = jnp.where(same & (bins < lanes), 1.0, 0.0).astype(BF16)

    for c in range(per):
        cut = slice(c * LANES, (c + 1) * LANES)
        hour = oh_ref[:, cut] - off_ref[:, cut]
        early = hour < 0
        keyv[c * nblk:(c + 1) * nblk, :] = jnp.where(early, cell_ref[:, cut] + CELLS, cell_ref[:, cut])
        hourv[c * nblk:(c + 1) * nblk, :] = jnp.where(early, hour + hb + 1, hour + 1).astype(F32)

    def count(r, total):
        for u in range(4):
            total = total + jnp.where(bins == keyv[pl.ds(r * 4 + u, 1), :], 1.0, 0.0)
        return total

    total = lax.fori_loop(0, lines // 4, count, jnp.zeros((NBIN, LANES), F32))
    total_b = total.astype(BF16)
    ahead = dot(total_b, upper)
    cnt_s = dot(total_b, ones)
    cnt_l = lax.dot_general(ones[:8], total_b, NT, preferred_element_type=F32)

    def starts(cnt, left):
        tiles = jnp.floor((cnt + 15.0) * (1.0 / 16.0))
        coarse = jnp.floor(tiles * (1.0 / 128.0))
        fine = tiles - 128.0 * coarse

        def run(v):
            return dot(below, v.astype(BF16)) if left else dot(v.astype(BF16), before)

        return 16.0 * (128.0 * run(coarse) + run(fine))

    tight_l = starts(cnt_l, False)
    base = starts(cnt_s, True) + ahead + jnp.where(bins >= CELLS, float(cap), 0.0)
    line8 = iota((8, LANES), 0)
    limit = float(span * LANES)
    far = jnp.where((cnt_l > float(LANES)) | (tight_l + cnt_l > limit), 1.0, 0.0)
    over = jnp.max(far, axis=1, keepdims=True)
    tab = jnp.where(line8 == 0, jnp.minimum(cnt_l, float(LANES)),
                    jnp.where(line8 == 1, jnp.minimum(tight_l, limit), over)).astype(I32)
    tabv[...] = tab
    metav[0, top:top + 8, :] = tab
    metav[1, top:top + 8, :] = pltpu.roll(tab, CELLS, 1)
    to_tab = pltpu.make_async_copy(tabv, tabs, sems.at[1])
    to_tab.start()

    def place(r, acc):
        for u in range(4):
            at = r * 4 + u
            hot = bins == keyv[pl.ds(at, 1), :]
            posv[pl.ds(at, 1), :] = jnp.sum(jnp.where(hot, acc, 0.0), axis=0, keepdims=True).astype(I32)
            acc = jnp.where(hot, acc + 1.0, acc)
        return acc

    lax.fori_loop(0, lines // 4, place, base)
    to_pos = pltpu.make_async_copy(posv, poss, sems.at[2])
    to_pos.start()
    to_tab.wait()
    ends = []
    for side in range(2):
        last = CELLS - 1 + CELLS * side
        ends.append(jnp.minimum(tabs[1, last] + tabs[0, last], span * LANES))

    high = iota((2 * span, LANES), 0)
    high = jnp.where(high >= span, high + (cap // LANES - span), high)
    obs = iota((1, LANES), 1).astype(F32)
    done = jnp.zeros((2 * span, LANES), F32)
    for c in range(per):
        def gather(r, acc):
            marks, spots = [], []
            for u in range(4):
                at = c * nblk + r * 4 + u
                pos = posv[pl.ds(at, 1), :]
                there = high == lax.shift_right_logical(pos, 7)
                marks.append(jnp.concatenate(
                    [jnp.where(there, v, 0.0).astype(BF16) for v in (hourv[pl.ds(at, 1), :], obs)], axis=0))
                spots.append(jnp.where(bins == (pos & 127), 1.0, 0.0).astype(BF16))
            return acc + lax.dot_general(jnp.concatenate(marks, axis=1), jnp.concatenate(spots, axis=1), NT,
                                         preferred_element_type=F32)

        acc = lax.fori_loop(0, nblk // 4, gather, jnp.zeros((4 * span, LANES), F32))
        hour, low = acc[:2 * span], acc[2 * span:]
        done = done + jnp.where(hour > 0.0, hour - 1.0 + 256.0 * (low + float(c * LANES)), 0.0)
    done = done.astype(I32)
    metav[0, 0:span, :] = done[:span]
    metav[1, 0:span, :] = done[span:]
    fetch.wait()

    def unpack(i, _):
        for u in range(8):
            at = pl.multiple_of(i * 128 + u * 16, 16)
            stage[pl.ds(at, 16), :] = fpv[pl.ds(at, 16), :].astype(F32)
        return 0

    lax.fori_loop(0, n // 128, unpack, 0)
    for side in range(2):
        def blank(i, _):
            at = pl.multiple_of(i * LANES + side * cap, LANES)
            rows[pl.ds(at, LANES), :] = jnp.zeros((LANES, LANES), F32)
            return 0

        lax.fori_loop(0, jnp.minimum(lax.shift_right_logical(ends[side] + 255 + 15, 7), span + 1), blank, 0)
    to_pos.wait()

    def permute(r, _):
        c = lax.shift_right_logical(r, 4)
        src = c * (LANES * nblk) + (r & 15)
        for l in range(LANES):
            rows[pl.ds(poss[r, l], 1), :] = stage[pl.ds(src + l * nblk, 1), :]
        return 0

    lax.fori_loop(0, lines, permute, 0)

    for side in range(2):
        def convert(i, _):
            at = pl.multiple_of(i * 128, 128)
            src = pl.multiple_of(at + side * cap, 128)
            outv[side, pl.ds(at, 128), :] = rows[pl.ds(src, 128), :].astype(BF16)
            return 0

        lax.fori_loop(0, jnp.minimum(lax.shift_right_logical(ends[side] + 255 + 15, 7), span + 1), convert, 0)
    copies = [pltpu.make_async_copy(outv.at[k], ref, sems.at[k]) for k, ref in enumerate((own_ref, neg_ref))]
    copies += [pltpu.make_async_copy(metav.at[k], ref, sems.at[3 + k]) for k, ref in enumerate((ometa_ref, nmeta_ref))]
    for copy in copies:
        copy.start()
    for copy in copies:
        copy.wait()


def sort_half(oh, off, cell, fp2, which=0, hb=240):
    nblk, nobs = off.shape
    n = nobs * nblk
    cap = capacity(n)
    lines = nblk * nobs // LANES
    vm = pl.BlockSpec(memory_space=pltpu.VMEM)
    any_ = pl.BlockSpec(memory_space=pl.ANY)
    return pl.pallas_call(
        functools.partial(sort_body, nobs, which, hb),
        out_shape=(jax.ShapeDtypeStruct((HEAD, LANES), BF16), jax.ShapeDtypeStruct((HEAD, LANES), BF16),
                   jax.ShapeDtypeStruct((META, LANES), I32), jax.ShapeDtypeStruct((META, LANES), I32)),
        in_specs=[vm, vm, vm, any_],
        out_specs=(any_, any_, any_, any_),
        scratch_shapes=[
            pltpu.VMEM((n, LANES), BF16), pltpu.VMEM((n, LANES), F32), pltpu.VMEM((2 * cap, LANES), F32),
            pltpu.VMEM((2, HEAD, LANES), BF16), pltpu.VMEM((lines, LANES), I32), pltpu.VMEM((lines, LANES), F32),
            pltpu.VMEM((lines, LANES), I32), pltpu.SMEM((lines, LANES), I32),
            pltpu.VMEM((2, META, LANES), I32), pltpu.SMEM((8, LANES), I32),
            pltpu.VMEM((8, LANES), I32), pltpu.SemaphoreType.DMA((5,)),
        ],
        compiler_params=pltpu.CompilerParams(vmem_limit_bytes=60 << 20),
        cost_estimate=pl.CostEstimate(flops=10**9, bytes_accessed=50 << 20, transcendentals=0),
        name="sort_half",
    )(oh, off, cell, fp2)


KH = 24
VM = pl.BlockSpec(memory_space=pltpu.VMEM)
ANY = pl.BlockSpec(memory_space=pl.ANY)
TAB = pl.BlockSpec((8, LANES), lambda *_: (META // 8 - 1, 0), memory_space=pltpu.SMEM)


def from_behind(value, axis, steps):
    count = lax.axis_size(axis)
    initial, last = (max(0, -steps), min(count, count - steps))
    return lax.ppermute(value, axis, [(source, source + steps) for source in range(initial, last)])


def extended(cells, sides, width):
    for axis, dim in sides:
        count = lax.axis_size(axis)
        ends = count - 1
        head = lax.slice_in_dim(cells, 0, width, axis=dim)
        tail = lax.slice_in_dim(cells, cells.shape[dim] - width, cells.shape[dim], axis=dim)
        cells = jnp.concatenate(
            [
                lax.ppermute(tail, axis, [(i, (i + 1) % count) for i in range(ends)]),
                cells,
                lax.ppermute(head, axis, [((i + 1) % count, i) for i in range(ends)]),
            ],
            axis=dim,
        )
    return cells


def misfits(partial_value, obs_value, obs_weight):
    predicted = lax.psum(partial_value, "tile")
    return (predicted - obs_value) * obs_weight


def general(flux, prior_std, footprint, obs_value, obs_weight, obs_hour, hour_offset, block_cell):
    hours = flux.shape[0]
    cells = flux.shape[1]
    width = footprint.shape[2]
    per_hour = cells // width
    earlier = from_behind(flux, "win", 1)
    joined = jnp.concatenate([earlier, flux], axis=0).reshape(2 * hours * per_hour, width)
    flat = (hours + obs_hour[:, None] - hour_offset) * per_hour + block_cell
    picked = joined[flat]
    partial_value = jnp.einsum("onc,onc->o", footprint, picked, preferred_element_type=jnp.float32)
    weighted = misfits(partial_value, obs_value, obs_weight)
    contrib = weighted[:, None, None] * footprint.astype(jnp.float32)
    summed = jax.ops.segment_sum(
        contrib.reshape(-1, width), flat.reshape(-1), num_segments=2 * hours * per_hour
    )
    summed = summed.reshape(2 * hours, cells)
    returned = from_behind(summed[:hours], "win", -1)
    adjoint = summed[hours:] + returned
    scaled = prior_std * adjoint
    rim = extended(scaled, (("win", 0),), KH)
    rows = jnp.arange(hours, dtype=jnp.int32)[:, None]
    columns = jnp.arange(hours + 2 * KH, dtype=jnp.int32)[None, :]
    distance = columns - rows - KH
    kernel = jnp.where(
        jnp.abs(distance) <= KH, jnp.exp(-2.0 * jnp.abs(distance).astype(jnp.float32) / KH), 0.0
    )
    smoothed = jnp.dot(
        kernel, rim, preferred_element_type=jnp.float32, precision=lax.Precision.HIGHEST
    )
    return prior_std * smoothed


def lanes_at(meta_ref, start):
    row = lax.shift_right_logical(start, 7)
    skip = start & 127
    turn = (LANES - skip) & 127
    near = pltpu.roll(meta_ref[pl.ds(row, 1), :], turn, 1)
    after = pltpu.roll(meta_ref[pl.ds(row + 1, 1), :], turn, 1)
    return jnp.where(iota((1, LANES), 1) < LANES - skip, near, after)


def chunk(tab_ref, meta_ref, rows_ref, b):
    count, start = tab_ref[0, b], tab_ref[1, b]
    code = lanes_at(meta_ref, start)
    live = iota((1, LANES), 1) < count
    hour = jnp.where(live, code & 255, -1)
    obs = lax.shift_right_logical(code, 8)
    return hour, obs, rows_ref[pl.ds(pl.multiple_of(start, 16), LANES), :]


def halves(v):
    top = v.astype(BF16).astype(F32)
    return top, v - top


def predict_body(k, *refs):
    flux_ref, rows, metas, tabs = refs[0], refs[1:1 + k], refs[1 + k:1 + 2 * k], refs[1 + 2 * k:1 + 3 * k]
    out_ref, fluxv, rowv, sems = refs[1 + 3 * k:]
    cells = flux_ref.shape[1]
    parts = 4
    wide = cells // parts
    loads = [pltpu.make_async_copy(rows[i], rowv.at[i], sems.at[i]) for i in range(k)]
    flows = [pltpu.make_async_copy(flux_ref.at[:, pl.ds(p * wide, wide)], fluxv.at[:, pl.ds(p * wide, wide)],
                                   sems.at[k + p]) for p in range(parts)]
    flows[0].start()
    for load in loads:
        load.start()
    for flow in flows[1:]:
        flow.start()
    hours = iota((flux_ref.shape[0], LANES), 0)
    eight = iota((8, LANES), 0)
    bins = iota((LANES, LANES), 0)
    for load in loads:
        load.wait()
    sums = tuple(jnp.zeros((16, LANES), F32) for _ in range(k))
    for p in range(parts):
        flows[p].wait()

        def group(g, sums):
            result = []
            for i in range(k):
                left, right = [], []
                for u in range(4):
                    b = p * (CELLS // parts) + g * 4 + u
                    hour, obs, fp = chunk(tabs[i], metas[i], rowv.at[i], b)
                    local = fluxv[:, pl.ds(pl.multiple_of(b * LANES, LANES), LANES)]
                    full = lax.dot_general(local, fp, NT, preferred_element_type=F32)
                    value = jnp.sum(jnp.where(hours == hour, full, 0.0), axis=0, keepdims=True)
                    here = eight == lax.shift_right_logical(obs, 7)
                    left.append(jnp.concatenate([jnp.where(here, v, 0.0) for v in halves(value)], axis=0).astype(BF16))
                    right.append(jnp.where(bins == (obs & 127), 1.0, 0.0).astype(BF16))
                result.append(sums[i] + lax.dot_general(jnp.concatenate(left, axis=1), jnp.concatenate(right, axis=1),
                                                        NT, preferred_element_type=F32))
            return tuple(result)

        sums = lax.fori_loop(0, CELLS // parts // 4, group, sums)
    for i in range(k):
        out_ref[i] = sums[i][:8] + sums[i][8:]


def predict(flux, pairs):
    k = len(pairs)
    rows, metas = [r for r, _ in pairs], [m for _, m in pairs]
    return pl.pallas_call(
        functools.partial(predict_body, k),
        grid=(1,),
        out_shape=jax.ShapeDtypeStruct((k, 8, LANES), F32),
        in_specs=[ANY] + [ANY] * k + [VM] * k + [TAB] * k,
        out_specs=VM,
        scratch_shapes=[pltpu.VMEM(flux.shape, BF16), pltpu.VMEM((k, HEAD, LANES), BF16),
                        pltpu.SemaphoreType.DMA((k + 4,))],
        compiler_params=pltpu.CompilerParams(vmem_limit_bytes=40 << 20),
        cost_estimate=pl.CostEstimate(flops=k * 2 * 240 * 8192 * 128, bytes_accessed=(3 + k) << 20, transcendentals=0),
        name="predict",
    )(flux, *rows, *metas, *metas)


def weights_of(stack, hour, obs, half):
    near = jnp.where(iota((LANES, LANES), 0) == (obs & 127), 1.0, 0.0).astype(BF16)
    got = jnp.dot(stack, near, preferred_element_type=F32)
    got = got[:8] + got[8:16] + got[16:24]
    mine = iota((8, LANES), 0) == lax.shift_right_logical(obs, 7) + 4 * half
    return jnp.sum(jnp.where(mine, got, 0.0), axis=0, keepdims=True)


def stack_of(w):
    a, rest = halves(w)
    b, c = halves(rest)
    return jnp.concatenate([a, b, c], axis=0).astype(BF16)


def spread(hour, hours, w):
    hit = hours == hour
    return [jnp.where(hit, v, 0.0).astype(BF16) for v in halves(w)]


def edges_body(own_w, next_w, ps_head, ps_tail, *refs):
    rows, metas, tabs = refs[0:4], refs[4:8], refs[8:12]
    head_ref, tail_ref, sorted_ref, rowv, sems = refs[12:]
    loads = [pltpu.make_async_copy(rows[i], rowv.at[i], sems.at[i]) for i in range(4)]
    for load in loads:
        load.start()
    stacks = [stack_of(own_w[...]), stack_of(next_w[...])]
    total = 240
    band = iota((2 * KH, LANES), 0)
    hours = jnp.where(band < KH, band, band + (total - 2 * KH))
    for load in loads:
        load.wait()

    def group(g, _):
        for u in range(2):
            b = g * 2 + u
            left, right = [], []
            for i in range(4):
                hour, obs, fp = chunk(tabs[i], metas[i], rowv.at[i], b)
                w = weights_of(stacks[i // 2], hour, obs, i % 2)
                sorted_ref[pl.ds(b * 4 + i, 1), :] = w
                left += spread(hour, hours, w)
                right += [fp, fp]
            part = jnp.dot(jnp.concatenate(left, axis=1), jnp.concatenate(right, axis=0), preferred_element_type=F32)
            col = pl.ds(pl.multiple_of(b * LANES, LANES), LANES)
            head_ref[:, col] = part[:KH] * ps_head[:, col]
            tail_ref[:, col] = part[KH:] * ps_tail[:, col]
        return 0

    lax.fori_loop(0, CELLS // 2, group, 0)


def edges(own_w, next_w, ps, pairs):
    rows, metas = [r for r, _ in pairs], [m for _, m in pairs]
    cells = ps.shape[1]
    last = ps.shape[0] // KH - 1
    return pl.pallas_call(
        edges_body,
        grid=(1,),
        out_shape=(jax.ShapeDtypeStruct((KH, cells), F32), jax.ShapeDtypeStruct((KH, cells), F32),
                   jax.ShapeDtypeStruct((4 * CELLS, LANES), F32)),
        in_specs=[VM, VM, pl.BlockSpec((KH, cells), lambda *_: (0, 0)), pl.BlockSpec((KH, cells), lambda *_: (last, 0))]
        + [ANY] * 4 + [VM] * 4 + [TAB] * 4,
        out_specs=(VM, VM, VM),
        scratch_shapes=[pltpu.VMEM((4, HEAD, LANES), BF16), pltpu.SemaphoreType.DMA((4,))],
        compiler_params=pltpu.CompilerParams(vmem_limit_bytes=40 << 20),
        cost_estimate=pl.CostEstimate(flops=10**8, bytes_accessed=8 << 20, transcendentals=0),
        name="edges",
    )(own_w, next_w, ps, ps, *rows, *metas, *metas)


def inner_body(sorted_ref, head_ref, tail_ref, kern_ref, ps_ref, *refs):
    rows, metas, tabs = refs[0:4], refs[4:8], refs[8:12]
    out_ref, rowv, psv, outv, sems = refs[12:]
    total, cells = ps_ref.shape
    parts = 8
    wide = cells // parts
    per = CELLS // parts
    inside = total - 2 * KH
    loads = [pltpu.make_async_copy(rows[i], rowv.at[i], sems.at[i]) for i in range(4)]
    flows = [pltpu.make_async_copy(ps_ref.at[:, pl.ds(p * wide, wide)], psv.at[:, pl.ds(p * wide, wide)],
                                   sems.at[4 + p]) for p in range(parts)]
    drains = [pltpu.make_async_copy(outv.at[p % 2], out_ref.at[:, pl.ds(p * wide, wide)], sems.at[4 + parts + p])
              for p in range(parts)]
    for load in loads:
        load.start()
    for flow in flows:
        flow.start()
    hours = iota((inside, LANES), 0) + KH
    pad = jnp.zeros((16, wide), BF16)
    for load in loads:
        load.wait()
    for p in range(parts):
        flows[p].wait()
        if p >= 2:
            drains[p - 2].wait()
        done = []
        for u in range(per):
            b = p * per + u
            left, right = [], []
            for i in range(4):
                hour, _, fp = chunk(tabs[i], metas[i], rowv.at[i], b)
                left += spread(hour, hours, sorted_ref[pl.ds(b * 4 + i, 1), :])
                right += [fp, fp]
            part = jnp.dot(jnp.concatenate(left, axis=1), jnp.concatenate(right, axis=0), preferred_element_type=F32)
            col = slice(b * LANES, (b + 1) * LANES)
            done.append(jnp.concatenate([head_ref[:, col], part * psv[KH:total - KH, col], tail_ref[:, col]], axis=0))
        s = jnp.concatenate(done, axis=1)
        top, low = halves(s)
        top, low = top.astype(BF16), low.astype(BF16)
        stack = jnp.concatenate([top, pad, low, pad, top, pad], axis=0)
        smooth = jnp.dot(kern_ref[...], stack, preferred_element_type=F32)
        outv[p % 2] = smooth * psv[:, p * wide:(p + 1) * wide]
        drains[p].start()
    for p in (parts - 2, parts - 1):
        drains[p].wait()


def inner(order, head, tail, kern, ps, pairs):
    rows, metas = [r for r, _ in pairs], [m for _, m in pairs]
    wide = ps.shape[1] // 8
    return pl.pallas_call(
        inner_body,
        grid=(1,),
        out_shape=jax.ShapeDtypeStruct(ps.shape, F32),
        in_specs=[VM, VM, VM, VM, ANY] + [ANY] * 4 + [VM] * 4 + [TAB] * 4,
        out_specs=ANY,
        scratch_shapes=[pltpu.VMEM((4, HEAD, LANES), BF16), pltpu.VMEM(ps.shape, F32),
                        pltpu.VMEM((2, ps.shape[0], wide), F32), pltpu.SemaphoreType.DMA((20,))],
        compiler_params=pltpu.CompilerParams(vmem_limit_bytes=50 << 20),
        cost_estimate=pl.CostEstimate(flops=4 * 10**9, bytes_accessed=22 << 20, transcendentals=0),
        name="inner",
    )(order, head, tail, kern, ps, *rows, *metas, *metas)


def finish_body(own_ref, ps_ref, above_ref, below_ref, kern_ref, out_ref):
    side = pl.program_id(0)
    halo = jnp.where(side == 0, above_ref[...], below_ref[...])
    top, low = halves(halo)
    top, low = top.astype(BF16), low.astype(BF16)
    stack = jnp.concatenate([top, low, top], axis=0)
    add = jnp.dot(kern_ref[0], stack, preferred_element_type=F32)
    out_ref[...] = own_ref[...] + ps_ref[...] * add


def finish(partial, ps, above, below, kern):
    cells = ps.shape[1]
    last = ps.shape[0] // KH - 1
    wide = 2048
    edge = pl.BlockSpec((KH, wide), lambda s, c: (s * last, c))
    whole = pl.BlockSpec((KH, wide), lambda s, c: (0, c))
    return pl.pallas_call(
        finish_body,
        grid=(2, cells // wide),
        out_shape=jax.ShapeDtypeStruct(ps.shape, F32),
        in_specs=[edge, edge, whole, whole, pl.BlockSpec((1, KH, 3 * KH), lambda s, c: (s, 0, 0))],
        out_specs=edge,
        input_output_aliases={0: 0},
        name="finish",
    )(partial, ps, above, below, kern)


def taps(distance):
    far = np.abs(distance)
    full = np.where(far <= KH, np.exp(np.float32(-2.0) * far.astype(np.float32) / np.float32(KH)), 0).astype(np.float32)
    top = full.astype(BF16)
    return top, (full - top.astype(np.float32)).astype(BF16)


def kernels(total):
    row, col = np.arange(total)[:, None], np.arange(256)[None, :]
    top, low = taps(np.where(col < total, row - col, total))
    main = np.concatenate([top, top, low], axis=1)
    row, col = np.arange(KH)[:, None], np.arange(KH)[None, :]
    ends = []
    for distance in (row + KH - col, KH + col - row):
        top, low = taps(distance)
        ends.append(np.concatenate([top, top, low], axis=1))
    return jnp.asarray(main), jnp.asarray(np.stack(ends))


def quick(flux, prior_std, obs_value, obs_weight, own, theirs):
    main, ends = kernels(flux.shape[0])
    mine = predict(flux, own)
    other = jnp.concatenate([predict(flux, theirs[:1]), predict(flux, theirs[1:])], axis=0)
    other = from_behind(other, "win", 1)
    partial = jnp.concatenate([(mine + other)[k, :4] for k in range(2)], axis=0)
    weighted = misfits(partial.reshape(-1), obs_value, obs_weight).reshape(8, LANES)
    later = from_behind(weighted, "win", -1)
    pairs = own + theirs
    head, tail, order = edges(weighted, later, prior_std, pairs)
    above = from_behind(tail, "win", 1)
    below = from_behind(head, "win", -1)
    partial = inner(order, head, tail, main, prior_std, pairs)
    return finish(partial, prior_std, above, below, ends)


def shards(flux, prior_std, footprint, obs_value, obs_weight, obs_hour, hour_offset, block_cell):
    count, nblk, width = footprint.shape
    half = count // 2
    own, theirs, over = [], [], []
    for k in range(2):
        cut = slice(k * half, (k + 1) * half)
        rows, early, meta, early_meta = sort_half(
            obs_hour[cut].reshape(1, half), hour_offset[cut].T, block_cell[cut].T,
            footprint.reshape(count * nblk, width), k, flux.shape[0])
        own.append((rows, meta))
        over.append(meta[META - 6, 0])
        theirs.append((from_behind(early, "win", -1), from_behind(early_meta, "win", -1)))
    bad = lax.psum((over[0] + over[1]).astype(F32), ("win", "tile")) > 0.0
    return lax.cond(
        bad,
        lambda: general(flux, prior_std, footprint, obs_value, obs_weight, obs_hour, hour_offset, block_cell),
        lambda: quick(flux, prior_std, obs_value, obs_weight, own, theirs))


def solution(mesh):
    return jax.shard_map(
        shards,
        mesh=mesh,
        in_specs=(
            P("win", "tile"),
            P("win", "tile"),
            P("win", "tile", None),
            P("win"),
            P("win"),
            P("win"),
            P("win", "tile"),
            P("win", "tile"),
        ),
        out_specs=P("win", "tile"),
        check_vma=False,
    )
```

```python
import functools

import jax
import jax.numpy as jnp
import numpy as np
from jax import lax
from jax.experimental import pallas as pl
from jax.experimental.pallas import tpu as pltpu
from jax.sharding import PartitionSpec as P

KH = 24
LANES = 128
CELLS = 64
NBIN = 2 * CELLS
HEAD = 41 * LANES
NEAR = 32
META = CELLS + CELLS + 8
F32, BF16, I32 = jnp.float32, jnp.bfloat16, jnp.int32
NT = (((1,), (1,)), ((), ()))
MESH = pl.DeviceIdType.MESH
VM = pl.BlockSpec(memory_space=pltpu.VMEM)
ANY = pl.BlockSpec(memory_space=pl.ANY)
TAB = pl.BlockSpec((8, LANES), lambda *_: (META // 8 - 1, 0), memory_space=pltpu.SMEM)
TABV = pl.BlockSpec((8, LANES), lambda *_: (META // 8 - 1, 0))


def iota(shape, dim):
    return lax.broadcasted_iota(I32, shape, dim)


def dot(a, b):
    return jnp.dot(a, b, preferred_element_type=F32)


def halves(v):
    top = v.astype(BF16).astype(F32)
    return top, v - top


def pick(table, lane):
    return jnp.take_along_axis(table, jnp.broadcast_to(lane, table.shape), axis=1, mode="promise_in_bounds")


def from_behind(value, axis, steps):
    count = lax.axis_size(axis)
    initial, last = (max(0, -steps), min(count, count - steps))
    return lax.ppermute(value, axis, [(source, source + steps) for source in range(initial, last)])


def extended(cells, sides, width):
    for axis, dim in sides:
        count = lax.axis_size(axis)
        ends = count - 1
        head = lax.slice_in_dim(cells, 0, width, axis=dim)
        tail = lax.slice_in_dim(cells, cells.shape[dim] - width, cells.shape[dim], axis=dim)
        cells = jnp.concatenate(
            [
                lax.ppermute(tail, axis, [(i, (i + 1) % count) for i in range(ends)]),
                cells,
                lax.ppermute(head, axis, [((i + 1) % count, i) for i in range(ends)]),
            ],
            axis=dim,
        )
    return cells


def misfits(partial_value, obs_value, obs_weight):
    predicted = lax.psum(partial_value, "tile")
    return (predicted - obs_value) * obs_weight


def general(flux, prior_std, footprint, obs_value, obs_weight, obs_hour, hour_offset, block_cell):
    hours = flux.shape[0]
    cells = flux.shape[1]
    width = footprint.shape[2]
    per_hour = cells // width
    earlier = from_behind(flux, "win", 1)
    joined = jnp.concatenate([earlier, flux], axis=0).reshape(2 * hours * per_hour, width)
    flat = (hours + obs_hour[:, None] - hour_offset) * per_hour + block_cell
    picked = joined[flat]
    partial_value = jnp.einsum("onc,onc->o", footprint, picked, preferred_element_type=jnp.float32)
    weighted = misfits(partial_value, obs_value, obs_weight)
    contrib = weighted[:, None, None] * footprint.astype(jnp.float32)
    summed = jax.ops.segment_sum(
        contrib.reshape(-1, width), flat.reshape(-1), num_segments=2 * hours * per_hour
    )
    summed = summed.reshape(2 * hours, cells)
    returned = from_behind(summed[:hours], "win", -1)
    adjoint = summed[hours:] + returned
    scaled = prior_std * adjoint
    rim = extended(scaled, (("win", 0),), KH)
    rows = jnp.arange(hours, dtype=jnp.int32)[:, None]
    columns = jnp.arange(hours + 2 * KH, dtype=jnp.int32)[None, :]
    distance = columns - rows - KH
    kernel = jnp.where(
        jnp.abs(distance) <= KH, jnp.exp(-2.0 * jnp.abs(distance).astype(jnp.float32) / KH), 0.0
    )
    smoothed = jnp.dot(
        kernel, rim, preferred_element_type=jnp.float32, precision=lax.Precision.HIGHEST
    )
    return prior_std * smoothed


def sort_body(nobs, which, hb, oh_ref, off_ref, cell_ref, fp_ref, own_ref, neg_ref, ometa_ref, nmeta_ref,
              fpv, stage, rows, outv, keyv, hourv, posv, poss, metav, tabs, tabv, sems):
    nblk = off_ref.shape[0]
    n = nobs * nblk
    per = nobs // LANES
    lines = nblk * per
    cap = n + CELLS * 16 + LANES
    span = HEAD // LANES - 1
    fetch = pltpu.make_async_copy(fp_ref.at[pl.ds(which * n, n)], fpv, sems.at[0])
    fetch.start()
    bins = iota((NBIN, LANES), 0)
    lanes = iota((NBIN, LANES), 1)
    upper = (bins < lanes).astype(BF16)
    ones = jnp.ones((LANES, LANES), BF16)
    same = (bins // CELLS) == (lanes // CELLS)
    below = jnp.where(same & (lanes < bins), 1.0, 0.0).astype(BF16)
    before = jnp.where(same & (bins < lanes), 1.0, 0.0).astype(BF16)

    for c in range(per):
        cut = slice(which * nobs + c * LANES, which * nobs + (c + 1) * LANES)
        hour = oh_ref[:, cut] - off_ref[:, cut]
        early = hour < 0
        hour = jnp.where(early, hour + hb, hour)
        key = jnp.where(early, cell_ref[:, cut] + CELLS, cell_ref[:, cut])
        rim = (hour < KH) | (hour >= hb - KH)
        at = slice(c * nblk, (c + 1) * nblk)
        keyv[0, at, :] = jnp.where(rim, key, -1)
        keyv[1, at, :] = jnp.where(rim, -1, key)
        keyv[2, at, :] = key
        hourv[at, :] = (hour + 1).astype(F32)

    def count(r, total):
        first, second = total
        for u in range(4):
            first = first + jnp.where(bins == keyv[0, pl.ds(r * 4 + u, 1), :], 1.0, 0.0)
            second = second + jnp.where(bins == keyv[1, pl.ds(r * 4 + u, 1), :], 1.0, 0.0)
        return first, second

    zero = jnp.zeros((NBIN, LANES), F32)
    first, second = lax.fori_loop(0, lines // 4, count, (zero, zero))
    first, second = first.astype(BF16), second.astype(BF16)
    ahead = [dot(v, upper) for v in (first, second)]
    rim_s = dot(first, ones)
    cnt_s = rim_s + dot(second, ones)
    rim_l = lax.dot_general(ones[:8], first, NT, preferred_element_type=F32)
    cnt_l = rim_l + lax.dot_general(ones[:8], second, NT, preferred_element_type=F32)

    def starts(cnt, left):
        tiles = jnp.floor((cnt + 15.0) * (1.0 / 16.0))
        coarse = jnp.floor(tiles * (1.0 / 128.0))
        fine = tiles - 128.0 * coarse

        def run(v):
            return dot(below, v.astype(BF16)) if left else dot(v.astype(BF16), before)

        return 16.0 * (128.0 * run(coarse) + run(fine))

    tight_l = starts(cnt_l, False)
    base = starts(cnt_s, True) + jnp.where(bins >= CELLS, float(cap), 0.0)
    line8 = iota((8, LANES), 0)
    limit = float(span * LANES)
    far = jnp.where((cnt_l > float(LANES)) | (rim_l > float(NEAR)) | (tight_l + cnt_l > limit), 1.0, 0.0)
    over = jnp.max(far, axis=1, keepdims=True)
    tab = jnp.where(line8 == 0, jnp.minimum(cnt_l, float(LANES)),
                    jnp.where(line8 == 1, jnp.minimum(tight_l, limit), over)).astype(I32)
    tabv[...] = tab
    metav[0, 2 * CELLS:META, :] = tab
    metav[1, 2 * CELLS:META, :] = pltpu.roll(tab, CELLS, 1)
    to_tab = pltpu.make_async_copy(tabv, tabs, sems.at[1])
    to_tab.start()

    for turn in range(2):
        def place(r, acc):
            for u in range(4):
                at = pl.ds(r * 4 + u, 1)
                hot = bins == keyv[turn, at, :]
                posf = jnp.sum(jnp.where(hot, acc, 0.0), axis=0, keepdims=True).astype(I32)
                posv[at, :] = posf if turn == 0 else posv[at, :] + posf
                acc = jnp.where(hot, acc + 1.0, acc)
            return acc

        lax.fori_loop(0, lines // 4, place, base + ahead[turn] + (rim_s if turn else 0.0))
    to_pos = pltpu.make_async_copy(posv, poss, sems.at[2])
    to_pos.start()
    starts_l = tight_l + jnp.where(iota((8, LANES), 1) >= CELLS, float(cap), 0.0)
    for g in range(lines // 8):
        at = slice(g * 8, (g + 1) * 8)
        key = keyv[2, at, :]
        rank = posv[at, :] - pick(starts_l, key).astype(I32)
        keyv[0, at, :] = rank
        spot = jnp.where(rank < LANES, (key & (CELLS - 1)) * LANES + rank, -1)
        metav[0, CELLS + g * 8:CELLS + (g + 1) * 8, :] = jnp.where(key < CELLS, spot, -1)
        metav[1, CELLS + g * 8:CELLS + (g + 1) * 8, :] = jnp.where(key < CELLS, -1, spot)

    obs = iota((1, LANES), 1).astype(F32)
    done = zero
    for c in range(per):
        def gather(r, acc):
            marks, spots = [], []
            for u in range(4):
                at = pl.ds(c * nblk + r * 4 + u, 1)
                hot = bins == keyv[2, at, :]
                marks.append(jnp.concatenate(
                    [jnp.where(hot, v, 0.0).astype(BF16) for v in (hourv[at, :], obs)], axis=0))
                spots.append(jnp.where(bins == keyv[0, at, :], 1.0, 0.0).astype(BF16))
            return acc + lax.dot_general(jnp.concatenate(marks, axis=1), jnp.concatenate(spots, axis=1), NT,
                                         preferred_element_type=F32)

        acc = lax.fori_loop(0, nblk // 4, gather, jnp.zeros((2 * NBIN, LANES), F32))
        hour, low = acc[:NBIN], acc[NBIN:]
        done = done + jnp.where(hour > 0.0, hour + 256.0 * (low + float(c * LANES)), 0.0)
    done = done.astype(I32)
    metav[0, 0:CELLS, :] = done[:CELLS]
    metav[1, 0:CELLS, :] = done[CELLS:]
    to_meta = [pltpu.make_async_copy(metav.at[k], ref, sems.at[3 + k]) for k, ref in enumerate((ometa_ref, nmeta_ref))]
    for copy in to_meta:
        copy.start()
    to_tab.wait()
    blocks = []
    for side in range(2):
        last = CELLS - 1 + CELLS * side
        end = jnp.minimum(tabs[1, last] + tabs[0, last], span * LANES)
        blocks.append(jnp.minimum(lax.shift_right_logical(end + 270, 7), span + 1))

    for side in range(2):
        def blank(i, _):
            at = pl.multiple_of(i * LANES + side * cap, LANES)
            rows[pl.ds(at, LANES), :] = jnp.zeros((LANES, LANES), F32)
            return 0

        lax.fori_loop(0, blocks[side], blank, 0)
    fetch.wait()

    def unpack(i, _):
        for u in range(8):
            at = pl.multiple_of(i * 128 + u * 16, 16)
            stage[pl.ds(at, 16), :] = fpv[pl.ds(at, 16), :].astype(F32)
        return 0

    lax.fori_loop(0, n // 128, unpack, 0)
    to_pos.wait()

    def permute(r, _):
        c = lax.shift_right_logical(r, 4)
        src = c * (LANES * nblk) + (r & 15)
        for l in range(LANES):
            rows[pl.ds(poss[r, l], 1), :] = stage[pl.ds(src + l * nblk, 1), :]
        return 0

    lax.fori_loop(0, lines, permute, 0)
    copies = []
    for side in (1, 0):
        def convert(i, _):
            at = pl.multiple_of(i * 128, 128)
            src = pl.multiple_of(at + side * cap, 128)
            outv[side, pl.ds(at, 128), :] = rows[pl.ds(src, 128), :].astype(BF16)
            return 0

        lax.fori_loop(0, blocks[side], convert, 0)
        copies.append(pltpu.make_async_copy(outv.at[side], (own_ref, neg_ref)[side], sems.at[5 + side]))
        copies[-1].start()
    for copy in to_meta + copies:
        copy.wait()


def sort_half(oh, off, cell, fp2, which, hb):
    nblk, count = off.shape
    nobs = count // 2
    n = nobs * nblk
    cap = n + CELLS * 16 + LANES
    lines = nblk * nobs // LANES
    return pl.pallas_call(
        functools.partial(sort_body, nobs, which, hb),
        out_shape=(jax.ShapeDtypeStruct((HEAD, LANES), BF16), jax.ShapeDtypeStruct((HEAD, LANES), BF16),
                   jax.ShapeDtypeStruct((META, LANES), I32), jax.ShapeDtypeStruct((META, LANES), I32)),
        in_specs=[VM, VM, VM, ANY],
        out_specs=(ANY, ANY, ANY, ANY),
        scratch_shapes=[
            pltpu.VMEM((n, LANES), BF16), pltpu.VMEM((n, LANES), F32), pltpu.VMEM((2 * cap, LANES), F32),
            pltpu.VMEM((2, HEAD, LANES), BF16), pltpu.VMEM((3, lines, LANES), I32), pltpu.VMEM((lines, LANES), F32),
            pltpu.VMEM((lines, LANES), I32), pltpu.SMEM((lines, LANES), I32),
            pltpu.VMEM((2, META, LANES), I32), pltpu.SMEM((8, LANES), I32),
            pltpu.VMEM((8, LANES), I32), pltpu.SemaphoreType.DMA((7,)),
        ],
        compiler_params=pltpu.CompilerParams(vmem_limit_bytes=40 << 20),
        cost_estimate=pl.CostEstimate(flops=10**9, bytes_accessed=50 << 20, transcendentals=0),
        name="sort_half",
    )(oh, off, cell, fp2)


def predict_body(k, slot, chained, *refs):
    flux_ref, rows, metas, tabs = refs[0], refs[1:1 + k], refs[1 + k:1 + 2 * k], refs[1 + 2 * k:1 + 3 * k]
    before_ref = refs[1 + 3 * k] if chained else None
    out_ref, fluxv, rowv, tablev, sems = refs[-5:]
    cells = flux_ref.shape[1]
    parts = 4
    wide = cells // parts
    loads = [pltpu.make_async_copy(rows[i], rowv.at[i], sems.at[i]) for i in range(k)]
    flows = [pltpu.make_async_copy(flux_ref.at[:, pl.ds(p * wide, wide)], fluxv.at[:, pl.ds(p * wide, wide)],
                                   sems.at[k + p]) for p in range(parts)]
    flows[0].start()
    for load in loads:
        load.start()
    for flow in flows[1:]:
        flow.start()
    hours = iota((flux_ref.shape[0], k * LANES), 0) + 1
    for load in loads:
        load.wait()
    for p in range(parts):
        flows[p].wait()

        def group(g, _):
            for u in range(4):
                b = p * (CELLS // parts) + g * 4 + u
                hour = jnp.concatenate([m[pl.ds(b, 1), :] & 255 for m in metas], axis=1)
                fp = jnp.concatenate(
                    [rowv[i, pl.ds(pl.multiple_of(tabs[i][1, b], 16), LANES), :] for i in range(k)], axis=0)
                local = fluxv[:, pl.ds(pl.multiple_of(b * LANES, LANES), LANES)]
                full = lax.dot_general(local, fp, NT, preferred_element_type=F32)
                value = jnp.sum(jnp.where(hours == hour, full, 0.0), axis=0, keepdims=True)
                for i in range(k):
                    tablev[i, pl.ds(b, 1), :] = value[:, i * LANES:(i + 1) * LANES]
            return 0

        lax.fori_loop(0, CELLS // parts // 4, group, 0)
    per = 4
    lines = []
    for i in range(k):
        spots = [metas[i][CELLS + g * 8:CELLS + (g + 1) * 8, :] for g in range(8)]
        cell = [lax.shift_right_arithmetic(s, 7) for s in spots]
        lane = [s & 127 for s in spots]

        def collect(b, acc):
            row = jnp.broadcast_to(tablev[i, pl.ds(b, 1), :], (8, LANES))
            acc = list(acc)
            for g in range(8):
                acc[g // 2] = acc[g // 2] + jnp.where(cell[g] == b, pick(row, lane[g]), 0.0)
            return tuple(acc)

        acc = lax.fori_loop(0, CELLS, collect, (jnp.zeros((8, LANES), F32),) * per)
        lines.append(jnp.concatenate([jnp.sum(a, axis=0, keepdims=True) for a in acc], axis=0))
    if k == 2:
        out_ref[...] = jnp.concatenate(lines, axis=0)
    else:
        blank = jnp.zeros((per, LANES), F32)
        both = jnp.concatenate([lines[0], blank] if slot == 0 else [blank, lines[0]], axis=0)
        out_ref[...] = both + before_ref[...] if chained else both


def predict(flux, pairs, slot=0, before=None):
    k = len(pairs)
    rows, metas = [r for r, _ in pairs], [m for _, m in pairs]
    more = [] if before is None else [before]
    return pl.pallas_call(
        functools.partial(predict_body, k, slot, before is not None),
        grid=(1,),
        out_shape=jax.ShapeDtypeStruct((8, LANES), F32),
        in_specs=[ANY] + [ANY] * k + [VM] * k + [TAB] * k + [VM] * len(more),
        out_specs=VM,
        scratch_shapes=[pltpu.VMEM(flux.shape, BF16), pltpu.VMEM((k, HEAD, LANES), BF16),
                        pltpu.VMEM((k, CELLS, LANES), F32), pltpu.SemaphoreType.DMA((k + 4,))],
        compiler_params=pltpu.CompilerParams(vmem_limit_bytes=20 << 20),
        cost_estimate=pl.CostEstimate(flops=k * 2 * 240 * 8192 * 128, bytes_accessed=(10 + 5 * k) << 20,
                                      transcendentals=0),
        name="predict",
    )(flux, *rows, *metas, *metas, *more)


def exchange_body(own_ref, next_ref, obs_ref, tab0_ref, tab1_ref, w_ref, bad_ref,
                  pair_o, pair_n, prev_n, next_o, next_obs, flags, mine, spread_bad,
                  s_pair, s_side, s_flag, r_pair, r_side, r_obs, r_flag, s_bad, r_bad):
    wins, tiles = lax.axis_size("win"), lax.axis_size("tile")
    w, t = lax.axis_index("win"), lax.axis_index("tile")
    up, down = w > 0, w < wins - 1
    barrier = pltpu.get_barrier_semaphore()

    def greet(device):
        pl.semaphore_signal(barrier, inc=1, device_id=device, device_id_type=MESH)

    peers = [lax.rem(t + d, tiles) for d in range(tiles)]
    others = [lax.rem(w + d, wins) for d in range(wins)]
    for d in range(1, tiles):
        greet((w, peers[d]))
    for d in range(1, wins):
        greet((others[d], t))

    @pl.when(up)
    def _():
        for d in range(1, tiles):
            greet((w - 1, peers[d]))

    @pl.when(down)
    def _():
        for d in range(1, tiles):
            greet((w + 1, peers[d]))

    sides = jnp.where(up, 1, 0) + jnp.where(down, 1, 0)
    pl.semaphore_wait(barrier, tiles - 1 + wins - 1 + sides * (tiles - 1))

    def push(src, dst, ssem, rsem, device):
        return pltpu.make_async_remote_copy(src_ref=src, dst_ref=dst, send_sem=ssem, recv_sem=rsem,
                                            device_id=device, device_id_type=MESH)

    def to_peer(d):
        return [push(own_ref, pair_o.at[t], s_pair.at[0, d], r_pair.at[0, t], (w, peers[d])),
                push(next_ref, pair_n.at[t], s_pair.at[1, d], r_pair.at[1, t], (w, peers[d]))]

    def to_up(d):
        return push(own_ref, next_o.at[t], s_side.at[0, d], r_side.at[0, t], (w - 1, peers[d]))

    def to_down(d):
        return push(next_ref, prev_n.at[t], s_side.at[1, d], r_side.at[1, t], (w + 1, peers[d]))

    def obs_up():
        return push(obs_ref, next_obs, s_side.at[2, 0], r_obs, (w - 1, t))

    def to_flag(d):
        return [push(tab0_ref, flags.at[0, w], s_flag.at[0, d], r_flag.at[0, w], (others[d], t)),
                push(tab1_ref, flags.at[1, w], s_flag.at[1, d], r_flag.at[1, w], (others[d], t))]

    def from_peer(d):
        q = peers[d]
        return [push(own_ref, pair_o.at[q], s_pair.at[0, d], r_pair.at[0, q], (w, q)),
                push(next_ref, pair_n.at[q], s_pair.at[1, d], r_pair.at[1, q], (w, q))]

    def from_down(d):
        q = peers[d]
        return push(own_ref, next_o.at[q], s_side.at[0, d], r_side.at[0, q], (w - 1, q))

    def from_up(d):
        q = peers[d]
        return push(next_ref, prev_n.at[q], s_side.at[1, d], r_side.at[1, q], (w + 1, q))

    def from_flag(d):
        v = others[d]
        return [push(tab0_ref, flags.at[0, v], s_flag.at[0, d], r_flag.at[0, v], (v, t)),
                push(tab1_ref, flags.at[1, v], s_flag.at[1, d], r_flag.at[1, v], (v, t))]

    for d in range(1, wins):
        for copy in to_flag(d):
            copy.start()

    @pl.when(up)
    def _():
        obs_up().start()
        for d in range(tiles):
            to_up(d).start()

    @pl.when(down)
    def _():
        for d in range(tiles):
            to_down(d).start()

    for d in range(1, tiles):
        for copy in to_peer(d):
            copy.start()

    bad = jnp.maximum(tab0_ref[...], tab1_ref[...])
    for d in range(1, wins):
        for k, copy in enumerate(from_flag(d)):
            copy.wait_recv()
            bad = jnp.maximum(bad, flags[k, others[d]])
    mine[...] = bad
    own, later = own_ref[...], next_ref[...]
    for d in range(1, tiles):
        for copy in from_peer(d):
            copy.wait_recv()
        own = own + pair_o[peers[d]]
        later = later + pair_n[peers[d]]
    for d in range(1, tiles):
        push(mine, spread_bad.at[t], s_bad.at[d], r_bad.at[t], (w, peers[d])).start()
    w_ref[0] = own
    w_ref[1] = later

    @pl.when(up)
    def _():
        total = w_ref[0]
        for d in range(tiles):
            from_up(d).wait_recv()
            total = total + prev_n[peers[d]]
        w_ref[0] = total

    w_ref[0] = (w_ref[0] - obs_ref[0]) * obs_ref[1]

    @pl.when(down)
    def _():
        total = w_ref[1]
        for d in range(tiles):
            from_down(d).wait_recv()
            total = total + next_o[peers[d]]
        pltpu.make_async_remote_copy(src_ref=obs_ref, dst_ref=next_obs, send_sem=s_side.at[2, 0], recv_sem=r_obs,
                                     device_id=(w + 1, t), device_id_type=MESH).wait_recv()
        w_ref[1] = (total - next_obs[0]) * next_obs[1]

    for d in range(1, tiles):
        q = peers[d]
        push(mine, spread_bad.at[q], s_bad.at[d], r_bad.at[q], (w, q)).wait_recv()
        bad = jnp.maximum(bad, spread_bad[q])
    bad_ref[...] = bad
    for d in range(1, wins):
        for copy in to_flag(d):
            copy.wait_send()
    for d in range(1, tiles):
        for copy in to_peer(d):
            copy.wait_send()
        push(mine, spread_bad.at[t], s_bad.at[d], r_bad.at[t], (w, peers[d])).wait_send()

    @pl.when(up)
    def _():
        obs_up().wait_send()
        for d in range(tiles):
            to_up(d).wait_send()

    @pl.when(down)
    def _():
        for d in range(tiles):
            to_down(d).wait_send()


def exchange(mine, other, obs, metas):
    wins, tiles = lax.axis_size("win"), lax.axis_size("tile")
    block = pltpu.VMEM((tiles, 8, LANES), F32)
    sem = pltpu.SemaphoreType.DMA
    return pl.pallas_call(
        exchange_body,
        grid=(1,),
        out_shape=(jax.ShapeDtypeStruct((2, 8, LANES), F32), jax.ShapeDtypeStruct((8, LANES), I32)),
        in_specs=[VM, VM, VM, TABV, TABV],
        out_specs=(VM, VM),
        scratch_shapes=[block, block, block, block, pltpu.VMEM((2, 8, LANES), F32),
                        pltpu.VMEM((2, wins, 8, LANES), I32), pltpu.VMEM((8, LANES), I32),
                        pltpu.VMEM((tiles, 8, LANES), I32),
                        sem((2, tiles)), sem((3, tiles)), sem((2, wins)), sem((2, tiles)), sem((2, tiles)), sem,
                        sem((2, wins)), sem((tiles,)), sem((tiles,))],
        compiler_params=pltpu.CompilerParams(collective_id=3, has_side_effects=True),
        name="exchange",
    )(mine, other, obs, *metas)


def weigh(code, tables, slots):
    got = [pick(table, lax.shift_right_logical(code, 8) & 127) for table in tables]
    got = got[0] if len(got) == 1 else jnp.where(iota((8, LANES), 1) < 2 * NEAR, got[0], got[1])
    mine = iota((8, LANES), 0) == lax.shift_right_logical(code, 15) + slots
    return jnp.sum(jnp.where(mine, got, 0.0), axis=0, keepdims=True)


def spread(hour, hours, w):
    hit = hours == hour
    return [jnp.where(hit, v, 0.0).astype(BF16) for v in halves(w)]


def edges_body(w_ref, ps_head, ps_tail, *refs):
    rows, metas, tabs = refs[0:4], refs[4:8], refs[8:12]
    head_ref, tail_ref, rowv, sems = refs[12:]
    loads = [pltpu.make_async_copy(rows[i], rowv.at[i], sems.at[i]) for i in range(4)]
    for load in loads:
        load.start()
    total = 240
    band = iota((2 * KH, LANES), 0)
    hours = jnp.where(band < KH, band, band + (total - 2 * KH)) + 1
    quarter = lax.shift_right_logical(iota((1, LANES), 1), 5)
    slots = (quarter & 1) * 4
    tables = [w_ref[0], w_ref[1]]
    for load in loads:
        load.wait()

    def group(g, _):
        for u in range(4):
            b = g * 4 + u
            code = metas[0][pl.ds(b, 1), :]
            fps = []
            for i in range(4):
                if i:
                    code = jnp.where(quarter == i, pltpu.roll(metas[i][pl.ds(b, 1), :], i * NEAR, 1), code)
                fps.append(rowv[i, pl.ds(pl.multiple_of(tabs[i][1, b], 16), NEAR), :])
            fp = jnp.concatenate(fps, axis=0)
            left = jnp.concatenate(spread(code & 255, hours, weigh(code, tables, slots)), axis=1)
            part = dot(left, jnp.concatenate([fp, fp], axis=0))
            col = pl.ds(pl.multiple_of(b * LANES, LANES), LANES)
            head_ref[:, col] = part[:KH] * ps_head[:, col]
            tail_ref[:, col] = part[KH:] * ps_tail[:, col]
        return 0

    lax.fori_loop(0, CELLS // 4, group, 0)


def edges(w, ps, pairs):
    rows, metas = [r for r, _ in pairs], [m for _, m in pairs]
    cells = ps.shape[1]
    last = ps.shape[0] // KH - 1
    return pl.pallas_call(
        edges_body,
        grid=(1,),
        out_shape=(jax.ShapeDtypeStruct((KH, cells), F32), jax.ShapeDtypeStruct((KH, cells), F32)),
        in_specs=[VM, pl.BlockSpec((KH, cells), lambda *_: (0, 0)), pl.BlockSpec((KH, cells), lambda *_: (last, 0))]
        + [ANY] * 4 + [VM] * 4 + [TAB] * 4,
        out_specs=(VM, VM),
        scratch_shapes=[pltpu.VMEM((4, HEAD, LANES), BF16), pltpu.SemaphoreType.DMA((4,))],
        compiler_params=pltpu.CompilerParams(vmem_limit_bytes=20 << 20),
        cost_estimate=pl.CostEstimate(flops=10**8, bytes_accessed=8 << 20, transcendentals=0),
        name="edges",
    )(w, ps, ps, *rows, *metas, *metas)


def inner_body(w_ref, head_ref, tail_ref, kern_ref, ps_ref, *refs):
    rows, metas, tabs = refs[0:4], refs[4:8], refs[8:12]
    out_ref, rowv, psv, outv, sv, sems, osems = refs[12:]
    total, cells = ps_ref.shape
    parts = 16
    wide = cells // parts
    per = CELLS // parts
    inside = total - 2 * KH
    loads = [pltpu.make_async_copy(rows[i], rowv.at[i], sems.at[i]) for i in range(4)]

    def flow(p):
        at = pl.ds(pl.multiple_of(p * wide, LANES), wide)
        return pltpu.make_async_copy(ps_ref.at[:, at], psv.at[:, at], sems.at[4 + p])

    def drain(p):
        at = pl.ds(pl.multiple_of(p * wide, LANES), wide)
        return pltpu.make_async_copy(outv.at[p & 1], out_ref.at[:, at], osems.at[p & 1])

    flow(0).start()
    for load in loads:
        load.start()
    for p in range(1, parts):
        flow(p).start()
    hours = iota((inside, LANES), 0) + KH + 1
    pad = jnp.zeros((16, wide), BF16)
    for load in loads:
        load.wait()

    def part_of(p, _):
        flow(p).wait()
        for u in range(per):
            b = p * per + u
            left, right = [], []
            for i in range(4):
                code = metas[i][pl.ds(b, 1), :]
                left += spread(code & 255, hours, weigh(code, [w_ref[i // 2]], (i % 2) * 4))
                fp = rowv[i, pl.ds(pl.multiple_of(tabs[i][1, b], 16), LANES), :]
                right += [fp, fp]
            part = dot(jnp.concatenate(left, axis=1), jnp.concatenate(right, axis=0))
            col = pl.ds(pl.multiple_of(b * LANES, LANES), LANES)
            here = slice(u * LANES, (u + 1) * LANES)
            sv[:KH, here] = head_ref[:, col]
            sv[KH:total - KH, here] = part * psv[KH:total - KH, col]
            sv[total - KH:, here] = tail_ref[:, col]
        top, low = halves(sv[...])
        top, low = top.astype(BF16), low.astype(BF16)
        stack = jnp.concatenate([top, pad, low, pad, top, pad], axis=0)
        smooth = dot(kern_ref[...], stack)

        @pl.when(p >= 2)
        def _():
            drain(p - 2).wait()

        outv[p & 1] = smooth * psv[:, pl.ds(pl.multiple_of(p * wide, LANES), wide)]
        drain(p).start()
        return 0

    lax.fori_loop(0, parts, part_of, 0)
    for p in (parts - 2, parts - 1):
        drain(p).wait()


def inner(w, head, tail, kern, ps, pairs):
    rows, metas = [r for r, _ in pairs], [m for _, m in pairs]
    wide = ps.shape[1] // 16
    return pl.pallas_call(
        inner_body,
        grid=(1,),
        out_shape=jax.ShapeDtypeStruct(ps.shape, F32),
        in_specs=[VM, VM, VM, VM, ANY] + [ANY] * 4 + [VM] * 4 + [TAB] * 4,
        out_specs=ANY,
        scratch_shapes=[pltpu.VMEM((4, HEAD, LANES), BF16), pltpu.VMEM(ps.shape, F32),
                        pltpu.VMEM((2, ps.shape[0], wide), F32), pltpu.VMEM((ps.shape[0], wide), F32),
                        pltpu.SemaphoreType.DMA((20,)), pltpu.SemaphoreType.DMA((2,))],
        compiler_params=pltpu.CompilerParams(vmem_limit_bytes=32 << 20),
        cost_estimate=pl.CostEstimate(flops=4 * 10**9, bytes_accessed=40 << 20, transcendentals=0),
        name="inner",
    )(w, head, tail, kern, ps, *rows, *metas, *metas)


def finish_body(own_ref, ps_ref, above_ref, below_ref, out_ref):
    row = iota((KH, LANES), 0).astype(F32)

    def fill(ref, scale, after, forward):
        for c in range(out_ref.shape[1] // LANES):
            cut = slice(c * LANES, (c + 1) * LANES)
            x = ref[:, cut] * scale
            for s in (1, 2, 4, 8, 16):
                gap = jnp.zeros((s, LANES), F32)
                x = x + (jnp.concatenate([gap, x[:KH - s]], axis=0) if forward
                         else jnp.concatenate([x[s:], gap], axis=0))
            out_ref[:, cut] = own_ref[:, cut] + ps_ref[:, cut] * (x * after)

    @pl.when(pl.program_id(0) == 0)
    def _():
        fill(above_ref, jnp.exp((row - KH) * (2.0 / KH)), jnp.exp(row * (-2.0 / KH)), False)

    @pl.when(pl.program_id(0) == 1)
    def _():
        fill(below_ref, jnp.exp(row * (-2.0 / KH)), jnp.exp((row - KH) * (2.0 / KH)), True)


def finish(partial, ps, above, below):
    cells = ps.shape[1]
    last = ps.shape[0] // KH - 1
    wide = 2048
    edge = pl.BlockSpec((KH, wide), lambda s, c: (s * last, c))
    return pl.pallas_call(
        finish_body,
        grid=(2, cells // wide),
        out_shape=jax.ShapeDtypeStruct(ps.shape, F32),
        in_specs=[edge, edge, pl.BlockSpec((KH, wide), lambda s, c: (0, jnp.where(s == 0, c, cells // wide - 1))),
                  pl.BlockSpec((KH, wide), lambda s, c: (0, jnp.where(s == 0, 0, c)))],
        out_specs=edge,
        input_output_aliases={0: 0},
        name="finish",
    )(partial, ps, above, below)


def taps(distance):
    far = np.abs(distance)
    full = np.where(far <= KH, np.exp(np.float32(-2.0) * far.astype(np.float32) / np.float32(KH)), 0).astype(np.float32)
    top = full.astype(BF16)
    return top, (full - top.astype(np.float32)).astype(BF16)


def smoother(total):
    row, col = np.arange(total)[:, None], np.arange(256)[None, :]
    top, low = taps(np.where(col < total, row - col, total))
    return jnp.asarray(np.concatenate([top, top, low], axis=1))


def quick(flux, prior_std, w, pairs):
    head, tail = edges(w, prior_std, pairs)
    above = from_behind(tail, "win", 1)
    below = from_behind(head, "win", -1)
    partial = inner(w, head, tail, smoother(flux.shape[0]), prior_std, pairs)
    return finish(partial, prior_std, above, below)


def shards(flux, prior_std, footprint, obs_value, obs_weight, obs_hour, hour_offset, block_cell):
    count, nblk, width = footprint.shape
    own, theirs = [], []
    for k in range(2):
        rows, early, meta, early_meta = sort_half(
            obs_hour.reshape(1, count), hour_offset.T, block_cell.T,
            footprint.reshape(count * nblk, width), k, flux.shape[0])
        own.append((rows, meta))
        theirs.append((from_behind(early, "win", -1), from_behind(early_meta, "win", -1)))
    obs = jnp.stack([obs_value.reshape(8, LANES), obs_weight.reshape(8, LANES)])
    mine = predict(flux, own)
    other = predict(flux, theirs[:1])
    other = predict(flux, theirs[1:], 1, other)
    w, bad = exchange(mine, other, obs, [meta for _, meta in own])
    return lax.cond(
        bad[2, 0] > 0,
        lambda: general(flux, prior_std, footprint, obs_value, obs_weight, obs_hour, hour_offset, block_cell),
        lambda: quick(flux, prior_std, w, own + theirs))


def solution(mesh):
    return jax.shard_map(
        shards,
        mesh=mesh,
        in_specs=(
            P("win", "tile"),
            P("win", "tile"),
            P("win", "tile", None),
            P("win"),
            P("win"),
            P("win"),
            P("win", "tile"),
            P("win", "tile"),
        ),
        out_specs=P("win", "tile"),
        check_vma=False,
    )
```

```python
import functools

import jax
import jax.numpy as jnp
import numpy as np
from jax import lax
from jax.experimental import pallas as pl
from jax.experimental.pallas import tpu as pltpu
from jax.sharding import PartitionSpec as P

KH = 24
LANES = 128
CELLS = 64
NBIN = 2 * CELLS
HEAD = 41 * LANES
NEAR = 32
META = CELLS + CELLS + 8
F32, BF16, I32 = jnp.float32, jnp.bfloat16, jnp.int32
NT = (((1,), (1,)), ((), ()))
MESH = pl.DeviceIdType.MESH
VM = pl.BlockSpec(memory_space=pltpu.VMEM)
HBM = pl.BlockSpec(memory_space=pltpu.HBM)
TAB = pl.BlockSpec((8, LANES), lambda *_: (META // 8 - 1, 0), memory_space=pltpu.SMEM)
TABV = pl.BlockSpec((8, LANES), lambda *_: (META // 8 - 1, 0))


def iota(shape, dim):
    return lax.broadcasted_iota(I32, shape, dim)


def dot(a, b):
    return jnp.dot(a, b, preferred_element_type=F32)


def halves(v):
    top = v.astype(BF16).astype(F32)
    return top, v - top


def pick(table, lane):
    return jnp.take_along_axis(table, jnp.broadcast_to(lane, table.shape), axis=1, mode="promise_in_bounds")


def from_behind(value, axis, steps):
    count = lax.axis_size(axis)
    initial, last = (max(0, -steps), min(count, count - steps))
    return lax.ppermute(value, axis, [(source, source + steps) for source in range(initial, last)])


def extended(cells, sides, width):
    for axis, dim in sides:
        count = lax.axis_size(axis)
        ends = count - 1
        head = lax.slice_in_dim(cells, 0, width, axis=dim)
        tail = lax.slice_in_dim(cells, cells.shape[dim] - width, cells.shape[dim], axis=dim)
        cells = jnp.concatenate(
            [
                lax.ppermute(tail, axis, [(i, (i + 1) % count) for i in range(ends)]),
                cells,
                lax.ppermute(head, axis, [((i + 1) % count, i) for i in range(ends)]),
            ],
            axis=dim,
        )
    return cells


def misfits(partial_value, obs_value, obs_weight):
    predicted = lax.psum(partial_value, "tile")
    return (predicted - obs_value) * obs_weight


def general(flux, prior_std, footprint, obs_value, obs_weight, obs_hour, hour_offset, block_cell):
    hours = flux.shape[0]
    cells = flux.shape[1]
    width = footprint.shape[2]
    per_hour = cells // width
    earlier = from_behind(flux, "win", 1)
    joined = jnp.concatenate([earlier, flux], axis=0).reshape(2 * hours * per_hour, width)
    flat = (hours + obs_hour[:, None] - hour_offset) * per_hour + block_cell
    picked = joined[flat]
    partial_value = jnp.einsum("onc,onc->o", footprint, picked, preferred_element_type=jnp.float32)
    weighted = misfits(partial_value, obs_value, obs_weight)
    contrib = weighted[:, None, None] * footprint.astype(jnp.float32)
    summed = jax.ops.segment_sum(
        contrib.reshape(-1, width), flat.reshape(-1), num_segments=2 * hours * per_hour
    )
    summed = summed.reshape(2 * hours, cells)
    returned = from_behind(summed[:hours], "win", -1)
    adjoint = summed[hours:] + returned
    scaled = prior_std * adjoint
    rim = extended(scaled, (("win", 0),), KH)
    rows = jnp.arange(hours, dtype=jnp.int32)[:, None]
    columns = jnp.arange(hours + 2 * KH, dtype=jnp.int32)[None, :]
    distance = columns - rows - KH
    kernel = jnp.where(
        jnp.abs(distance) <= KH, jnp.exp(-2.0 * jnp.abs(distance).astype(jnp.float32) / KH), 0.0
    )
    smoothed = jnp.dot(
        kernel, rim, preferred_element_type=jnp.float32, precision=lax.Precision.HIGHEST
    )
    return prior_std * smoothed


def sort_body(nobs, which, hb, oh_ref, off_ref, cell_ref, fp_ref, own_ref, neg_ref, ometa_ref, nmeta_ref,
              fpv, stage, rows, keyv, hourv, posv, poss, tabs, tabv, sems):
    nblk = off_ref.shape[0]
    n = nobs * nblk
    per = nobs // LANES
    lines = nblk * per
    cap = n + CELLS * 16 + LANES
    span = HEAD // LANES - 1
    outs, metas = (own_ref, neg_ref), (ometa_ref, nmeta_ref)
    fetch = pltpu.make_async_copy(fp_ref.at[pl.ds(which * n, n)], fpv, sems.at[0])
    fetch.start()
    bins = iota((NBIN, LANES), 0)
    lanes = iota((NBIN, LANES), 1)
    upper = (bins < lanes).astype(BF16)
    ones = jnp.ones((LANES, LANES), BF16)
    same = (bins // CELLS) == (lanes // CELLS)
    below = jnp.where(same & (lanes < bins), 1.0, 0.0).astype(BF16)
    before = jnp.where(same & (bins < lanes), 1.0, 0.0).astype(BF16)

    for c in range(per):
        cut = slice(which * nobs + c * LANES, which * nobs + (c + 1) * LANES)
        hour = oh_ref[:, cut] - off_ref[:, cut]
        early = hour < 0
        hour = jnp.where(early, hour + hb, hour)
        key = jnp.where(early, cell_ref[:, cut] + CELLS, cell_ref[:, cut])
        rim = (hour < KH) | (hour >= hb - KH)
        at = slice(c * nblk, (c + 1) * nblk)
        keyv[0, at, :] = jnp.where(rim, key, -1)
        keyv[1, at, :] = jnp.where(rim, -1, key)
        keyv[2, at, :] = key
        hourv[at, :] = (hour + 1).astype(F32)

    def count(r, total):
        first, second = total
        for u in range(4):
            first = first + jnp.where(bins == keyv[0, pl.ds(r * 4 + u, 1), :], 1.0, 0.0)
            second = second + jnp.where(bins == keyv[1, pl.ds(r * 4 + u, 1), :], 1.0, 0.0)
        return first, second

    zero = jnp.zeros((NBIN, LANES), F32)
    first, second = lax.fori_loop(0, lines // 4, count, (zero, zero))
    first, second = first.astype(BF16), second.astype(BF16)
    ahead = [dot(v, upper) for v in (first, second)]
    rim_s = dot(first, ones)
    cnt_s = rim_s + dot(second, ones)
    rim_l = lax.dot_general(ones[:8], first, NT, preferred_element_type=F32)
    cnt_l = rim_l + lax.dot_general(ones[:8], second, NT, preferred_element_type=F32)

    def starts(cnt, left):
        tiles = jnp.floor((cnt + 15.0) * (1.0 / 16.0))
        coarse = jnp.floor(tiles * (1.0 / 128.0))
        fine = tiles - 128.0 * coarse

        def run(v):
            return dot(below, v.astype(BF16)) if left else dot(v.astype(BF16), before)

        return 16.0 * (128.0 * run(coarse) + run(fine))

    tight_l = starts(cnt_l, False)
    base = starts(cnt_s, True) + jnp.where(bins >= CELLS, float(cap), 0.0)
    line8 = iota((8, LANES), 0)
    limit = float(span * LANES)
    far = jnp.where((cnt_l > float(LANES)) | (rim_l > float(NEAR)) | (tight_l + cnt_l > limit), 1.0, 0.0)
    over = jnp.max(far, axis=1, keepdims=True)
    tab = jnp.where(line8 == 0, jnp.minimum(cnt_l, float(LANES)),
                    jnp.where(line8 == 1, jnp.minimum(tight_l, limit), over)).astype(I32)
    tabv[...] = tab
    metas[0][2 * CELLS:META, :] = tab
    metas[1][2 * CELLS:META, :] = pltpu.roll(tab, CELLS, 1)
    to_tab = pltpu.make_async_copy(tabv, tabs, sems.at[1])
    to_tab.start()

    for turn in range(2):
        def place(r, acc):
            for u in range(4):
                at = pl.ds(r * 4 + u, 1)
                hot = bins == keyv[turn, at, :]
                posf = jnp.sum(jnp.where(hot, acc, 0.0), axis=0, keepdims=True).astype(I32)
                posv[at, :] = posf if turn == 0 else posv[at, :] + posf
                acc = jnp.where(hot, acc + 1.0, acc)
            return acc

        lax.fori_loop(0, lines // 4, place, base + ahead[turn] + (rim_s if turn else 0.0))
    to_pos = pltpu.make_async_copy(posv, poss, sems.at[2])
    to_pos.start()
    starts_l = tight_l + jnp.where(iota((8, LANES), 1) >= CELLS, float(cap), 0.0)
    for g in range(lines // 8):
        at = slice(g * 8, (g + 1) * 8)
        key = keyv[2, at, :]
        rank = posv[at, :] - pick(starts_l, key).astype(I32)
        keyv[0, at, :] = rank
        spot = jnp.where(rank < LANES, (key & (CELLS - 1)) * LANES + rank, -1)
        metas[0][CELLS + g * 8:CELLS + (g + 1) * 8, :] = jnp.where(key < CELLS, spot, -1)
        metas[1][CELLS + g * 8:CELLS + (g + 1) * 8, :] = jnp.where(key < CELLS, -1, spot)

    obs = iota((1, LANES), 1).astype(F32)
    done = zero
    for c in range(per):
        def gather(r, acc):
            marks, spots = [], []
            for u in range(4):
                at = pl.ds(c * nblk + r * 4 + u, 1)
                hot = bins == keyv[2, at, :]
                marks.append(jnp.concatenate(
                    [jnp.where(hot, v, 0.0).astype(BF16) for v in (hourv[at, :], obs)], axis=0))
                spots.append(jnp.where(bins == keyv[0, at, :], 1.0, 0.0).astype(BF16))
            return acc + lax.dot_general(jnp.concatenate(marks, axis=1), jnp.concatenate(spots, axis=1), NT,
                                         preferred_element_type=F32)

        acc = lax.fori_loop(0, nblk // 4, gather, jnp.zeros((2 * NBIN, LANES), F32))
        hour, low = acc[:NBIN], acc[NBIN:]
        done = done + jnp.where(hour > 0.0, hour + 256.0 * (low + float(c * LANES)), 0.0)
    done = done.astype(I32)
    metas[0][0:CELLS, :] = done[:CELLS]
    metas[1][0:CELLS, :] = done[CELLS:]
    to_tab.wait()
    blocks = []
    for side in range(2):
        last = CELLS - 1 + CELLS * side
        end = jnp.minimum(tabs[1, last] + tabs[0, last], span * LANES)
        blocks.append(jnp.minimum(lax.shift_right_logical(end + 270, 7), span + 1))

    for side in range(2):
        def blank(i, _):
            at = pl.multiple_of(i * LANES + side * cap, LANES)
            rows[pl.ds(at, LANES), :] = jnp.zeros((LANES, LANES), F32)
            return 0

        lax.fori_loop(0, blocks[side], blank, 0)
    fetch.wait()

    def unpack(i, _):
        for u in range(8):
            at = pl.multiple_of(i * 128 + u * 16, 16)
            stage[pl.ds(at, 16), :] = fpv[pl.ds(at, 16), :].astype(F32)
        return 0

    lax.fori_loop(0, n // 128, unpack, 0)
    to_pos.wait()

    def permute(r, _):
        c = lax.shift_right_logical(r, 4)
        src = c * (LANES * nblk) + (r & 15)
        for l in range(LANES):
            rows[pl.ds(poss[r, l], 1), :] = stage[pl.ds(src + l * nblk, 1), :]
        return 0

    lax.fori_loop(0, lines, permute, 0)
    for side in range(2):
        def convert(i, _):
            at = pl.multiple_of(i * 128, 128)
            src = pl.multiple_of(at + side * cap, 128)
            outs[side][pl.ds(at, 128), :] = rows[pl.ds(src, 128), :].astype(BF16)
            return 0

        lax.fori_loop(0, blocks[side], convert, 0)


def sort_half(oh, off, cell, fp2, which, hb):
    nblk, count = off.shape
    nobs = count // 2
    n = nobs * nblk
    cap = n + CELLS * 16 + LANES
    lines = nblk * nobs // LANES
    return pl.pallas_call(
        functools.partial(sort_body, nobs, which, hb),
        out_shape=(jax.ShapeDtypeStruct((HEAD, LANES), BF16), jax.ShapeDtypeStruct((HEAD, LANES), BF16),
                   jax.ShapeDtypeStruct((META, LANES), I32), jax.ShapeDtypeStruct((META, LANES), I32)),
        in_specs=[VM, VM, VM, HBM],
        out_specs=(VM, VM, VM, VM),
        scratch_shapes=[
            pltpu.VMEM((n, LANES), BF16), pltpu.VMEM((n, LANES), F32), pltpu.VMEM((2 * cap, LANES), F32),
            pltpu.VMEM((3, lines, LANES), I32), pltpu.VMEM((lines, LANES), F32),
            pltpu.VMEM((lines, LANES), I32), pltpu.SMEM((lines, LANES), I32),
            pltpu.SMEM((8, LANES), I32),
            pltpu.VMEM((8, LANES), I32), pltpu.SemaphoreType.DMA((3,)),
        ],
        compiler_params=pltpu.CompilerParams(vmem_limit_bytes=24 << 20),
        cost_estimate=pl.CostEstimate(flops=10**9, bytes_accessed=50 << 20, transcendentals=0),
        name="sort_half",
    )(oh, off, cell, fp2)


def predict_body(k, slot, chained, *refs):
    flux_ref, rows, metas, tabs = refs[0], refs[1:1 + k], refs[1 + k:1 + 2 * k], refs[1 + 2 * k:1 + 3 * k]
    out_ref, tablev = refs[-2:]
    hours = iota((flux_ref.shape[0], k * LANES), 0) + 1
    step = 8

    def group(g, _):
        for u in range(step):
            b = g * step + u
            hour = jnp.concatenate([m[pl.ds(b, 1), :] & 255 for m in metas], axis=1)
            fp = jnp.concatenate(
                [rows[i][pl.ds(pl.multiple_of(tabs[i][1, b], 16), LANES), :] for i in range(k)], axis=0)
            local = flux_ref[:, pl.ds(pl.multiple_of(b * LANES, LANES), LANES)]
            full = lax.dot_general(local, fp, NT, preferred_element_type=F32)
            value = jnp.sum(jnp.where(hours == hour, full, 0.0), axis=0, keepdims=True)
            for i in range(k):
                tablev[i, pl.ds(b, 1), :] = value[:, i * LANES:(i + 1) * LANES]
        return 0

    lax.fori_loop(0, CELLS // step, group, 0)
    per = 4
    lines = []
    for i in range(k):
        spots = [metas[i][CELLS + g * 8:CELLS + (g + 1) * 8, :] for g in range(8)]
        cell = [lax.shift_right_arithmetic(s, 7) for s in spots]
        lane = [s & 127 for s in spots]

        def collect(q, acc):
            acc = list(acc)
            for u in range(4):
                b = q * 4 + u
                row = jnp.broadcast_to(tablev[i, pl.ds(b, 1), :], (8, LANES))
                for g in range(8):
                    acc[g // 2] = acc[g // 2] + jnp.where(cell[g] == b, pick(row, lane[g]), 0.0)
            return tuple(acc)

        acc = lax.fori_loop(0, CELLS // 4, collect, (jnp.zeros((8, LANES), F32),) * per)
        lines.append(jnp.concatenate([jnp.sum(a, axis=0, keepdims=True) for a in acc], axis=0))
    blank = jnp.zeros((per, LANES), F32)
    if k == 2:
        out_ref[...] = jnp.concatenate(lines, axis=0)
    elif not chained:
        out_ref[...] = jnp.concatenate([lines[0], blank], axis=0)
    else:
        mine_ref, other_ref, tab0_ref, tab1_ref = refs[1 + 3 * k:5 + 3 * k]
        out_ref[0] = mine_ref[...]
        out_ref[1] = jnp.concatenate([blank, lines[0]], axis=0) + other_ref[...]
        out_ref[2] = jnp.maximum(tab0_ref[...], tab1_ref[...]).astype(F32)


def predict(flux, pairs, slot=0, more=()):
    k = len(pairs)
    rows, metas = [r for r, _ in pairs], [m for _, m in pairs]
    return pl.pallas_call(
        functools.partial(predict_body, k, slot, len(more) > 0),
        grid=(1,),
        out_shape=jax.ShapeDtypeStruct((3, 8, LANES) if more else (8, LANES), F32),
        in_specs=[VM] + [VM] * k + [VM] * k + [TAB] * k + ([VM, VM, TABV, TABV] if more else []),
        out_specs=VM,
        scratch_shapes=[pltpu.VMEM((k, CELLS, LANES), F32)],
        compiler_params=pltpu.CompilerParams(vmem_limit_bytes=20 << 20),
        cost_estimate=pl.CostEstimate(flops=k * 2 * 240 * 8192 * 128, bytes_accessed=(10 + 5 * k) << 20,
                                      transcendentals=0),
        name="predict",
    )(flux, *rows, *metas, *metas, *more)


def exchange_body(p_ref, obs_ref, w_ref, bad_ref, pair, prev_n, next_o, next_obs, flags, mine,
                  s_pair, s_side, s_flag, r_pair, r_side, r_obs, r_flag):
    wins, tiles = lax.axis_size("win"), lax.axis_size("tile")
    w, t = lax.axis_index("win"), lax.axis_index("tile")
    up, down = w > 0, w < wins - 1
    barrier = pltpu.get_barrier_semaphore()
    peers = [lax.rem(t + d, tiles) for d in range(tiles)]
    others = [lax.rem(w + d, wins) for d in range(wins)]

    def greet(device):
        pl.semaphore_signal(barrier, inc=1, device_id=device, device_id_type=MESH)

    for d in range(1, tiles):
        greet((w, peers[d]))
    for d in range(1, wins):
        greet((others[d], t))

    @pl.when(up)
    def _():
        for d in range(1, tiles):
            greet((w - 1, peers[d]))

    @pl.when(down)
    def _():
        for d in range(1, tiles):
            greet((w + 1, peers[d]))

    sides = jnp.where(up, 1, 0) + jnp.where(down, 1, 0)
    pl.semaphore_wait(barrier, tiles - 1 + wins - 1 + sides * (tiles - 1))

    def push(src, dst, ssem, rsem, device):
        return pltpu.make_async_remote_copy(src_ref=src, dst_ref=dst, send_sem=ssem, recv_sem=rsem,
                                            device_id=device, device_id_type=MESH)

    def peer(d, at):
        return push(p_ref, pair.at[at], s_pair.at[d], r_pair.at[at], (w, peers[d]))

    def above(d, at):
        return push(p_ref.at[0], next_o.at[at], s_side.at[0, d], r_side.at[0, at], (w - 1, peers[d]))

    def under(d, at):
        return push(p_ref.at[1], prev_n.at[at], s_side.at[1, d], r_side.at[1, at], (w + 1, peers[d]))

    def obs_to(v):
        return push(obs_ref, next_obs, s_side.at[2, 0], r_obs, (v, t))

    def flag(d, at):
        return push(mine, flags.at[at], s_flag.at[d], r_flag.at[at], (others[d], t))

    for d in range(1, tiles):
        peer(d, t).start()

    @pl.when(up)
    def _():
        for d in range(tiles):
            above(d, t).start()
        obs_to(w - 1).start()

    @pl.when(down)
    def _():
        for d in range(tiles):
            under(d, t).start()

    own, later, bad = p_ref[0], p_ref[1], p_ref[2]
    for d in range(1, tiles):
        peer(d, peers[d]).wait_recv()
        got = pair.at[peers[d]]
        own, later, bad = own + got[0], later + got[1], jnp.maximum(bad, got[2])
    mine[...] = bad
    w_ref[0] = own
    w_ref[1] = later

    @pl.when(up)
    def _():
        total = w_ref[0]
        for d in range(tiles):
            under(d, peers[d]).wait_recv()
            total = total + prev_n[peers[d]]
        w_ref[0] = total

    w_ref[0] = (w_ref[0] - obs_ref[0]) * obs_ref[1]
    for d in range(1, wins):
        flag(d, w).start()

    @pl.when(down)
    def _():
        total = w_ref[1]
        for d in range(tiles):
            above(d, peers[d]).wait_recv()
            total = total + next_o[peers[d]]
        obs_to(w + 1).wait_recv()
        w_ref[1] = (total - next_obs[0]) * next_obs[1]

    for d in range(1, wins):
        flag(d, others[d]).wait_recv()
        bad = jnp.maximum(bad, flags[others[d]])
    bad_ref[...] = bad
    for d in range(1, wins):
        flag(d, w).wait_send()
    for d in range(1, tiles):
        peer(d, t).wait_send()

    @pl.when(up)
    def _():
        obs_to(w - 1).wait_send()
        for d in range(tiles):
            above(d, t).wait_send()

    @pl.when(down)
    def _():
        for d in range(tiles):
            under(d, t).wait_send()


def exchange(packet, obs):
    wins, tiles = lax.axis_size("win"), lax.axis_size("tile")
    block = pltpu.VMEM((tiles, 8, LANES), F32)
    sem = pltpu.SemaphoreType.DMA
    return pl.pallas_call(
        exchange_body,
        out_shape=(jax.ShapeDtypeStruct((2, 8, LANES), F32), jax.ShapeDtypeStruct((8, LANES), F32)),
        in_specs=[VM, VM],
        out_specs=(VM, VM),
        scratch_shapes=[pltpu.VMEM((tiles, 3, 8, LANES), F32), block, block, pltpu.VMEM((2, 8, LANES), F32),
                        pltpu.VMEM((wins, 8, LANES), F32), pltpu.VMEM((8, LANES), F32),
                        sem((tiles,)), sem((3, tiles)), sem((wins,)), sem((tiles,)), sem((2, tiles)), sem,
                        sem((wins,))],
        compiler_params=pltpu.CompilerParams(collective_id=3, has_side_effects=True),
        name="exchange",
    )(packet, obs)


def weigh(code, tables, slots):
    got = [pick(table, lax.shift_right_logical(code, 8) & 127) for table in tables]
    got = got[0] if len(got) == 1 else jnp.where(iota((8, LANES), 1) < 2 * NEAR, got[0], got[1])
    mine = iota((8, LANES), 0) == lax.shift_right_logical(code, 15) + slots
    return jnp.sum(jnp.where(mine, got, 0.0), axis=0, keepdims=True)


def spread(hour, hours, w):
    hit = hours == hour
    return [jnp.where(hit, v, 0.0).astype(BF16) for v in halves(w)]


def edges_body(w_ref, ps_head, ps_tail, *refs):
    rows, metas, tabs = refs[0:4], refs[4:8], refs[8:12]
    head_ref, tail_ref = refs[12:]
    total = 240
    band = iota((2 * KH, LANES), 0)
    hours = jnp.where(band < KH, band, band + (total - 2 * KH)) + 1
    quarter = lax.shift_right_logical(iota((1, LANES), 1), 5)
    slots = (quarter & 1) * 4
    tables = [w_ref[0], w_ref[1]]

    def group(g, _):
        for u in range(4):
            b = g * 4 + u
            code = metas[0][pl.ds(b, 1), :]
            fps = []
            for i in range(4):
                if i:
                    code = jnp.where(quarter == i, pltpu.roll(metas[i][pl.ds(b, 1), :], i * NEAR, 1), code)
                fps.append(rows[i][pl.ds(pl.multiple_of(tabs[i][1, b], 16), NEAR), :])
            fp = jnp.concatenate(fps, axis=0)
            left = jnp.concatenate(spread(code & 255, hours, weigh(code, tables, slots)), axis=1)
            part = dot(left, jnp.concatenate([fp, fp], axis=0))
            col = pl.ds(pl.multiple_of(b * LANES, LANES), LANES)
            head_ref[:, col] = part[:KH] * ps_head[:, col]
            tail_ref[:, col] = part[KH:] * ps_tail[:, col]
        return 0

    lax.fori_loop(0, CELLS // 4, group, 0)


def edges(w, ps, pairs):
    rows, metas = [r for r, _ in pairs], [m for _, m in pairs]
    cells = ps.shape[1]
    last = ps.shape[0] // KH - 1
    return pl.pallas_call(
        edges_body,
        grid=(1,),
        out_shape=(jax.ShapeDtypeStruct((KH, cells), F32), jax.ShapeDtypeStruct((KH, cells), F32)),
        in_specs=[VM, pl.BlockSpec((KH, cells), lambda *_: (0, 0)), pl.BlockSpec((KH, cells), lambda *_: (last, 0))]
        + [VM] * 4 + [VM] * 4 + [TAB] * 4,
        out_specs=(VM, VM),
        compiler_params=pltpu.CompilerParams(vmem_limit_bytes=20 << 20),
        cost_estimate=pl.CostEstimate(flops=10**8, bytes_accessed=8 << 20, transcendentals=0),
        name="edges",
    )(w, ps, ps, *rows, *metas, *metas)


def inner_body(w_ref, head_ref, tail_ref, kern_ref, ps_ref, *refs):
    rows, metas, tabs = refs[0:4], refs[4:8], refs[8:12]
    out_ref, outv, sv, osems = refs[12:]
    total, cells = ps_ref.shape
    parts = 16
    wide = cells // parts
    per = CELLS // parts
    inside = total - 2 * KH
    def drain(p):
        at = pl.ds(pl.multiple_of(p * wide, LANES), wide)
        return pltpu.make_async_copy(outv.at[p & 1], out_ref.at[:, at], osems.at[p & 1])

    hours = iota((inside, LANES), 0) + KH + 1
    pad = jnp.zeros((16, wide), BF16)

    def part_of(p, _):
        for u in range(per):
            b = p * per + u
            left, right = [], []
            for i in range(4):
                code = metas[i][pl.ds(b, 1), :]
                left += spread(code & 255, hours, weigh(code, [w_ref[i // 2]], (i % 2) * 4))
                fp = rows[i][pl.ds(pl.multiple_of(tabs[i][1, b], 16), LANES), :]
                right += [fp, fp]
            part = dot(jnp.concatenate(left, axis=1), jnp.concatenate(right, axis=0))
            col = pl.ds(pl.multiple_of(b * LANES, LANES), LANES)
            here = slice(u * LANES, (u + 1) * LANES)
            sv[:KH, here] = head_ref[:, col]
            sv[KH:total - KH, here] = part * ps_ref[KH:total - KH, col]
            sv[total - KH:, here] = tail_ref[:, col]
        top, low = halves(sv[...])
        top, low = top.astype(BF16), low.astype(BF16)
        stack = jnp.concatenate([top, pad, low, pad, top, pad], axis=0)
        smooth = dot(kern_ref[...], stack)

        @pl.when(p >= 2)
        def _():
            drain(p - 2).wait()

        outv[p & 1] = smooth * ps_ref[:, pl.ds(pl.multiple_of(p * wide, LANES), wide)]
        drain(p).start()
        return 0

    lax.fori_loop(0, parts, part_of, 0)
    for p in (parts - 2, parts - 1):
        drain(p).wait()


def inner(w, head, tail, kern, ps, pairs):
    rows, metas = [r for r, _ in pairs], [m for _, m in pairs]
    wide = ps.shape[1] // 16
    return pl.pallas_call(
        inner_body,
        grid=(1,),
        out_shape=jax.ShapeDtypeStruct(ps.shape, F32),
        in_specs=[VM, VM, VM, VM, VM] + [VM] * 4 + [VM] * 4 + [TAB] * 4,
        out_specs=HBM,
        scratch_shapes=[pltpu.VMEM((2, ps.shape[0], wide), F32), pltpu.VMEM((ps.shape[0], wide), F32),
                        pltpu.SemaphoreType.DMA((2,))],
        compiler_params=pltpu.CompilerParams(vmem_limit_bytes=32 << 20),
        cost_estimate=pl.CostEstimate(flops=4 * 10**9, bytes_accessed=40 << 20, transcendentals=0),
        name="inner",
    )(w, head, tail, kern, ps, *rows, *metas, *metas)


def finish_body(own_ref, ps_ref, above_ref, below_ref, out_ref, ownv, psv, halov, loads, stores):
    total = ps_ref.shape[0]
    row = iota((KH, LANES), 0).astype(F32)
    grow, decay = jnp.exp((row - KH) * (2.0 / KH)), jnp.exp(row * (-2.0 / KH))

    def fetch(side):
        at = pl.ds(side * (total - KH), KH)
        pieces = ((own_ref.at[at], ownv), (ps_ref.at[at], psv), ((above_ref, below_ref)[side], halov))
        return [pltpu.make_async_copy(src, dst.at[side], loads.at[side, i]) for i, (src, dst) in enumerate(pieces)]

    def store(side):
        return pltpu.make_async_copy(ownv.at[side], out_ref.at[pl.ds(side * (total - KH), KH)], stores.at[side])

    for side in range(2):
        for copy in fetch(side):
            copy.start()
    for side in range(2):
        for copy in fetch(side):
            copy.wait()
        scale, after = (grow, decay) if side == 0 else (decay, grow)

        def fill(q, _):
            for u in range(4):
                cut = pl.ds(pl.multiple_of((q * 4 + u) * LANES, LANES), LANES)
                x = halov[side, :, cut] * scale
                for s in (1, 2, 4, 8, 16):
                    gap = jnp.zeros((s, LANES), F32)
                    x = x + (jnp.concatenate([gap, x[:KH - s]], axis=0) if side
                             else jnp.concatenate([x[s:], gap], axis=0))
                ownv[side, :, cut] = ownv[side, :, cut] + psv[side, :, cut] * (x * after)
            return 0

        lax.fori_loop(0, ps_ref.shape[1] // LANES // 4, fill, 0)
        store(side).start()
    for side in range(2):
        store(side).wait()


def finish(partial, ps, above, below):
    band = pltpu.VMEM((2, KH, ps.shape[1]), F32)
    return pl.pallas_call(
        finish_body,
        out_shape=jax.ShapeDtypeStruct(ps.shape, F32),
        in_specs=[HBM] * 4,
        out_specs=HBM,
        scratch_shapes=[band, band, band, pltpu.SemaphoreType.DMA((2, 3)), pltpu.SemaphoreType.DMA((2,))],
        input_output_aliases={0: 0},
        name="finish",
    )(partial, ps, above, below)


def taps(distance):
    far = np.abs(distance)
    full = np.where(far <= KH, np.exp(np.float32(-2.0) * far.astype(np.float32) / np.float32(KH)), 0).astype(np.float32)
    top = full.astype(BF16)
    return top, (full - top.astype(np.float32)).astype(BF16)


def smoother(total):
    row, col = np.arange(total)[:, None], np.arange(256)[None, :]
    top, low = taps(np.where(col < total, row - col, total))
    return jnp.asarray(np.concatenate([top, top, low], axis=1))


def quick(flux, prior_std, w, pairs):
    head, tail = edges(w, prior_std, pairs)
    above = from_behind(tail, "win", 1)
    below = from_behind(head, "win", -1)
    partial = inner(w, head, tail, smoother(flux.shape[0]), prior_std, pairs)
    return finish(partial, prior_std, above, below)


def shards(flux, prior_std, footprint, obs_value, obs_weight, obs_hour, hour_offset, block_cell):
    count, nblk, width = footprint.shape
    own, theirs = [], []
    for k in range(2):
        rows, early, meta, early_meta = sort_half(
            obs_hour.reshape(1, count), hour_offset.T, block_cell.T,
            footprint.reshape(count * nblk, width), k, flux.shape[0])
        own.append((rows, meta))
        theirs.append((from_behind(early, "win", -1), from_behind(early_meta, "win", -1)))
    obs = jnp.stack([obs_value.reshape(8, LANES), obs_weight.reshape(8, LANES)])
    mine = predict(flux, own)
    other = predict(flux, theirs[:1])
    packet = predict(flux, theirs[1:], 1, (mine, other, own[0][1], own[1][1]))
    w, bad = exchange(packet, obs)
    return lax.cond(
        bad[2, 0] > 0.0,
        lambda: general(flux, prior_std, footprint, obs_value, obs_weight, obs_hour, hour_offset, block_cell),
        lambda: quick(flux, prior_std, w, own + theirs))


def solution(mesh):
    return jax.shard_map(
        shards,
        mesh=mesh,
        in_specs=(
            P("win", "tile"),
            P("win", "tile"),
            P("win", "tile", None),
            P("win"),
            P("win"),
            P("win"),
            P("win", "tile"),
            P("win", "tile"),
        ),
        out_specs=P("win", "tile"),
        check_vma=False,
    )
```

```python
import functools

import jax
import jax.numpy as jnp
import numpy as np
from jax import lax
from jax.experimental import pallas as pl
from jax.experimental.pallas import tpu as pltpu
from jax.sharding import PartitionSpec as P

KH = 24
LANES = 128
CELLS = 64
NBIN = 2 * CELLS
HEAD = 41 * LANES
NEAR = 32
META = CELLS + CELLS + 8
F32, BF16, I32 = jnp.float32, jnp.bfloat16, jnp.int32
NT = (((1,), (1,)), ((), ()))
MESH = pl.DeviceIdType.MESH
VM = pl.BlockSpec(memory_space=pltpu.VMEM)
HBM = pl.BlockSpec(memory_space=pltpu.HBM)

def tab_of(half):
    return pl.BlockSpec((8, LANES), lambda *_: (META // 8 * (half + 1) - 1, 0), memory_space=pltpu.SMEM)


def tabv_of(half):
    return pl.BlockSpec((8, LANES), lambda *_: (META // 8 * (half + 1) - 1, 0))


def tabs_from(metas):
    return [metas[0], metas[0], metas[1], metas[1]]


def iota(shape, dim):
    return lax.broadcasted_iota(I32, shape, dim)


def dot(a, b):
    return jnp.dot(a, b, preferred_element_type=F32)


def halves(v):
    top = v.astype(BF16).astype(F32)
    return top, v - top


def pick(table, lane):
    return jnp.take_along_axis(table, jnp.broadcast_to(lane, table.shape), axis=1, mode="promise_in_bounds")


def from_behind(value, axis, steps):
    count = lax.axis_size(axis)
    initial, last = (max(0, -steps), min(count, count - steps))
    return lax.ppermute(value, axis, [(source, source + steps) for source in range(initial, last)])


def extended(cells, sides, width):
    for axis, dim in sides:
        count = lax.axis_size(axis)
        ends = count - 1
        head = lax.slice_in_dim(cells, 0, width, axis=dim)
        tail = lax.slice_in_dim(cells, cells.shape[dim] - width, cells.shape[dim], axis=dim)
        cells = jnp.concatenate(
            [
                lax.ppermute(tail, axis, [(i, (i + 1) % count) for i in range(ends)]),
                cells,
                lax.ppermute(head, axis, [((i + 1) % count, i) for i in range(ends)]),
            ],
            axis=dim,
        )
    return cells


def misfits(partial_value, obs_value, obs_weight):
    predicted = lax.psum(partial_value, "tile")
    return (predicted - obs_value) * obs_weight


def general(flux, prior_std, footprint, obs_value, obs_weight, obs_hour, hour_offset, block_cell):
    hours = flux.shape[0]
    cells = flux.shape[1]
    width = footprint.shape[2]
    per_hour = cells // width
    earlier = from_behind(flux, "win", 1)
    joined = jnp.concatenate([earlier, flux], axis=0).reshape(2 * hours * per_hour, width)
    flat = (hours + obs_hour[:, None] - hour_offset) * per_hour + block_cell
    picked = joined[flat]
    partial_value = jnp.einsum("onc,onc->o", footprint, picked, preferred_element_type=jnp.float32)
    weighted = misfits(partial_value, obs_value, obs_weight)
    contrib = weighted[:, None, None] * footprint.astype(jnp.float32)
    summed = jax.ops.segment_sum(
        contrib.reshape(-1, width), flat.reshape(-1), num_segments=2 * hours * per_hour
    )
    summed = summed.reshape(2 * hours, cells)
    returned = from_behind(summed[:hours], "win", -1)
    adjoint = summed[hours:] + returned
    scaled = prior_std * adjoint
    rim = extended(scaled, (("win", 0),), KH)
    rows = jnp.arange(hours, dtype=jnp.int32)[:, None]
    columns = jnp.arange(hours + 2 * KH, dtype=jnp.int32)[None, :]
    distance = columns - rows - KH
    kernel = jnp.where(
        jnp.abs(distance) <= KH, jnp.exp(-2.0 * jnp.abs(distance).astype(jnp.float32) / KH), 0.0
    )
    smoothed = jnp.dot(
        kernel, rim, preferred_element_type=jnp.float32, precision=lax.Precision.HIGHEST
    )
    return prior_std * smoothed


class Sorter:
    def __init__(self, nobs, hb, oh_ref, off_ref, cell_ref, metas, keyv, hourv, posv, tabv):
        self.nobs, self.hb, self.inputs, self.metas = nobs, hb, (oh_ref, off_ref, cell_ref), metas
        self.keyv, self.hourv, self.posv, self.tabv = keyv, hourv, posv, tabv
        self.nblk = off_ref.shape[0]
        self.lines = self.nblk * nobs // LANES
        self.cap = capacity(self.nblk * nobs)

    def prepare(self, which, aside):
        nobs, nblk, cap, lines = self.nobs, self.nblk, self.cap, self.lines
        keyv, hourv, posv, metas = self.keyv, self.hourv, self.posv, self.metas
        oh_ref, off_ref, cell_ref = self.inputs
        per = nobs // LANES
        span = HEAD // LANES - 1
        at0 = which * META
        bins = iota((NBIN, LANES), 0)
        lanes = iota((NBIN, LANES), 1)
        upper = (bins < lanes).astype(BF16)
        ones = jnp.ones((LANES, LANES), BF16)
        same = (bins // CELLS) == (lanes // CELLS)
        below = jnp.where(same & (lanes < bins), 1.0, 0.0).astype(BF16)
        before = jnp.where(same & (bins < lanes), 1.0, 0.0).astype(BF16)
        for c in range(per):
            cut = slice(which * nobs + c * LANES, which * nobs + (c + 1) * LANES)
            hour = oh_ref[:, cut] - off_ref[:, cut]
            early = hour < 0
            hour = jnp.where(early, hour + self.hb, hour)
            key = jnp.where(early, cell_ref[:, cut] + CELLS, cell_ref[:, cut])
            rim = (hour < KH) | (hour >= self.hb - KH)
            at = slice(c * nblk, (c + 1) * nblk)
            keyv[0, at, :] = jnp.where(rim, key, -1)
            keyv[1, at, :] = jnp.where(rim, -1, key)
            keyv[2, at, :] = key
            hourv[at, :] = (hour + 1).astype(F32)

        def count(r, total):
            first, second = total
            for u in range(4):
                first = first + jnp.where(bins == keyv[0, pl.ds(r * 4 + u, 1), :], 1.0, 0.0)
                second = second + jnp.where(bins == keyv[1, pl.ds(r * 4 + u, 1), :], 1.0, 0.0)
                aside(0, r, u)
            return first, second

        zero = jnp.zeros((NBIN, LANES), F32)
        first, second = lax.fori_loop(0, lines // 4, count, (zero, zero))
        first, second = first.astype(BF16), second.astype(BF16)
        ahead = [dot(v, upper) for v in (first, second)]
        rim_s = dot(first, ones)
        cnt_s = rim_s + dot(second, ones)
        rim_l = lax.dot_general(ones[:8], first, NT, preferred_element_type=F32)
        cnt_l = rim_l + lax.dot_general(ones[:8], second, NT, preferred_element_type=F32)

        def starts(cnt, left):
            tiles = jnp.floor((cnt + 15.0) * (1.0 / 16.0))
            coarse = jnp.floor(tiles * (1.0 / 128.0))
            fine = tiles - 128.0 * coarse

            def run(v):
                return dot(below, v.astype(BF16)) if left else dot(v.astype(BF16), before)

            return 16.0 * (128.0 * run(coarse) + run(fine))

        tight_l = starts(cnt_l, False)
        base = starts(cnt_s, True) + jnp.where(bins >= CELLS, float(cap), 0.0)
        line8 = iota((8, LANES), 0)
        limit = float(span * LANES)
        far = jnp.where((cnt_l > float(LANES)) | (rim_l > float(NEAR)) | (tight_l + cnt_l > limit), 1.0, 0.0)
        over = jnp.max(far, axis=1, keepdims=True)
        tab = jnp.where(line8 == 0, jnp.minimum(cnt_l, float(LANES)),
                        jnp.where(line8 == 1, jnp.minimum(tight_l, limit), over)).astype(I32)
        self.tabv[...] = tab
        metas[0][at0 + 2 * CELLS:at0 + META, :] = tab
        metas[1][at0 + 2 * CELLS:at0 + META, :] = pltpu.roll(tab, CELLS, 1)
        for turn in range(2):
            def place(r, acc):
                for u in range(4):
                    at = pl.ds(r * 4 + u, 1)
                    hot = bins == keyv[turn, at, :]
                    posf = jnp.sum(jnp.where(hot, acc, 0.0), axis=0, keepdims=True).astype(I32)
                    posv[at, :] = posf if turn == 0 else posv[at, :] + posf
                    acc = jnp.where(hot, acc + 1.0, acc)
                    aside(1 + turn, r, u)
                return acc

            lax.fori_loop(0, lines // 4, place, base + ahead[turn] + (rim_s if turn else 0.0))
        aside(-1, 0, 0)
        starts_l = tight_l + jnp.where(iota((8, LANES), 1) >= CELLS, float(cap), 0.0)
        for g in range(lines // 8):
            at = slice(g * 8, (g + 1) * 8)
            key = keyv[2, at, :]
            rank = posv[at, :] - pick(starts_l, key).astype(I32)
            keyv[0, at, :] = rank
            spot = jnp.where(rank < LANES, (key & (CELLS - 1)) * LANES + rank, -1)
            lo = at0 + CELLS + g * 8
            metas[0][lo:lo + 8, :] = jnp.where(key < CELLS, spot, -1)
            metas[1][lo:lo + 8, :] = jnp.where(key < CELLS, -1, spot)
        obs = iota((1, LANES), 1).astype(F32)
        done = zero
        for c in range(per):
            def gather(r, acc):
                marks, spots = [], []
                for u in range(4):
                    at = pl.ds(c * nblk + r * 4 + u, 1)
                    hot = bins == keyv[2, at, :]
                    marks.append(jnp.concatenate(
                        [jnp.where(hot, v, 0.0).astype(BF16) for v in (hourv[at, :], obs)], axis=0))
                    spots.append(jnp.where(bins == keyv[0, at, :], 1.0, 0.0).astype(BF16))
                    aside(3, r + c * (nblk // 4), u)
                return acc + lax.dot_general(jnp.concatenate(marks, axis=1), jnp.concatenate(spots, axis=1), NT,
                                             preferred_element_type=F32)

            acc = lax.fori_loop(0, nblk // 4, gather, jnp.zeros((2 * NBIN, LANES), F32))
            hour, low = acc[:NBIN], acc[NBIN:]
            done = done + jnp.where(hour > 0.0, hour + 256.0 * (low + float(c * LANES)), 0.0)
        done = done.astype(I32)
        metas[0][at0:at0 + CELLS, :] = done[:CELLS]
        metas[1][at0:at0 + CELLS, :] = done[CELLS:]


def capacity(n):
    return n + CELLS * 16 + LANES


def blank_block(rows, cap, q):
    blocks = HEAD // LANES
    q = jnp.minimum(q, 2 * blocks - 1)
    at = jnp.where(q < blocks, q, q - blocks + cap // LANES)
    rows[pl.ds(pl.multiple_of(at * LANES, LANES), LANES), :] = jnp.zeros((LANES, LANES), F32)


def unpack_block(stage, fpv, q):
    at = pl.multiple_of(q * LANES, LANES)
    stage[pl.ds(at, LANES), :] = fpv[pl.ds(at, LANES), :].astype(F32)


def permute_line(rows, stage, poss, nblk, r, low=0, high=LANES):
    src = lax.shift_right_logical(r, 4) * (LANES * nblk) + (r & 15)
    for l in range(low, high):
        rows[pl.ds(poss[r, l], 1), :] = stage[pl.ds(src + l * nblk, 1), :]


def convert_all(rows, cap, outs, ends):
    for side in range(2):
        end = jnp.minimum(ends[side], HEAD - LANES)
        blocks = jnp.minimum(lax.shift_right_logical(end + 270, 7), HEAD // LANES)

        def convert(i, _):
            at = pl.multiple_of(i * LANES, LANES)
            src = pl.multiple_of(at + side * cap, LANES)
            outs[side][pl.ds(at, LANES), :] = rows[pl.ds(src, LANES), :].astype(BF16)
            return 0

        lax.fori_loop(0, blocks, convert, 0)


def first_body(nobs, hb, oh_ref, off_ref, cell_ref, fp_ref, own_ref, neg_ref, ometa_ref, nmeta_ref, pos_ref,
               fpv, stage, rows, keyv, hourv, posv, poss, tabs, tabv, sems):
    nblk = off_ref.shape[0]
    n = nobs * nblk
    fetch = pltpu.make_async_copy(fp_ref.at[pl.ds(0, n)], fpv, sems.at[0])
    fetch.start()
    sorter = Sorter(nobs, hb, oh_ref, off_ref, cell_ref, (ometa_ref, nmeta_ref), keyv, hourv, posv, tabv)
    cap, lines = sorter.cap, sorter.lines

    def ready(phase, r, u):
        if phase == -1:
            fetch.wait()
        elif phase == 0 and u < 3:
            blank_block(rows, cap, r * 6 + u * 2)
            blank_block(rows, cap, r * 6 + u * 2 + 1)
        elif phase == 3:
            unpack_block(stage, fpv, r * 4 + u)

    sorter.prepare(0, ready)
    to_tab = pltpu.make_async_copy(tabv, tabs, sems.at[1])
    to_tab.start()
    to_pos = pltpu.make_async_copy(posv, poss, sems.at[2])
    to_pos.start()
    to_tab.wait()
    to_pos.wait()
    ends = [tabs[1, k] + tabs[0, k] for k in (CELLS - 1, NBIN - 1)]

    def during(phase, r, u):
        if phase >= 0:
            permute_line(rows, stage, poss, nblk, phase * (lines // 4) + r, u * 32, u * 32 + 32)

    sorter.prepare(1, during)
    pos_ref[...] = posv[...]
    convert_all(rows, cap, (own_ref, neg_ref), ends)


def second_body(nobs, pos_ref, otab_ref, ntab_ref, fp_ref, own_ref, neg_ref, fpv, stage, rows, sems):
    n = fpv.shape[0]
    lines, nblk = pos_ref.shape[0], n // nobs
    cap = capacity(n)
    fetch = pltpu.make_async_copy(fp_ref.at[pl.ds(n, n)], fpv, sems.at[0])
    fetch.start()
    ends = [tab[1, CELLS - 1] + tab[0, CELLS - 1] for tab in (otab_ref, ntab_ref)]

    def blank(i, _):
        for u in range(2):
            blank_block(rows, cap, i * 2 + u)
        return 0

    lax.fori_loop(0, HEAD // LANES, blank, 0)
    fetch.wait()

    def lead(i, _):
        unpack_block(stage, fpv, i)
        return 0

    lax.fori_loop(0, nblk, lead, 0)

    def line(r, _):
        unpack_block(stage, fpv, jnp.minimum(r + nblk, lines - 1))
        permute_line(rows, stage, pos_ref, nblk, r)
        return 0

    lax.fori_loop(0, lines, line, 0)
    convert_all(rows, cap, (own_ref, neg_ref), ends)


def sort_both(oh, off, cell, fp2, hb):
    nblk, count = off.shape
    nobs = count // 2
    n = nobs * nblk
    cap = capacity(n)
    lines = n // LANES
    rows = jax.ShapeDtypeStruct((HEAD, LANES), BF16)
    meta = jax.ShapeDtypeStruct((2 * META, LANES), I32)
    smem = pl.BlockSpec(memory_space=pltpu.SMEM)
    params = pltpu.CompilerParams(vmem_limit_bytes=20 << 20)
    cost = pl.CostEstimate(flops=10**9, bytes_accessed=50 << 20, transcendentals=0)
    work = [pltpu.VMEM((n, LANES), BF16), pltpu.VMEM((n, LANES), F32), pltpu.VMEM((2 * cap, LANES), F32)]
    own0, neg0, ometa, nmeta, pos = pl.pallas_call(
        functools.partial(first_body, nobs, hb),
        out_shape=(rows, rows, meta, meta, jax.ShapeDtypeStruct((lines, LANES), I32)),
        in_specs=[VM, VM, VM, HBM],
        out_specs=(VM,) * 5,
        scratch_shapes=work + [
            pltpu.VMEM((3, lines, LANES), I32), pltpu.VMEM((lines, LANES), F32), pltpu.VMEM((lines, LANES), I32),
            pltpu.SMEM((lines, LANES), I32), pltpu.SMEM((8, LANES), I32), pltpu.VMEM((8, LANES), I32),
            pltpu.SemaphoreType.DMA((3,))],
        compiler_params=pltpu.CompilerParams(vmem_limit_bytes=20 << 20),
        cost_estimate=cost, name="sort_first",
    )(oh, off, cell, fp2)
    own1, neg1 = pl.pallas_call(
        functools.partial(second_body, nobs),
        grid=(1,),
        out_shape=(rows, rows),
        in_specs=[smem, tab_of(1), tab_of(1), HBM],
        out_specs=(VM, VM),
        scratch_shapes=work + [pltpu.SemaphoreType.DMA((1,))],
        compiler_params=params, cost_estimate=cost, name="sort_second",
    )(pos, ometa, nmeta, fp2)
    return (own0, own1), (neg0, neg1), ometa, nmeta


def predict_body(k, slot, chained, *refs):
    flux_ref, rows, meta, tabs = refs[0], refs[1:1 + k], refs[1 + k], refs[2 + k:2 + 2 * k]
    first = [(slot + i) * META for i in range(k)]
    out_ref, tablev = refs[-2:]
    hours = iota((flux_ref.shape[0], k * LANES), 0) + 1
    step = 8

    def group(g, _):
        for u in range(step):
            b = g * step + u
            hour = jnp.concatenate([meta[pl.ds(f + b, 1), :] & 255 for f in first], axis=1)
            fp = jnp.concatenate(
                [rows[i][pl.ds(pl.multiple_of(tabs[i][1, b], 16), LANES), :] for i in range(k)], axis=0)
            local = flux_ref[:, pl.ds(pl.multiple_of(b * LANES, LANES), LANES)]
            full = lax.dot_general(local, fp, NT, preferred_element_type=F32)
            value = jnp.sum(jnp.where(hours == hour, full, 0.0), axis=0, keepdims=True)
            for i in range(k):
                tablev[i, pl.ds(b, 1), :] = value[:, i * LANES:(i + 1) * LANES]
        return 0

    lax.fori_loop(0, CELLS // step, group, 0)
    per = 4
    lines = []
    for i in range(k):
        lo = first[i] + CELLS
        spots = [meta[lo + g * 8:lo + (g + 1) * 8, :] for g in range(8)]
        cell = [lax.shift_right_arithmetic(s, 7) for s in spots]
        lane = [s & 127 for s in spots]

        def collect(q, acc):
            acc = list(acc)
            for u in range(4):
                b = q * 4 + u
                row = jnp.broadcast_to(tablev[i, pl.ds(b, 1), :], (8, LANES))
                for g in range(8):
                    acc[g // 2] = acc[g // 2] + jnp.where(cell[g] == b, pick(row, lane[g]), 0.0)
            return tuple(acc)

        acc = lax.fori_loop(0, CELLS // 4, collect, (jnp.zeros((8, LANES), F32),) * per)
        lines.append(jnp.concatenate([jnp.sum(a, axis=0, keepdims=True) for a in acc], axis=0))
    blank = jnp.zeros((per, LANES), F32)
    if k == 2:
        out_ref[...] = jnp.concatenate(lines, axis=0)
    elif not chained:
        out_ref[...] = jnp.concatenate([lines[0], blank], axis=0)
    else:
        mine_ref, other_ref, tab0_ref, tab1_ref = refs[2 + 2 * k:6 + 2 * k]
        out_ref[0] = mine_ref[...]
        out_ref[1] = jnp.concatenate([blank, lines[0]], axis=0) + other_ref[...]
        out_ref[2] = jnp.maximum(tab0_ref[...], tab1_ref[...]).astype(F32)


def predict(flux, rows, meta, slot=0, more=()):
    k = len(rows)
    tabs = [tab_of(slot + i) for i in range(k)]
    return pl.pallas_call(
        functools.partial(predict_body, k, slot, len(more) > 0),
        grid=(1,),
        out_shape=jax.ShapeDtypeStruct((3, 8, LANES) if more else (8, LANES), F32),
        in_specs=[VM] * (k + 2) + tabs + ([VM, VM, tabv_of(0), tabv_of(1)] if more else []),
        out_specs=VM,
        scratch_shapes=[pltpu.VMEM((k, CELLS, LANES), F32)],
        compiler_params=pltpu.CompilerParams(vmem_limit_bytes=8 << 20),
        cost_estimate=pl.CostEstimate(flops=k * 2 * 240 * 8192 * 128, bytes_accessed=(10 + 5 * k) << 20,
                                      transcendentals=0),
        name="predict",
    )(flux, *rows, meta, *([meta] * k), *more)


def exchange_body(p_ref, value_ref, weight_ref, w_ref, bad_ref, pair, prev_n, next_o, next_obs, flags, mine,
                  s_pair, s_side, s_flag, r_pair, r_side, r_obs, r_flag):
    wins, tiles = lax.axis_size("win"), lax.axis_size("tile")
    w, t = lax.axis_index("win"), lax.axis_index("tile")
    up, down = w > 0, w < wins - 1
    barrier = pltpu.get_barrier_semaphore()
    peers = [lax.rem(t + d, tiles) for d in range(tiles)]
    others = [lax.rem(w + d, wins) for d in range(wins)]

    def greet(device):
        pl.semaphore_signal(barrier, inc=1, device_id=device, device_id_type=MESH)

    for d in range(1, tiles):
        greet((w, peers[d]))
    for d in range(1, wins):
        greet((others[d], t))

    @pl.when(up)
    def _():
        for d in range(1, tiles):
            greet((w - 1, peers[d]))

    @pl.when(down)
    def _():
        for d in range(1, tiles):
            greet((w + 1, peers[d]))

    sides = jnp.where(up, 1, 0) + jnp.where(down, 1, 0)
    pl.semaphore_wait(barrier, tiles - 1 + wins - 1 + sides * (tiles - 1))

    def push(src, dst, ssem, rsem, device):
        return pltpu.make_async_remote_copy(src_ref=src, dst_ref=dst, send_sem=ssem, recv_sem=rsem,
                                            device_id=device, device_id_type=MESH)

    def peer(d, at):
        return push(p_ref, pair.at[at], s_pair.at[d], r_pair.at[at], (w, peers[d]))

    def above(d, at):
        return push(p_ref.at[0], next_o.at[at], s_side.at[0, d], r_side.at[0, at], (w - 1, peers[d]))

    def under(d, at):
        return push(p_ref.at[1], prev_n.at[at], s_side.at[1, d], r_side.at[1, at], (w + 1, peers[d]))

    def obs_to(v):
        return [push(ref, next_obs.at[k], s_side.at[2, k], r_obs.at[k], (v, t))
                for k, ref in enumerate((value_ref, weight_ref))]

    def flag(d, at):
        return push(mine, flags.at[at], s_flag.at[d], r_flag.at[at], (others[d], t))

    for d in range(1, tiles):
        peer(d, t).start()

    @pl.when(up)
    def _():
        for d in range(tiles):
            above(d, t).start()
        for copy in obs_to(w - 1):
            copy.start()

    @pl.when(down)
    def _():
        for d in range(tiles):
            under(d, t).start()

    own, later, bad = p_ref[0], p_ref[1], p_ref[2]
    for d in range(1, tiles):
        peer(d, peers[d]).wait_recv()
        got = pair.at[peers[d]]
        own, later, bad = own + got[0], later + got[1], jnp.maximum(bad, got[2])
    mine[...] = bad
    w_ref[0] = own
    w_ref[1] = later

    @pl.when(up)
    def _():
        total = w_ref[0]
        for d in range(tiles):
            under(d, peers[d]).wait_recv()
            total = total + prev_n[peers[d]]
        w_ref[0] = total

    w_ref[0] = (w_ref[0] - value_ref[...]) * weight_ref[...]
    for d in range(1, wins):
        flag(d, w).start()

    @pl.when(down)
    def _():
        total = w_ref[1]
        for d in range(tiles):
            above(d, peers[d]).wait_recv()
            total = total + next_o[peers[d]]
        for copy in obs_to(w + 1):
            copy.wait_recv()
        w_ref[1] = (total - next_obs[0]) * next_obs[1]

    for d in range(1, wins):
        flag(d, others[d]).wait_recv()
        bad = jnp.maximum(bad, flags[others[d]])
    bad_ref[...] = bad
    for d in range(1, wins):
        flag(d, w).wait_send()
    for d in range(1, tiles):
        peer(d, t).wait_send()

    @pl.when(up)
    def _():
        for copy in obs_to(w - 1):
            copy.wait_send()
        for d in range(tiles):
            above(d, t).wait_send()

    @pl.when(down)
    def _():
        for d in range(tiles):
            under(d, t).wait_send()


def exchange(packet, value, weight):
    wins, tiles = lax.axis_size("win"), lax.axis_size("tile")
    block = pltpu.VMEM((tiles, 8, LANES), F32)
    sem = pltpu.SemaphoreType.DMA
    return pl.pallas_call(
        exchange_body,
        out_shape=(jax.ShapeDtypeStruct((2, 8, LANES), F32), jax.ShapeDtypeStruct((8, LANES), F32)),
        in_specs=[VM, VM, VM],
        out_specs=(VM, VM),
        scratch_shapes=[pltpu.VMEM((tiles, 3, 8, LANES), F32), block, block, pltpu.VMEM((2, 8, LANES), F32),
                        pltpu.VMEM((wins, 8, LANES), F32), pltpu.VMEM((8, LANES), F32),
                        sem((tiles,)), sem((3, tiles)), sem((wins,)), sem((tiles,)), sem((2, tiles)), sem((2,)),
                        sem((wins,))],
        compiler_params=pltpu.CompilerParams(collective_id=3, has_side_effects=True),
        name="exchange",
    )(packet, value, weight)


def weigh(code, tables, slots):
    got = [pick(table, lax.shift_right_logical(code, 8) & 127) for table in tables]
    got = got[0] if len(got) == 1 else jnp.where(iota((8, LANES), 1) < 2 * NEAR, got[0], got[1])
    mine = iota((8, LANES), 0) == lax.shift_right_logical(code, 15) + slots
    return jnp.sum(jnp.where(mine, got, 0.0), axis=0, keepdims=True)


def spread(hour, hours, w):
    hit = hours == hour
    return [jnp.where(hit, v, 0.0).astype(BF16) for v in halves(w)]


def edges_body(w_ref, ps_head, ps_tail, *refs):
    rows, metas, tabs = refs[0:4], refs[4:6], refs[6:10]
    head_ref, tail_ref = refs[10:]
    total = 240
    band = iota((2 * KH, LANES), 0)
    hours = jnp.where(band < KH, band, band + (total - 2 * KH)) + 1
    quarter = lax.shift_right_logical(iota((1, LANES), 1), 5)
    slots = (quarter & 1) * 4
    tables = [w_ref[0], w_ref[1]]

    def group(g, _):
        for u in range(4):
            b = g * 4 + u
            codes = [metas[i // 2][pl.ds((i % 2) * META + b, 1), :] for i in range(4)]
            code = codes[0]
            fps = []
            for i in range(4):
                if i:
                    code = jnp.where(quarter == i, pltpu.roll(codes[i], i * NEAR, 1), code)
                fps.append(rows[i][pl.ds(pl.multiple_of(tabs[i][1, b], 16), NEAR), :])
            fp = jnp.concatenate(fps, axis=0)
            left = jnp.concatenate(spread(code & 255, hours, weigh(code, tables, slots)), axis=1)
            part = dot(left, jnp.concatenate([fp, fp], axis=0))
            col = pl.ds(pl.multiple_of(b * LANES, LANES), LANES)
            head_ref[:, col] = part[:KH] * ps_head[:, col]
            tail_ref[:, col] = part[KH:] * ps_tail[:, col]
        return 0

    lax.fori_loop(0, CELLS // 4, group, 0)


def edges(w, ps, rows, metas):
    cells = ps.shape[1]
    last = ps.shape[0] // KH - 1
    return pl.pallas_call(
        edges_body,
        grid=(1,),
        out_shape=(jax.ShapeDtypeStruct((KH, cells), F32), jax.ShapeDtypeStruct((KH, cells), F32)),
        in_specs=[VM, pl.BlockSpec((KH, cells), lambda *_: (0, 0)), pl.BlockSpec((KH, cells), lambda *_: (last, 0))]
        + [VM] * 4 + [VM] * 2 + [tab_of(0), tab_of(1)] * 2,
        out_specs=(VM, VM),
        compiler_params=pltpu.CompilerParams(vmem_limit_bytes=8 << 20),
        cost_estimate=pl.CostEstimate(flops=10**8, bytes_accessed=8 << 20, transcendentals=0),
        name="edges",
    )(w, ps, ps, *rows, *metas, *tabs_from(metas))


def inner_body(w_ref, head_ref, tail_ref, kern_ref, ps_ref, *refs):
    rows, metas, tabs = refs[0:4], refs[4:6], refs[6:10]
    out_ref, outv, sv, osems = refs[10:]
    total, cells = ps_ref.shape
    parts = 16
    wide = cells // parts
    per = CELLS // parts
    inside = total - 2 * KH
    def drain(p):
        at = pl.ds(pl.multiple_of(p * wide, LANES), wide)
        return pltpu.make_async_copy(outv.at[p & 1], out_ref.at[:, at], osems.at[p & 1])

    hours = iota((inside, LANES), 0) + KH + 1
    pad = jnp.zeros((16, wide), BF16)

    def part_of(p, _):
        for u in range(per):
            b = p * per + u
            left, right = [], []
            for i in range(4):
                code = metas[i // 2][pl.ds((i % 2) * META + b, 1), :]
                left += spread(code & 255, hours, weigh(code, [w_ref[i // 2]], (i % 2) * 4))
                fp = rows[i][pl.ds(pl.multiple_of(tabs[i][1, b], 16), LANES), :]
                right += [fp, fp]
            part = dot(jnp.concatenate(left, axis=1), jnp.concatenate(right, axis=0))
            col = pl.ds(pl.multiple_of(b * LANES, LANES), LANES)
            here = slice(u * LANES, (u + 1) * LANES)
            sv[:KH, here] = head_ref[:, col]
            sv[KH:total - KH, here] = part * ps_ref[KH:total - KH, col]
            sv[total - KH:, here] = tail_ref[:, col]
        top, low = halves(sv[...])
        top, low = top.astype(BF16), low.astype(BF16)
        stack = jnp.concatenate([top, pad, low, pad, top, pad], axis=0)
        smooth = dot(kern_ref[...], stack)

        @pl.when(p >= 2)
        def _():
            drain(p - 2).wait()

        outv[p & 1] = smooth * ps_ref[:, pl.ds(pl.multiple_of(p * wide, LANES), wide)]
        drain(p).start()
        return 0

    lax.fori_loop(0, parts, part_of, 0)
    for p in (parts - 2, parts - 1):
        drain(p).wait()


def inner(w, head, tail, kern, ps, rows, metas):
    wide = ps.shape[1] // 16
    return pl.pallas_call(
        inner_body,
        grid=(1,),
        out_shape=jax.ShapeDtypeStruct(ps.shape, F32),
        in_specs=[VM, VM, VM, VM, VM] + [VM] * 4 + [VM] * 2 + [tab_of(0), tab_of(1)] * 2,
        out_specs=HBM,
        scratch_shapes=[pltpu.VMEM((2, ps.shape[0], wide), F32), pltpu.VMEM((ps.shape[0], wide), F32),
                        pltpu.SemaphoreType.DMA((2,))],
        compiler_params=pltpu.CompilerParams(vmem_limit_bytes=10 << 20),
        cost_estimate=pl.CostEstimate(flops=4 * 10**9, bytes_accessed=40 << 20, transcendentals=0),
        name="inner",
    )(w, head, tail, kern, ps, *rows, *metas, *tabs_from(metas))


def finish_body(own_ref, ps_ref, above_ref, below_ref, out_ref, ownv, psv, halov, loads, stores):
    total = ps_ref.shape[0]
    row = iota((KH, LANES), 0).astype(F32)
    grow, decay = jnp.exp((row - KH) * (2.0 / KH)), jnp.exp(row * (-2.0 / KH))

    def fetch(side):
        at = pl.ds(side * (total - KH), KH)
        pieces = ((own_ref.at[at], ownv), (ps_ref.at[at], psv), ((above_ref, below_ref)[side], halov))
        return [pltpu.make_async_copy(src, dst.at[side], loads.at[side, i]) for i, (src, dst) in enumerate(pieces)]

    def store(side):
        return pltpu.make_async_copy(ownv.at[side], out_ref.at[pl.ds(side * (total - KH), KH)], stores.at[side])

    for side in range(2):
        for copy in fetch(side):
            copy.start()
    for side in range(2):
        for copy in fetch(side):
            copy.wait()
        scale, after = (grow, decay) if side == 0 else (decay, grow)

        def fill(q, _):
            for u in range(4):
                cut = pl.ds(pl.multiple_of((q * 4 + u) * LANES, LANES), LANES)
                x = halov[side, :, cut] * scale
                for s in (1, 2, 4, 8, 16):
                    gap = jnp.zeros((s, LANES), F32)
                    x = x + (jnp.concatenate([gap, x[:KH - s]], axis=0) if side
                             else jnp.concatenate([x[s:], gap], axis=0))
                ownv[side, :, cut] = ownv[side, :, cut] + psv[side, :, cut] * (x * after)
            return 0

        lax.fori_loop(0, ps_ref.shape[1] // LANES // 4, fill, 0)
        store(side).start()
    for side in range(2):
        store(side).wait()


def finish(partial, ps, above, below):
    band = pltpu.VMEM((2, KH, ps.shape[1]), F32)
    return pl.pallas_call(
        finish_body,
        out_shape=jax.ShapeDtypeStruct(ps.shape, F32),
        in_specs=[HBM, HBM, HBM, HBM],
        out_specs=HBM,
        scratch_shapes=[band, band, band, pltpu.SemaphoreType.DMA((2, 3)), pltpu.SemaphoreType.DMA((2,))],
        input_output_aliases={0: 0},
        name="finish",
    )(partial, ps, above, below)


def taps(distance):
    far = np.abs(distance)
    full = np.where(far <= KH, np.exp(np.float32(-2.0) * far.astype(np.float32) / np.float32(KH)), 0).astype(np.float32)
    top = full.astype(BF16)
    return top, (full - top.astype(np.float32)).astype(BF16)


def smoother(total):
    row, col = np.arange(total)[:, None], np.arange(256)[None, :]
    top, low = taps(np.where(col < total, row - col, total))
    return jnp.asarray(np.concatenate([top, top, low], axis=1))


def quick(flux, prior_std, w, rows, metas):
    head, tail = edges(w, prior_std, rows, metas)
    above = from_behind(tail, "win", 1)
    below = from_behind(head, "win", -1)
    partial = inner(w, head, tail, smoother(flux.shape[0]), prior_std, rows, metas)
    return finish(partial, prior_std, above, below)


def shards(flux, prior_std, footprint, obs_value, obs_weight, obs_hour, hour_offset, block_cell):
    count, nblk, width = footprint.shape
    own, early, ometa, nmeta = sort_both(obs_hour.reshape(1, count), hour_offset.T, block_cell.T,
                                         footprint.reshape(count * nblk, width), flux.shape[0])
    meta = from_behind(nmeta, "win", -1)
    theirs = [from_behind(early[0], "win", -1), from_behind(early[1], "win", -1)]
    mine = predict(flux, own, ometa)
    other = predict(flux, theirs[:1], meta)
    packet = predict(flux, theirs[1:], meta, 1, (mine, other, ometa, ometa))
    w, bad = exchange(packet, obs_value.reshape(8, LANES), obs_weight.reshape(8, LANES))
    return lax.cond(
        bad[2, 0] > 0.0,
        lambda: general(flux, prior_std, footprint, obs_value, obs_weight, obs_hour, hour_offset, block_cell),
        lambda: quick(flux, prior_std, w, [*own, *theirs], (ometa, meta)))


def solution(mesh):
    return jax.shard_map(
        shards,
        mesh=mesh,
        in_specs=(
            P("win", "tile"),
            P("win", "tile"),
            P("win", "tile", None),
            P("win"),
            P("win"),
            P("win"),
            P("win", "tile"),
            P("win", "tile"),
        ),
        out_specs=P("win", "tile"),
        check_vma=False,
    )
```

```python
import functools

import jax
import jax.numpy as jnp
import numpy as np
from jax import lax
from jax.experimental import pallas as pl
from jax.experimental.pallas import tpu as pltpu
from jax.sharding import PartitionSpec as P


KH = 24
LANES = 128
CELLS = 64
NBIN = 2 * CELLS
HEAD = 41 * LANES
NEAR = 32
META = CELLS + CELLS + 8
F32, BF16, I32 = jnp.float32, jnp.bfloat16, jnp.int32
NT = (((1,), (1,)), ((), ()))
MESH = pl.DeviceIdType.MESH
VM = pl.BlockSpec(memory_space=pltpu.VMEM)
HBM = pl.BlockSpec(memory_space=pltpu.HBM)


def tab_of(half):
    return pl.BlockSpec((8, LANES), lambda *_: (META // 8 * (half + 1) - 1, 0), memory_space=pltpu.SMEM)


def tabv_of(half):
    return pl.BlockSpec((8, LANES), lambda *_: (META // 8 * (half + 1) - 1, 0))


def tabs_from(metas):
    return [metas[0], metas[0], metas[1], metas[1]]


def iota(shape, dim):
    return lax.broadcasted_iota(I32, shape, dim)


def dot(a, b):
    return jnp.dot(a, b, preferred_element_type=F32)


def halves(v):
    top = v.astype(BF16).astype(F32)
    return top, v - top


def pick(table, lane):
    return jnp.take_along_axis(table, jnp.broadcast_to(lane, table.shape), axis=1, mode="promise_in_bounds")


def from_behind(value, axis, steps):
    count = lax.axis_size(axis)
    initial, last = (max(0, -steps), min(count, count - steps))
    return lax.ppermute(value, axis, [(source, source + steps) for source in range(initial, last)])


def extended(cells, sides, width):
    for axis, dim in sides:
        count = lax.axis_size(axis)
        ends = count - 1
        head = lax.slice_in_dim(cells, 0, width, axis=dim)
        tail = lax.slice_in_dim(cells, cells.shape[dim] - width, cells.shape[dim], axis=dim)
        cells = jnp.concatenate(
            [
                lax.ppermute(tail, axis, [(i, (i + 1) % count) for i in range(ends)]),
                cells,
                lax.ppermute(head, axis, [((i + 1) % count, i) for i in range(ends)]),
            ],
            axis=dim,
        )
    return cells


def misfits(partial_value, obs_value, obs_weight):
    predicted = lax.psum(partial_value, "tile")
    return (predicted - obs_value) * obs_weight


def general(flux, prior_std, footprint, obs_value, obs_weight, obs_hour, hour_offset, block_cell):
    hours = flux.shape[0]
    cells = flux.shape[1]
    width = footprint.shape[2]
    per_hour = cells // width
    earlier = from_behind(flux, "win", 1)
    joined = jnp.concatenate([earlier, flux], axis=0).reshape(2 * hours * per_hour, width)
    flat = (hours + obs_hour[:, None] - hour_offset) * per_hour + block_cell
    picked = joined[flat]
    partial_value = jnp.einsum("onc,onc->o", footprint, picked, preferred_element_type=jnp.float32)
    weighted = misfits(partial_value, obs_value, obs_weight)
    contrib = weighted[:, None, None] * footprint.astype(jnp.float32)
    summed = jax.ops.segment_sum(
        contrib.reshape(-1, width), flat.reshape(-1), num_segments=2 * hours * per_hour
    )
    summed = summed.reshape(2 * hours, cells)
    returned = from_behind(summed[:hours], "win", -1)
    adjoint = summed[hours:] + returned
    scaled = prior_std * adjoint
    rim = extended(scaled, (("win", 0),), KH)
    rows = jnp.arange(hours, dtype=jnp.int32)[:, None]
    columns = jnp.arange(hours + 2 * KH, dtype=jnp.int32)[None, :]
    distance = columns - rows - KH
    kernel = jnp.where(
        jnp.abs(distance) <= KH, jnp.exp(-2.0 * jnp.abs(distance).astype(jnp.float32) / KH), 0.0
    )
    smoothed = jnp.dot(
        kernel, rim, preferred_element_type=jnp.float32, precision=lax.Precision.HIGHEST
    )
    return prior_std * smoothed


class Sorter:
    def __init__(self, nobs, hb, oh_ref, off_ref, cell_ref, metas, keyv, hourv, posv, tabv):
        self.nobs, self.hb, self.inputs, self.metas = nobs, hb, (oh_ref, off_ref, cell_ref), metas
        self.keyv, self.hourv, self.posv, self.tabv = keyv, hourv, posv, tabv
        self.nblk = off_ref.shape[0]
        self.lines = self.nblk * nobs // LANES
        self.cap = capacity(self.nblk * nobs)

    def prepare(self, which, aside):
        nobs, nblk, cap, lines = self.nobs, self.nblk, self.cap, self.lines
        keyv, hourv, posv, metas = self.keyv, self.hourv, self.posv, self.metas
        oh_ref, off_ref, cell_ref = self.inputs
        per = nobs // LANES
        span = HEAD // LANES - 1
        at0 = which * META
        bins = iota((NBIN, LANES), 0)
        lanes = iota((NBIN, LANES), 1)
        upper = (bins < lanes).astype(BF16)
        ones = jnp.ones((LANES, LANES), BF16)
        same = (bins // CELLS) == (lanes // CELLS)
        below = jnp.where(same & (lanes < bins), 1.0, 0.0).astype(BF16)
        before = jnp.where(same & (bins < lanes), 1.0, 0.0).astype(BF16)
        for c in range(per):
            cut = slice(which * nobs + c * LANES, which * nobs + (c + 1) * LANES)
            hour = oh_ref[:, cut] - off_ref[:, cut]
            early = hour < 0
            hour = jnp.where(early, hour + self.hb, hour)
            key = jnp.where(early, cell_ref[:, cut] + CELLS, cell_ref[:, cut])
            rim = (hour < KH) | (hour >= self.hb - KH)
            at = slice(c * nblk, (c + 1) * nblk)
            keyv[0, at, :] = jnp.where(rim, key, -1)
            keyv[1, at, :] = jnp.where(rim, -1, key)
            keyv[2, at, :] = key
            hourv[at, :] = (hour + 1).astype(F32)

        def count(r, total):
            first, second = total
            for u in range(4):
                first = first + jnp.where(bins == keyv[0, pl.ds(r * 4 + u, 1), :], 1.0, 0.0)
                second = second + jnp.where(bins == keyv[1, pl.ds(r * 4 + u, 1), :], 1.0, 0.0)
                aside(0, r, u)
            return first, second

        zero = jnp.zeros((NBIN, LANES), F32)
        first, second = lax.fori_loop(0, lines // 4, count, (zero, zero))
        first, second = first.astype(BF16), second.astype(BF16)
        ahead = [dot(v, upper) for v in (first, second)]
        rim_s = dot(first, ones)
        cnt_s = rim_s + dot(second, ones)
        rim_l = lax.dot_general(ones[:8], first, NT, preferred_element_type=F32)
        cnt_l = rim_l + lax.dot_general(ones[:8], second, NT, preferred_element_type=F32)

        def starts(cnt, left):
            tiles = jnp.floor((cnt + 15.0) * (1.0 / 16.0))
            coarse = jnp.floor(tiles * (1.0 / 128.0))
            fine = tiles - 128.0 * coarse

            def run(v):
                return dot(below, v.astype(BF16)) if left else dot(v.astype(BF16), before)

            return 16.0 * (128.0 * run(coarse) + run(fine))

        tight_l = starts(cnt_l, False)
        base = starts(cnt_s, True) + jnp.where(bins >= CELLS, float(cap), 0.0)
        line8 = iota((8, LANES), 0)
        limit = float(span * LANES)
        far = jnp.where((cnt_l > float(LANES)) | (rim_l > float(NEAR)) | (tight_l + cnt_l > limit), 1.0, 0.0)
        over = jnp.max(far, axis=1, keepdims=True)
        tab = jnp.where(line8 == 0, jnp.minimum(cnt_l, float(LANES)),
                        jnp.where(line8 == 1, jnp.minimum(tight_l, limit), over)).astype(I32)
        self.tabv[...] = tab
        metas[0][at0 + 2 * CELLS:at0 + META, :] = tab
        metas[1][at0 + 2 * CELLS:at0 + META, :] = pltpu.roll(tab, CELLS, 1)
        for turn in range(2):
            def place(r, acc):
                for u in range(4):
                    at = pl.ds(r * 4 + u, 1)
                    hot = bins == keyv[turn, at, :]
                    posf = jnp.sum(jnp.where(hot, acc, 0.0), axis=0, keepdims=True).astype(I32)
                    posv[at, :] = posf if turn == 0 else posv[at, :] + posf
                    acc = jnp.where(hot, acc + 1.0, acc)
                    aside(1 + turn, r, u)
                return acc

            lax.fori_loop(0, lines // 4, place, base + ahead[turn] + (rim_s if turn else 0.0))
        aside(-1, 0, 0)
        starts_l = tight_l + jnp.where(iota((8, LANES), 1) >= CELLS, float(cap), 0.0)
        for g in range(lines // 8):
            at = slice(g * 8, (g + 1) * 8)
            key = keyv[2, at, :]
            rank = posv[at, :] - pick(starts_l, key).astype(I32)
            keyv[0, at, :] = rank
            spot = jnp.where(rank < LANES, (key & (CELLS - 1)) * LANES + rank, -1)
            lo = at0 + CELLS + g * 8
            metas[0][lo:lo + 8, :] = jnp.where(key < CELLS, spot, -1)
            metas[1][lo:lo + 8, :] = jnp.where(key < CELLS, -1, spot)
        obs = iota((1, LANES), 1).astype(F32)
        done = zero
        for c in range(per):
            def gather(r, acc):
                marks, spots = [], []
                for u in range(2):
                    at = pl.ds(c * nblk + r * 2 + u, 1)
                    hot = bins == keyv[2, at, :]
                    marks.append(jnp.concatenate(
                        [jnp.where(hot, v, 0.0).astype(BF16) for v in (hourv[at, :], obs)], axis=0))
                    spots.append(jnp.where(bins == keyv[0, at, :], 1.0, 0.0).astype(BF16))
                    aside(3, r + c * (nblk // 2), u)
                return acc + lax.dot_general(jnp.concatenate(marks, axis=1), jnp.concatenate(spots, axis=1), NT,
                                             preferred_element_type=F32)

            acc = lax.fori_loop(0, nblk // 2, gather, jnp.zeros((2 * NBIN, LANES), F32))
            hour, low = acc[:NBIN], acc[NBIN:]
            done = done + jnp.where(hour > 0.0, hour + 256.0 * (low + float(c * LANES)), 0.0)
        done = done.astype(I32)
        metas[0][at0:at0 + CELLS, :] = done[:CELLS]
        metas[1][at0:at0 + CELLS, :] = done[CELLS:]


def capacity(n):
    return n + CELLS * 16 + LANES


def blank_block(rows, cap, q):
    blocks = HEAD // LANES
    q = jnp.minimum(q, 2 * blocks - 1)
    at = jnp.where(q < blocks, q, q - blocks + cap // LANES)
    rows[pl.ds(pl.multiple_of(at * LANES, LANES), LANES), :] = jnp.zeros((LANES, LANES), F32)


def unpack_block(stage, fpv, q):
    at = pl.multiple_of(q * LANES, LANES)
    stage[pl.ds(at, LANES), :] = fpv[pl.ds(at, LANES), :].astype(F32)


def permute_all(rows, stage, posv, slots, sems, nblk):
    half = nblk // 2

    def load(i, k):
        return pltpu.make_async_copy(posv.at[pl.ds(i * nblk + k * half, half)], slots[k], sems.at[k])

    for k in range(2):
        load(0, k).start()
    last = posv.shape[0] // nblk - 1

    def batch(i, _):
        src = i * (LANES * nblk)
        for k in range(2):
            load(i, k).wait()
            for q in range(half):
                for l in range(LANES):
                    rows[pl.ds(slots[k][q, l], 1), :] = stage[pl.ds(src + l * nblk + k * half + q, 1), :]

            @pl.when(i < last)
            def _():
                load(i + 1, k).start()

        return 0

    lax.fori_loop(0, last + 1, batch, 0)


def convert_all(rows, cap, outs, ends):
    for side in range(2):
        end = jnp.minimum(ends[side], HEAD - LANES)
        blocks = jnp.minimum(lax.shift_right_logical(end + 270, 7), HEAD // LANES)

        def convert(i, _):
            at = pl.multiple_of(i * LANES, LANES)
            src = pl.multiple_of(at + side * cap, LANES)
            outs[side][pl.ds(at, LANES), :] = rows[pl.ds(src, LANES), :].astype(BF16)
            return 0

        lax.fori_loop(0, blocks, convert, 0)


def sort_body(nobs, which, hb, *refs):
    oh_ref, off_ref, cell_ref, fp_ref = refs[:4]
    given = refs[4:4 + 4 * which]
    own_ref, neg_ref, ometa_ref, nmeta_ref = refs[4 + 4 * which:8 + 4 * which]
    fpv, stage, rows, keyv, hourv, posv, slot0, slot1, tabs, tabv, sems = refs[-11:]
    nblk = off_ref.shape[0]
    n = nobs * nblk
    fetch = pltpu.make_async_copy(fp_ref.at[pl.ds(which * n, n)], fpv, sems.at[0])
    fetch.start()
    if which:
        keeps = [pltpu.make_async_copy(given[2 + k], refs[12 + k], sems.at[4 + k]) for k in range(2)]
        for keep in keeps:
            keep.start()
        ometa_ref[:META, :] = given[0][...]
        nmeta_ref[:META, :] = given[1][...]
    sorter = Sorter(nobs, hb, oh_ref, off_ref, cell_ref, (ometa_ref, nmeta_ref), keyv, hourv, posv, tabv)
    cap = sorter.cap

    def aside(phase, r, u):
        if phase == -1:
            fetch.wait()
        elif phase == 0 and u < 3:
            blank_block(rows, cap, r * 6 + u * 2)
            blank_block(rows, cap, r * 6 + u * 2 + 1)
        elif phase == 3:
            unpack_block(stage, fpv, r * 2 + u)

    sorter.prepare(which, aside)
    to_tab = pltpu.make_async_copy(tabv, tabs, sems.at[1])
    to_tab.start()
    permute_all(rows, stage, posv, (slot0, slot1), sems.at[pl.ds(2, 2)], nblk)
    to_tab.wait()
    ends = [tabs[1, k] + tabs[0, k] for k in (CELLS - 1, NBIN - 1)]
    convert_all(rows, cap, (own_ref, neg_ref), ends)
    if which:
        for keep in keeps:
            keep.wait()


def sort_half(oh, off, cell, fp2, which, hb, given=()):
    nblk, count = off.shape
    nobs = count // 2
    n = nobs * nblk
    cap = capacity(n)
    lines = n // LANES
    rows = jax.ShapeDtypeStruct((HEAD, LANES), BF16)
    meta = jax.ShapeDtypeStruct(((1 + which) * META, LANES), I32)
    kept = [jax.ShapeDtypeStruct(v.shape, v.dtype) for v in given[2:]]
    slot = pltpu.SMEM((nblk // 2, LANES), I32)
    return pl.pallas_call(
        functools.partial(sort_body, nobs, which, hb),
        out_shape=(rows, rows, meta, meta, *kept),
        in_specs=[VM, VM, VM, HBM] + ([VM, VM, HBM, HBM] if which else []),
        out_specs=(VM,) * (4 + 2 * which),
        scratch_shapes=[
            pltpu.VMEM((n, LANES), BF16), pltpu.VMEM((n, LANES), F32), pltpu.VMEM((2 * cap, LANES), F32),
            pltpu.VMEM((3, lines, LANES), I32), pltpu.VMEM((lines, LANES), F32), pltpu.VMEM((lines, LANES), I32),
            slot, slot, pltpu.SMEM((8, LANES), I32), pltpu.VMEM((8, LANES), I32), pltpu.SemaphoreType.DMA((6,))],
        compiler_params=pltpu.CompilerParams(vmem_limit_bytes=20 << 20),
        cost_estimate=pl.CostEstimate(flops=10**9, bytes_accessed=50 << 20, transcendentals=0),
        name="sort_half",
    )(oh, off, cell, fp2, *given)


def predict_body(k, slot, chained, *refs):
    flux_ref, rows, meta, tabs = refs[0], refs[1:1 + k], refs[1 + k], refs[2 + k:2 + 2 * k]
    first = [(slot + i) * META for i in range(k)]
    out_ref, tablev = refs[-2:]
    hours = iota((flux_ref.shape[0], k * LANES), 0) + 1
    step = 8

    def group(g, _):
        for u in range(step):
            b = g * step + u
            hour = jnp.concatenate([meta[pl.ds(f + b, 1), :] & 255 for f in first], axis=1)
            fp = jnp.concatenate(
                [rows[i][pl.ds(pl.multiple_of(tabs[i][1, b], 16), LANES), :] for i in range(k)], axis=0)
            local = flux_ref[:, pl.ds(pl.multiple_of(b * LANES, LANES), LANES)]
            full = lax.dot_general(local, fp, NT, preferred_element_type=F32)
            value = jnp.sum(jnp.where(hours == hour, full, 0.0), axis=0, keepdims=True)
            for i in range(k):
                tablev[i, pl.ds(b, 1), :] = value[:, i * LANES:(i + 1) * LANES]
        return 0

    lax.fori_loop(0, CELLS // step, group, 0)
    per = 4
    lines = []
    for i in range(k):
        lo = first[i] + CELLS
        spots = [meta[lo + g * 8:lo + (g + 1) * 8, :] for g in range(8)]
        cell = [lax.shift_right_arithmetic(s, 7) for s in spots]
        lane = [s & 127 for s in spots]

        def collect(q, acc):
            acc = list(acc)
            for u in range(4):
                b = q * 4 + u
                row = jnp.broadcast_to(tablev[i, pl.ds(b, 1), :], (8, LANES))
                for g in range(8):
                    acc[g // 2] = acc[g // 2] + jnp.where(cell[g] == b, pick(row, lane[g]), 0.0)
            return tuple(acc)

        acc = lax.fori_loop(0, CELLS // 4, collect, (jnp.zeros((8, LANES), F32),) * per)
        lines.append(jnp.concatenate([jnp.sum(a, axis=0, keepdims=True) for a in acc], axis=0))
    blank = jnp.zeros((per, LANES), F32)
    if k == 2:
        out_ref[...] = jnp.concatenate(lines, axis=0)
    elif not chained:
        out_ref[...] = jnp.concatenate([lines[0], blank], axis=0)
    else:
        mine_ref, other_ref, tab0_ref, tab1_ref = refs[2 + 2 * k:6 + 2 * k]
        out_ref[0] = mine_ref[...]
        out_ref[1] = jnp.concatenate([blank, lines[0]], axis=0) + other_ref[...]
        out_ref[2] = jnp.maximum(tab0_ref[...], tab1_ref[...]).astype(F32)


def predict(flux, rows, meta, slot=0, more=()):
    k = len(rows)
    tabs = [tab_of(slot + i) for i in range(k)]
    return pl.pallas_call(
        functools.partial(predict_body, k, slot, len(more) > 0),
        grid=(1,),
        out_shape=jax.ShapeDtypeStruct((3, 8, LANES) if more else (8, LANES), F32),
        in_specs=[VM] * (k + 2) + tabs + ([VM, VM, tabv_of(0), tabv_of(1)] if more else []),
        out_specs=VM,
        scratch_shapes=[pltpu.VMEM((k, CELLS, LANES), F32)],
        compiler_params=pltpu.CompilerParams(vmem_limit_bytes=8 << 20),
        cost_estimate=pl.CostEstimate(flops=k * 2 * 240 * 8192 * 128, bytes_accessed=(10 + 5 * k) << 20,
                                      transcendentals=0),
        name="predict",
    )(flux, *rows, meta, *([meta] * k), *more)


def exchange_body(p_ref, value_ref, weight_ref, w_ref, bad_ref, pair, prev_n, next_o, next_obs, flags, mine,
                  s_pair, s_side, s_flag, r_pair, r_side, r_obs, r_flag):
    wins, tiles = lax.axis_size("win"), lax.axis_size("tile")
    w, t = lax.axis_index("win"), lax.axis_index("tile")
    up, down = w > 0, w < wins - 1
    barrier = pltpu.get_barrier_semaphore()
    peers = [lax.rem(t + d, tiles) for d in range(tiles)]
    others = [lax.rem(w + d, wins) for d in range(wins)]

    def greet(device):
        pl.semaphore_signal(barrier, inc=1, device_id=device, device_id_type=MESH)

    for d in range(1, tiles):
        greet((w, peers[d]))
    for d in range(1, wins):
        greet((others[d], t))

    @pl.when(up)
    def _():
        for d in range(1, tiles):
            greet((w - 1, peers[d]))

    @pl.when(down)
    def _():
        for d in range(1, tiles):
            greet((w + 1, peers[d]))

    sides = jnp.where(up, 1, 0) + jnp.where(down, 1, 0)
    pl.semaphore_wait(barrier, tiles - 1 + wins - 1 + sides * (tiles - 1))

    def push(src, dst, ssem, rsem, device):
        return pltpu.make_async_remote_copy(src_ref=src, dst_ref=dst, send_sem=ssem, recv_sem=rsem,
                                            device_id=device, device_id_type=MESH)

    def peer(d, at):
        return push(p_ref, pair.at[at], s_pair.at[d], r_pair.at[at], (w, peers[d]))

    def above(d, at):
        return push(p_ref.at[0], next_o.at[at], s_side.at[0, d], r_side.at[0, at], (w - 1, peers[d]))

    def under(d, at):
        return push(p_ref.at[1], prev_n.at[at], s_side.at[1, d], r_side.at[1, at], (w + 1, peers[d]))

    def obs_to(v):
        return [push(ref, next_obs.at[k], s_side.at[2, k], r_obs.at[k], (v, t))
                for k, ref in enumerate((value_ref, weight_ref))]

    def flag(d, at):
        return push(mine, flags.at[at], s_flag.at[d], r_flag.at[at], (others[d], t))

    for d in range(1, tiles):
        peer(d, t).start()

    @pl.when(up)
    def _():
        for d in range(tiles):
            above(d, t).start()
        for copy in obs_to(w - 1):
            copy.start()

    @pl.when(down)
    def _():
        for d in range(tiles):
            under(d, t).start()

    own, later, bad = p_ref[0], p_ref[1], p_ref[2]
    for d in range(1, tiles):
        peer(d, peers[d]).wait_recv()
        got = pair.at[peers[d]]
        own, later, bad = own + got[0], later + got[1], jnp.maximum(bad, got[2])
    mine[...] = bad
    w_ref[0] = own
    w_ref[1] = later

    @pl.when(up)
    def _():
        total = w_ref[0]
        for d in range(tiles):
            under(d, peers[d]).wait_recv()
            total = total + prev_n[peers[d]]
        w_ref[0] = total

    w_ref[0] = (w_ref[0] - value_ref[...]) * weight_ref[...]
    for d in range(1, wins):
        flag(d, w).start()

    @pl.when(down)
    def _():
        total = w_ref[1]
        for d in range(tiles):
            above(d, peers[d]).wait_recv()
            total = total + next_o[peers[d]]
        for copy in obs_to(w + 1):
            copy.wait_recv()
        w_ref[1] = (total - next_obs[0]) * next_obs[1]

    for d in range(1, wins):
        flag(d, others[d]).wait_recv()
        bad = jnp.maximum(bad, flags[others[d]])
    bad_ref[...] = bad
    for d in range(1, wins):
        flag(d, w).wait_send()
    for d in range(1, tiles):
        peer(d, t).wait_send()

    @pl.when(up)
    def _():
        for copy in obs_to(w - 1):
            copy.wait_send()
        for d in range(tiles):
            above(d, t).wait_send()

    @pl.when(down)
    def _():
        for d in range(tiles):
            under(d, t).wait_send()


def exchange(packet, value, weight):
    wins, tiles = lax.axis_size("win"), lax.axis_size("tile")
    block = pltpu.VMEM((tiles, 8, LANES), F32)
    sem = pltpu.SemaphoreType.DMA
    return pl.pallas_call(
        exchange_body,
        out_shape=(jax.ShapeDtypeStruct((2, 8, LANES), F32), jax.ShapeDtypeStruct((8, LANES), F32)),
        in_specs=[VM, VM, VM],
        out_specs=(VM, VM),
        scratch_shapes=[pltpu.VMEM((tiles, 3, 8, LANES), F32), block, block, pltpu.VMEM((2, 8, LANES), F32),
                        pltpu.VMEM((wins, 8, LANES), F32), pltpu.VMEM((8, LANES), F32),
                        sem((tiles,)), sem((3, tiles)), sem((wins,)), sem((tiles,)), sem((2, tiles)), sem((2,)),
                        sem((wins,))],
        compiler_params=pltpu.CompilerParams(collective_id=3, has_side_effects=True, vmem_limit_bytes=2 << 20),
        name="exchange",
    )(packet, value, weight)


def weigh(code, tables, slots):
    got = [pick(table, lax.shift_right_logical(code, 8) & 127) for table in tables]
    got = got[0] if len(got) == 1 else jnp.where(iota((8, LANES), 1) < 2 * NEAR, got[0], got[1])
    mine = iota((8, LANES), 0) == lax.shift_right_logical(code, 15) + slots
    return jnp.sum(jnp.where(mine, got, 0.0), axis=0, keepdims=True)


def spread(hour, hours, w):
    hit = hours == hour
    return [jnp.where(hit, v, 0.0).astype(BF16) for v in halves(w)]


def edges_body(w_ref, ps_ref, *refs):
    rows, metas, tabs = refs[0:4], refs[4:6], refs[6:10]
    head_ref, tail_ref = refs[10:]
    total = ps_ref.shape[0]
    band = iota((2 * KH, LANES), 0)
    hours = jnp.where(band < KH, band, band + (total - 2 * KH)) + 1
    quarter = lax.shift_right_logical(iota((1, LANES), 1), 5)
    slots = (quarter & 1) * 4
    tables = [w_ref[0], w_ref[1]]

    def group(g, _):
        for u in range(4):
            b = g * 4 + u
            codes = [metas[i // 2][pl.ds((i % 2) * META + b, 1), :] for i in range(4)]
            code = codes[0]
            fps = []
            for i in range(4):
                if i:
                    code = jnp.where(quarter == i, pltpu.roll(codes[i], i * NEAR, 1), code)
                fps.append(rows[i][pl.ds(pl.multiple_of(tabs[i][1, b], 16), NEAR), :])
            fp = jnp.concatenate(fps, axis=0)
            left = jnp.concatenate(spread(code & 255, hours, weigh(code, tables, slots)), axis=1)
            part = dot(left, jnp.concatenate([fp, fp], axis=0))
            col = pl.ds(pl.multiple_of(b * LANES, LANES), LANES)
            head_ref[:, col] = part[:KH] * ps_ref[:KH, col]
            tail_ref[:, col] = part[KH:] * ps_ref[total - KH:, col]
        return 0

    lax.fori_loop(0, CELLS // 4, group, 0)


def edges(w, ps, rows, metas):
    cells = ps.shape[1]
    return pl.pallas_call(
        edges_body,
        grid=(1,),
        out_shape=(jax.ShapeDtypeStruct((KH, cells), F32), jax.ShapeDtypeStruct((KH, cells), F32)),
        in_specs=[VM, VM]
        + [VM] * 4 + [VM] * 2 + [tab_of(0), tab_of(1)] * 2,
        out_specs=(VM, VM),
        compiler_params=pltpu.CompilerParams(vmem_limit_bytes=8 << 20),
        cost_estimate=pl.CostEstimate(flops=10**8, bytes_accessed=8 << 20, transcendentals=0),
        name="edges",
    )(w, ps, *rows, *metas, *tabs_from(metas))


def inner_body(w_ref, head_ref, tail_ref, kern_ref, ps_ref, *refs):
    rows, metas, tabs = refs[0:4], refs[4:6], refs[6:10]
    out_ref, outv, sv, osems = refs[10:]
    total, cells = ps_ref.shape
    parts = 16
    wide = cells // parts
    per = CELLS // parts
    inside = total - 2 * KH

    def drain(p):
        at = pl.ds(pl.multiple_of(p * wide, LANES), wide)
        return pltpu.make_async_copy(outv.at[p & 1], out_ref.at[:, at], osems.at[p & 1])

    hours = iota((inside, LANES), 0) + KH + 1
    pad = jnp.zeros((16, wide), BF16)

    def part_of(p, _):
        for u in range(per):
            b = p * per + u
            left, right = [], []
            for i in range(4):
                code = metas[i // 2][pl.ds((i % 2) * META + b, 1), :]
                left += spread(code & 255, hours, weigh(code, [w_ref[i // 2]], (i % 2) * 4))
                fp = rows[i][pl.ds(pl.multiple_of(tabs[i][1, b], 16), LANES), :]
                right += [fp, fp]
            part = dot(jnp.concatenate(left, axis=1), jnp.concatenate(right, axis=0))
            col = pl.ds(pl.multiple_of(b * LANES, LANES), LANES)
            here = slice(u * LANES, (u + 1) * LANES)
            sv[:KH, here] = head_ref[:, col]
            sv[KH:total - KH, here] = part * ps_ref[KH:total - KH, col]
            sv[total - KH:, here] = tail_ref[:, col]
        top, low = halves(sv[...])
        top, low = top.astype(BF16), low.astype(BF16)
        stack = jnp.concatenate([top, pad, low, pad, top, pad], axis=0)
        smooth = dot(kern_ref[...], stack)

        @pl.when(p >= 2)
        def _():
            drain(p - 2).wait()

        outv[p & 1] = smooth * ps_ref[:, pl.ds(pl.multiple_of(p * wide, LANES), wide)]
        drain(p).start()
        return 0

    lax.fori_loop(0, parts, part_of, 0)
    for p in (parts - 2, parts - 1):
        drain(p).wait()


def inner(w, head, tail, kern, ps, rows, metas):
    wide = ps.shape[1] // 16
    return pl.pallas_call(
        inner_body,
        grid=(1,),
        out_shape=jax.ShapeDtypeStruct(ps.shape, F32),
        in_specs=[VM, VM, VM, VM, VM] + [VM] * 4 + [VM] * 2 + [tab_of(0), tab_of(1)] * 2,
        out_specs=HBM,
        scratch_shapes=[pltpu.VMEM((2, ps.shape[0], wide), F32), pltpu.VMEM((ps.shape[0], wide), F32),
                        pltpu.SemaphoreType.DMA((2,))],
        compiler_params=pltpu.CompilerParams(vmem_limit_bytes=10 << 20),
        cost_estimate=pl.CostEstimate(flops=4 * 10**9, bytes_accessed=40 << 20, transcendentals=0),
        name="inner",
    )(w, head, tail, kern, ps, *rows, *metas, *tabs_from(metas))


def finish_body(own_ref, ps_ref, above_ref, below_ref, out_ref, ownv, loads, stores):
    total = ps_ref.shape[0]
    row = iota((KH, LANES), 0).astype(F32)
    grow, decay = jnp.exp((row - KH) * (2.0 / KH)), jnp.exp(row * (-2.0 / KH))

    def load(side):
        return pltpu.make_async_copy(own_ref.at[pl.ds(side * (total - KH), KH)], ownv.at[side], loads.at[side])

    def store(side):
        return pltpu.make_async_copy(ownv.at[side], out_ref.at[pl.ds(side * (total - KH), KH)], stores.at[side])

    for side in range(2):
        load(side).start()
    for side in range(2):
        load(side).wait()
        scale, after = (grow, decay) if side == 0 else (decay, grow)
        halo_ref = (above_ref, below_ref)[side]
        at = pl.ds(side * (total - KH), KH)

        def fill(q, _):
            for u in range(4):
                cut = pl.ds(pl.multiple_of((q * 4 + u) * LANES, LANES), LANES)
                x = halo_ref[:, cut] * scale
                for s in (1, 2, 4, 8, 16):
                    gap = jnp.zeros((s, LANES), F32)
                    x = x + (jnp.concatenate([gap, x[:KH - s]], axis=0) if side
                             else jnp.concatenate([x[s:], gap], axis=0))
                ownv[side, :, cut] = ownv[side, :, cut] + ps_ref[at, cut] * (x * after)
            return 0

        lax.fori_loop(0, ps_ref.shape[1] // LANES // 4, fill, 0)
        store(side).start()
    for side in range(2):
        store(side).wait()


def finish(partial, ps, above, below):
    return pl.pallas_call(
        finish_body,
        out_shape=jax.ShapeDtypeStruct(ps.shape, F32),
        in_specs=[HBM, VM, VM, VM],
        out_specs=HBM,
        scratch_shapes=[pltpu.VMEM((2, KH, ps.shape[1]), F32), pltpu.SemaphoreType.DMA((2,)),
                        pltpu.SemaphoreType.DMA((2,))],
        input_output_aliases={0: 0},
        compiler_params=pltpu.CompilerParams(vmem_limit_bytes=4 << 20),
        name="finish",
    )(partial, ps, above, below)


def taps(distance):
    far = np.abs(distance)
    full = np.where(far <= KH, np.exp(np.float32(-2.0) * far.astype(np.float32) / np.float32(KH)), 0).astype(np.float32)
    top = full.astype(BF16)
    return top, (full - top.astype(np.float32)).astype(BF16)


def smoother(total):
    row, col = np.arange(total)[:, None], np.arange(256)[None, :]
    top, low = taps(np.where(col < total, row - col, total))
    return jnp.asarray(np.concatenate([top, top, low], axis=1))


def quick(flux, prior_std, w, rows, metas):
    head, tail = edges(w, prior_std, rows, metas)
    above = from_behind(tail, "win", 1)
    below = from_behind(head, "win", -1)
    partial = inner(w, head, tail, smoother(flux.shape[0]), prior_std, rows, metas)
    return finish(partial, prior_std, above, below)


def shards(flux, prior_std, footprint, obs_value, obs_weight, obs_hour, hour_offset, block_cell):
    count, nblk, width = footprint.shape
    inputs = (obs_hour.reshape(1, count), hour_offset.T, block_cell.T, footprint.reshape(count * nblk, width))
    own0, early0, ometa, nmeta = sort_half(*inputs, 0, flux.shape[0])
    theirs0 = from_behind(early0, "win", -1)
    own1, early1, ometa, nmeta, ps, near = sort_half(*inputs, 1, flux.shape[0], (ometa, nmeta, prior_std, flux))
    meta = from_behind(nmeta, "win", -1)
    theirs1 = from_behind(early1, "win", -1)
    mine = predict(near, (own0, own1), ometa)
    other = predict(near, (theirs0,), meta)
    packet = predict(near, (theirs1,), meta, 1, (mine, other, ometa, ometa))
    w, bad = exchange(packet, obs_value.reshape(8, LANES), obs_weight.reshape(8, LANES))
    return lax.cond(
        bad[2, 0] > 0.0,
        lambda: general(flux, prior_std, footprint, obs_value, obs_weight, obs_hour, hour_offset, block_cell),
        lambda: quick(flux, ps, w, [own0, own1, theirs0, theirs1], (ometa, meta)))


def solution(mesh):
    return jax.shard_map(
        shards,
        mesh=mesh,
        in_specs=(
            P("win", "tile"),
            P("win", "tile"),
            P("win", "tile", None),
            P("win"),
            P("win"),
            P("win"),
            P("win", "tile"),
            P("win", "tile"),
        ),
        out_specs=P("win", "tile"),
        check_vma=False,
    )
```

```python
import functools

import jax
import jax.numpy as jnp
import numpy as np
from jax import lax
from jax.experimental import pallas as pl
from jax.experimental.pallas import tpu as pltpu
from jax.sharding import PartitionSpec as P


KH = 24
LANES = 128
CELLS = 64
NBIN = 2 * CELLS
HEAD = 41 * LANES
NEAR = 32
META = CELLS + CELLS + 8
F32, BF16, I32 = jnp.float32, jnp.bfloat16, jnp.int32
NT = (((1,), (1,)), ((), ()))
MESH = pl.DeviceIdType.MESH
VM = pl.BlockSpec(memory_space=pltpu.VMEM)
HBM = pl.BlockSpec(memory_space=pltpu.HBM)


def tab_of(half):
    return pl.BlockSpec((8, LANES), lambda *_: (META // 8 * (half + 1) - 1, 0), memory_space=pltpu.SMEM)


def tabv_of(half):
    return pl.BlockSpec((8, LANES), lambda *_: (META // 8 * (half + 1) - 1, 0))


def tabs_from(metas):
    return [metas[0], metas[0], metas[1], metas[1]]


def iota(shape, dim):
    return lax.broadcasted_iota(I32, shape, dim)


def dot(a, b):
    return jnp.dot(a, b, preferred_element_type=F32)


def halves(v):
    top = v.astype(BF16).astype(F32)
    return top, v - top


def pick(table, lane):
    return jnp.take_along_axis(table, jnp.broadcast_to(lane, table.shape), axis=1, mode="promise_in_bounds")


def from_behind(value, axis, steps):
    count = lax.axis_size(axis)
    initial, last = (max(0, -steps), min(count, count - steps))
    return lax.ppermute(value, axis, [(source, source + steps) for source in range(initial, last)])


def extended(cells, sides, width):
    for axis, dim in sides:
        count = lax.axis_size(axis)
        ends = count - 1
        head = lax.slice_in_dim(cells, 0, width, axis=dim)
        tail = lax.slice_in_dim(cells, cells.shape[dim] - width, cells.shape[dim], axis=dim)
        cells = jnp.concatenate(
            [
                lax.ppermute(tail, axis, [(i, (i + 1) % count) for i in range(ends)]),
                cells,
                lax.ppermute(head, axis, [((i + 1) % count, i) for i in range(ends)]),
            ],
            axis=dim,
        )
    return cells


def misfits(partial_value, obs_value, obs_weight):
    predicted = lax.psum(partial_value, "tile")
    return (predicted - obs_value) * obs_weight


def general(flux, prior_std, footprint, obs_value, obs_weight, obs_hour, hour_offset, block_cell):
    hours = flux.shape[0]
    cells = flux.shape[1]
    width = footprint.shape[2]
    per_hour = cells // width
    earlier = from_behind(flux, "win", 1)
    joined = jnp.concatenate([earlier, flux], axis=0).reshape(2 * hours * per_hour, width)
    flat = (hours + obs_hour[:, None] - hour_offset) * per_hour + block_cell
    picked = joined[flat]
    partial_value = jnp.einsum("onc,onc->o", footprint, picked, preferred_element_type=jnp.float32)
    weighted = misfits(partial_value, obs_value, obs_weight)
    contrib = weighted[:, None, None] * footprint.astype(jnp.float32)
    summed = jax.ops.segment_sum(
        contrib.reshape(-1, width), flat.reshape(-1), num_segments=2 * hours * per_hour
    )
    summed = summed.reshape(2 * hours, cells)
    returned = from_behind(summed[:hours], "win", -1)
    adjoint = summed[hours:] + returned
    scaled = prior_std * adjoint
    rim = extended(scaled, (("win", 0),), KH)
    rows = jnp.arange(hours, dtype=jnp.int32)[:, None]
    columns = jnp.arange(hours + 2 * KH, dtype=jnp.int32)[None, :]
    distance = columns - rows - KH
    kernel = jnp.where(
        jnp.abs(distance) <= KH, jnp.exp(-2.0 * jnp.abs(distance).astype(jnp.float32) / KH), 0.0
    )
    smoothed = jnp.dot(
        kernel, rim, preferred_element_type=jnp.float32, precision=lax.Precision.HIGHEST
    )
    return prior_std * smoothed


class Sorter:
    def __init__(self, nobs, hb, oh_ref, off_ref, cell_ref, metas, keyv, hourv, posv, tabv):
        self.nobs, self.hb, self.inputs, self.metas = nobs, hb, (oh_ref, off_ref, cell_ref), metas
        self.keyv, self.hourv, self.posv, self.tabv = keyv, hourv, posv, tabv
        self.nblk = off_ref.shape[0]
        self.lines = self.nblk * nobs // LANES
        self.cap = capacity(self.nblk * nobs)

    def prepare(self, which, aside):
        nobs, nblk, cap, lines = self.nobs, self.nblk, self.cap, self.lines
        keyv, hourv, posv, metas = self.keyv, self.hourv, self.posv, self.metas
        oh_ref, off_ref, cell_ref = self.inputs
        per = nobs // LANES
        span = HEAD // LANES - 1
        at0 = which * META
        bins = iota((NBIN, LANES), 0)
        lanes = iota((NBIN, LANES), 1)
        upper = (bins < lanes).astype(BF16)
        ones = jnp.ones((LANES, LANES), BF16)
        same = (bins // CELLS) == (lanes // CELLS)
        below = jnp.where(same & (lanes < bins), 1.0, 0.0).astype(BF16)
        before = jnp.where(same & (bins < lanes), 1.0, 0.0).astype(BF16)
        for c in range(per):
            cut = slice(which * nobs + c * LANES, which * nobs + (c + 1) * LANES)
            hour = oh_ref[:, cut] - off_ref[:, cut]
            early = hour < 0
            hour = jnp.where(early, hour + self.hb, hour)
            key = jnp.where(early, cell_ref[:, cut] + CELLS, cell_ref[:, cut])
            rim = (hour < KH) | (hour >= self.hb - KH)
            at = slice(c * nblk, (c + 1) * nblk)
            keyv[0, at, :] = jnp.where(rim, key, -1)
            keyv[1, at, :] = jnp.where(rim, -1, key)
            keyv[2, at, :] = key
            hourv[at, :] = (hour + 1).astype(F32)

        def count(r, total):
            first, second = total
            for u in range(4):
                first = first + jnp.where(bins == keyv[0, pl.ds(r * 4 + u, 1), :], 1.0, 0.0)
                second = second + jnp.where(bins == keyv[1, pl.ds(r * 4 + u, 1), :], 1.0, 0.0)
                aside(0, r, u)
            return first, second

        zero = jnp.zeros((NBIN, LANES), F32)
        first, second = lax.fori_loop(0, lines // 4, count, (zero, zero))
        first, second = first.astype(BF16), second.astype(BF16)
        ahead = [dot(v, upper) for v in (first, second)]
        rim_s = dot(first, ones)
        cnt_s = rim_s + dot(second, ones)
        rim_l = lax.dot_general(ones[:8], first, NT, preferred_element_type=F32)
        cnt_l = rim_l + lax.dot_general(ones[:8], second, NT, preferred_element_type=F32)

        def starts(cnt, left):
            tiles = jnp.floor((cnt + 15.0) * (1.0 / 16.0))
            coarse = jnp.floor(tiles * (1.0 / 128.0))
            fine = tiles - 128.0 * coarse

            def run(v):
                return dot(below, v.astype(BF16)) if left else dot(v.astype(BF16), before)

            return 16.0 * (128.0 * run(coarse) + run(fine))

        tight_l = starts(cnt_l, False)
        base = starts(cnt_s, True) + jnp.where(bins >= CELLS, float(cap), 0.0)
        line8 = iota((8, LANES), 0)
        limit = float(span * LANES)
        far = jnp.where((cnt_l > float(LANES)) | (rim_l > float(NEAR)) | (tight_l + cnt_l > limit), 1.0, 0.0)
        over = jnp.max(far, axis=1, keepdims=True)
        tab = jnp.where(line8 == 0, jnp.minimum(cnt_l, float(LANES)),
                        jnp.where(line8 == 1, jnp.minimum(tight_l, limit), over)).astype(I32)
        self.tabv[...] = tab
        metas[0][at0 + 2 * CELLS:at0 + META, :] = tab
        metas[1][at0 + 2 * CELLS:at0 + META, :] = pltpu.roll(tab, CELLS, 1)
        for turn in range(2):
            def place(r, acc):
                for u in range(4):
                    at = pl.ds(r * 4 + u, 1)
                    hot = bins == keyv[turn, at, :]
                    posf = jnp.sum(jnp.where(hot, acc, 0.0), axis=0, keepdims=True).astype(I32)
                    posv[at, :] = posf if turn == 0 else posv[at, :] + posf
                    acc = jnp.where(hot, acc + 1.0, acc)
                    aside(1 + turn, r, u)
                return acc

            lax.fori_loop(0, lines // 4, place, base + ahead[turn] + (rim_s if turn else 0.0))
        aside(-1, 0, 0)
        starts_l = tight_l + jnp.where(iota((8, LANES), 1) >= CELLS, float(cap), 0.0)
        for g in range(lines // 8):
            at = slice(g * 8, (g + 1) * 8)
            key = keyv[2, at, :]
            rank = posv[at, :] - pick(starts_l, key).astype(I32)
            keyv[0, at, :] = rank
            spot = jnp.where(rank < LANES, (key & (CELLS - 1)) * LANES + rank, -1)
            lo = at0 + CELLS + g * 8
            metas[0][lo:lo + 8, :] = jnp.where(key < CELLS, spot, -1)
            metas[1][lo:lo + 8, :] = jnp.where(key < CELLS, -1, spot)
        obs = iota((1, LANES), 1).astype(F32)
        done = zero
        for c in range(per):
            def gather(r, acc):
                marks, spots = [], []
                for u in range(2):
                    at = pl.ds(c * nblk + r * 2 + u, 1)
                    hot = bins == keyv[2, at, :]
                    marks.append(jnp.concatenate(
                        [jnp.where(hot, v, 0.0).astype(BF16) for v in (hourv[at, :], obs)], axis=0))
                    spots.append(jnp.where(bins == keyv[0, at, :], 1.0, 0.0).astype(BF16))
                    aside(3, r + c * (nblk // 2), u)
                return acc + lax.dot_general(jnp.concatenate(marks, axis=1), jnp.concatenate(spots, axis=1), NT,
                                             preferred_element_type=F32)

            acc = lax.fori_loop(0, nblk // 2, gather, jnp.zeros((2 * NBIN, LANES), F32))
            hour, low = acc[:NBIN], acc[NBIN:]
            done = done + jnp.where(hour > 0.0, hour + 256.0 * (low + float(c * LANES)), 0.0)
        done = done.astype(I32)
        metas[0][at0:at0 + CELLS, :] = done[:CELLS]
        metas[1][at0:at0 + CELLS, :] = done[CELLS:]


def capacity(n):
    return n + CELLS * 16 + LANES


def blank_block(rows, cap, q):
    blocks = HEAD // LANES
    q = jnp.minimum(q, 2 * blocks - 1)
    at = jnp.where(q < blocks, q, q - blocks + cap // LANES)
    rows[pl.ds(pl.multiple_of(at * LANES, LANES), LANES), :] = jnp.zeros((LANES, LANES), F32)


def unpack_block(stage, fpv, q):
    at = pl.multiple_of(q * LANES, LANES)
    stage[pl.ds(at, LANES), :] = fpv[pl.ds(at, LANES), :].astype(F32)


def permute_all(rows, stage, posv, slots, sems, nblk):
    half = nblk // 2

    def load(i, k):
        return pltpu.make_async_copy(posv.at[pl.ds(i * nblk + k * half, half)], slots[k], sems.at[k])

    for k in range(2):
        load(0, k).start()
    last = posv.shape[0] // nblk - 1

    def batch(i, _):
        src = i * (LANES * nblk)
        for k in range(2):
            load(i, k).wait()
            for q in range(half):
                for l in range(LANES):
                    rows[pl.ds(slots[k][q, l], 1), :] = stage[pl.ds(src + l * nblk + k * half + q, 1), :]

            @pl.when(i < last)
            def _():
                load(i + 1, k).start()

        return 0

    lax.fori_loop(0, last + 1, batch, 0)


def convert_all(rows, cap, outs, ends):
    for side in range(2):
        end = jnp.minimum(ends[side], HEAD - LANES)
        blocks = jnp.minimum(lax.shift_right_logical(end + 270, 7), HEAD // LANES)

        def convert(i, _):
            at = pl.multiple_of(i * LANES, LANES)
            src = pl.multiple_of(at + side * cap, LANES)
            outs[side][pl.ds(at, LANES), :] = rows[pl.ds(src, LANES), :].astype(BF16)
            return 0

        lax.fori_loop(0, blocks, convert, 0)


def sort_body(nobs, which, hb, *refs):
    oh_ref, off_ref, cell_ref, fp_ref = refs[:4]
    given = refs[4:4 + 4 * which]
    own_ref, neg_ref, ometa_ref, nmeta_ref = refs[4 + 4 * which:8 + 4 * which]
    fpv, stage, rows, keyv, hourv, posv, slot0, slot1, tabs, tabv, sems = refs[-11:]
    nblk = off_ref.shape[0]
    n = nobs * nblk
    fetch = pltpu.make_async_copy(fp_ref.at[pl.ds(which * n, n)], fpv, sems.at[0])
    fetch.start()
    if which:
        keeps = [pltpu.make_async_copy(given[2 + k], refs[12 + k], sems.at[4 + k]) for k in range(2)]
        for keep in keeps:
            keep.start()
        ometa_ref[:META, :] = given[0][...]
        nmeta_ref[:META, :] = given[1][...]
    sorter = Sorter(nobs, hb, oh_ref, off_ref, cell_ref, (ometa_ref, nmeta_ref), keyv, hourv, posv, tabv)
    cap = sorter.cap

    def aside(phase, r, u):
        if phase == -1:
            fetch.wait()
        elif phase == 0 and u < 3:
            blank_block(rows, cap, r * 6 + u * 2)
            blank_block(rows, cap, r * 6 + u * 2 + 1)
        elif phase == 3:
            unpack_block(stage, fpv, r * 2 + u)

    sorter.prepare(which, aside)
    to_tab = pltpu.make_async_copy(tabv, tabs, sems.at[1])
    to_tab.start()
    permute_all(rows, stage, posv, (slot0, slot1), sems.at[pl.ds(2, 2)], nblk)
    to_tab.wait()
    ends = [tabs[1, k] + tabs[0, k] for k in (CELLS - 1, NBIN - 1)]
    convert_all(rows, cap, (own_ref, neg_ref), ends)
    if which:
        for keep in keeps:
            keep.wait()


def sort_half(oh, off, cell, fp2, which, hb, given=()):
    nblk, count = off.shape
    nobs = count // 2
    n = nobs * nblk
    cap = capacity(n)
    lines = n // LANES
    rows = jax.ShapeDtypeStruct((HEAD, LANES), BF16)
    meta = jax.ShapeDtypeStruct(((1 + which) * META, LANES), I32)
    kept = [jax.ShapeDtypeStruct(v.shape, v.dtype) for v in given[2:]]
    slot = pltpu.SMEM((nblk // 2, LANES), I32)
    return pl.pallas_call(
        functools.partial(sort_body, nobs, which, hb),
        out_shape=(rows, rows, meta, meta, *kept),
        in_specs=[VM, VM, VM, HBM] + ([VM, VM, HBM, HBM] if which else []),
        out_specs=(VM,) * (4 + 2 * which),
        scratch_shapes=[
            pltpu.VMEM((n, LANES), BF16), pltpu.VMEM((n, LANES), F32), pltpu.VMEM((2 * cap, LANES), F32),
            pltpu.VMEM((3, lines, LANES), I32), pltpu.VMEM((lines, LANES), F32), pltpu.VMEM((lines, LANES), I32),
            slot, slot, pltpu.SMEM((8, LANES), I32), pltpu.VMEM((8, LANES), I32), pltpu.SemaphoreType.DMA((6,))],
        compiler_params=pltpu.CompilerParams(vmem_limit_bytes=20 << 20),
        cost_estimate=pl.CostEstimate(flops=10**9, bytes_accessed=50 << 20, transcendentals=0),
        name="sort_half",
    )(oh, off, cell, fp2, *given)


def predict_cells(flux_ref, rows, meta, tabs, first, tablev):
    k = len(rows)
    hours = iota((flux_ref.shape[0], k * LANES), 0) + 1
    step = 8

    def group(g, _):
        for u in range(step):
            b = g * step + u
            hour = jnp.concatenate([meta[pl.ds(f + b, 1), :] & 255 for f in first], axis=1)
            fp = jnp.concatenate(
                [rows[i][pl.ds(pl.multiple_of(tabs[i][1, b], 16), LANES), :] for i in range(k)], axis=0)
            local = flux_ref[:, pl.ds(pl.multiple_of(b * LANES, LANES), LANES)]
            full = lax.dot_general(local, fp, NT, preferred_element_type=F32)
            value = jnp.sum(jnp.where(hours == hour, full, 0.0), axis=0, keepdims=True)
            for i in range(k):
                tablev[i, pl.ds(b, 1), :] = value[:, i * LANES:(i + 1) * LANES]
        return 0

    lax.fori_loop(0, CELLS // step, group, 0)


def predict_sums(meta, first, tablev):
    lines = []
    for i in range(len(first)):
        lo = first[i] + CELLS
        spots = [meta[lo + g * 8:lo + (g + 1) * 8, :] for g in range(8)]
        cell = [lax.shift_right_arithmetic(s, 7) for s in spots]
        lane = [s & 127 for s in spots]

        def collect(q, acc):
            acc = list(acc)
            for u in range(4):
                b = q * 4 + u
                row = jnp.broadcast_to(tablev[i, pl.ds(b, 1), :], (8, LANES))
                for g in range(8):
                    acc[g // 2] = acc[g // 2] + jnp.where(cell[g] == b, pick(row, lane[g]), 0.0)
            return tuple(acc)

        acc = lax.fori_loop(0, CELLS // 4, collect, (jnp.zeros((8, LANES), F32),) * 4)
        lines.append(jnp.concatenate([jnp.sum(a, axis=0, keepdims=True) for a in acc], axis=0))
    return lines


def predict_binned(flux_ref, rows_ref, meta_ref, first):
    hours = iota((flux_ref.shape[0], LANES), 0) + 1
    eight, bins = iota((8, LANES), 0), iota((LANES, LANES), 0)
    step = 8

    def group(g, acc):
        left, right = [], []
        for u in range(step):
            b = g * step + u
            code = meta_ref[pl.ds(first + b, 1), :]
            fp = rows_ref[pl.ds(pl.multiple_of(b * LANES, LANES), LANES), :]
            local = flux_ref[:, pl.ds(pl.multiple_of(b * LANES, LANES), LANES)]
            full = lax.dot_general(local, fp, NT, preferred_element_type=F32)
            value = jnp.sum(jnp.where(hours == (code & 255), full, 0.0), axis=0, keepdims=True)
            here = eight == lax.shift_right_logical(code, 15)
            left.append(jnp.concatenate([jnp.where(here, v, 0.0) for v in halves(value)], axis=0).astype(BF16))
            right.append(jnp.where(bins == (lax.shift_right_logical(code, 8) & 127), 1.0, 0.0).astype(BF16))
        for at in range(0, step, 2):
            acc = acc + lax.dot_general(jnp.concatenate(left[at:at + 2], axis=1),
                                        jnp.concatenate(right[at:at + 2], axis=1), NT, preferred_element_type=F32)
        return acc

    acc = lax.fori_loop(0, CELLS // step, group, jnp.zeros((16, LANES), F32))
    return acc[:4] + acc[8:12]


def predict_body(k, *refs):
    flux_ref, rows, meta, tabs = refs[0], refs[1:1 + k], refs[1 + k], refs[2 + k:2 + 2 * k]
    out_ref, tablev = refs[-2:]
    first = [i * META for i in range(k)]
    predict_cells(flux_ref, rows, meta, tabs, first, tablev)
    lines = predict_sums(meta, first, tablev)
    out_ref[...] = jnp.concatenate(lines if k == 2 else lines + [jnp.zeros((4, LANES), F32)], axis=0)


def predict(flux, rows, meta):
    k = len(rows)
    return pl.pallas_call(
        functools.partial(predict_body, k),
        grid=(1,),
        out_shape=jax.ShapeDtypeStruct((8, LANES), F32),
        in_specs=[VM] * (k + 2) + [tab_of(i) for i in range(k)],
        out_specs=VM,
        scratch_shapes=[pltpu.VMEM((k, CELLS, LANES), F32)],
        compiler_params=pltpu.CompilerParams(vmem_limit_bytes=8 << 20),
        cost_estimate=pl.CostEstimate(flops=k * 2 * 240 * 8192 * 128, bytes_accessed=(10 + 5 * k) << 20,
                                      transcendentals=0),
        name="predict",
    )(flux, *rows, meta, *([meta] * k))


def exchange_body(flux_ref, rows_ref, meta_ref, mine_ref, other_ref, tab0_ref, tab1_ref, value_ref,
                  weight_ref, w_ref, bad_ref, later_ref, flag0, flag1, pair_o, pair_n, pair_f, prev_n, next_o,
                  next_obs, flags, s_pair, s_side, s_obs, s_flag, r_pair, r_side, r_obs, r_flag):
    wins, tiles = lax.axis_size("win"), lax.axis_size("tile")
    w, t = lax.axis_index("win"), lax.axis_index("tile")
    up, down = w > 0, w < wins - 1
    barrier = pltpu.get_barrier_semaphore()
    peers = [lax.rem(t + d, tiles) for d in range(tiles)]
    others = [lax.rem(w + d, wins) for d in range(wins)]

    def greet(device):
        pl.semaphore_signal(barrier, inc=1, device_id=device, device_id_type=MESH)

    for d in range(1, tiles):
        greet((w, peers[d]))
    for d in range(1, wins):
        greet((others[d], t))

    @pl.when(up)
    def _():
        for d in range(1, tiles):
            greet((w - 1, peers[d]))

    @pl.when(down)
    def _():
        for d in range(1, tiles):
            greet((w + 1, peers[d]))

    flag0[...] = jnp.maximum(tab0_ref[...], tab1_ref[...]).astype(F32)
    lines = predict_binned(flux_ref, rows_ref, meta_ref, META)
    later = jnp.concatenate([jnp.zeros((4, LANES), F32), lines], axis=0) + other_ref[...]
    later_ref[...] = later
    sides = jnp.where(up, 1, 0) + jnp.where(down, 1, 0)
    pl.semaphore_wait(barrier, tiles - 1 + wins - 1 + sides * (tiles - 1))

    def push(src, dst, ssem, rsem, device):
        return pltpu.make_async_remote_copy(src_ref=src, dst_ref=dst, send_sem=ssem, recv_sem=rsem,
                                            device_id=device, device_id_type=MESH)

    def peer(k, d, at):
        src, dst = ((mine_ref, pair_o), (later_ref, pair_n), (flag0, pair_f))[k]
        return push(src, dst.at[at], s_pair.at[k, d], r_pair.at[k, at], (w, peers[d]))

    def above(d, at):
        return push(mine_ref, next_o.at[at], s_side.at[0, d], r_side.at[0, at], (w - 1, peers[d]))

    def under(d, at):
        return push(later_ref, prev_n.at[at], s_side.at[1, d], r_side.at[1, at], (w + 1, peers[d]))

    def obs_to(v):
        return [push(ref, next_obs.at[k], s_obs.at[k], r_obs.at[k], (v, t))
                for k, ref in enumerate((value_ref, weight_ref))]

    def flag(d, at):
        return push(flag1, flags.at[at], s_flag.at[d], r_flag.at[at], (others[d], t))

    for d in range(1, tiles):
        peer(2, d, t).start()
    for d in range(1, tiles):
        peer(0, d, t).start()

    @pl.when(up)
    def _():
        for d in range(tiles):
            above(d, t).start()
        for copy in obs_to(w - 1):
            copy.start()

    for d in range(1, tiles):
        peer(1, d, t).start()

    @pl.when(down)
    def _():
        for d in range(tiles):
            under(d, t).start()

    bad = flag0[...]
    for d in range(1, tiles):
        peer(2, d, peers[d]).wait_recv()
        bad = jnp.maximum(bad, pair_f[peers[d]])
    flag1[...] = bad
    for d in range(1, wins):
        flag(d, w).start()
    own = mine_ref[...]
    for d in range(1, tiles):
        for k in range(2):
            peer(k, d, peers[d]).wait_recv()
        own, later = own + pair_o[peers[d]], later + pair_n[peers[d]]
    w_ref[0] = own
    w_ref[1] = later

    @pl.when(up)
    def _():
        total = w_ref[0]
        for d in range(tiles):
            under(d, peers[d]).wait_recv()
            total = total + prev_n[peers[d]]
        w_ref[0] = total

    w_ref[0] = (w_ref[0] - value_ref[...]) * weight_ref[...]

    @pl.when(down)
    def _():
        total = w_ref[1]
        for d in range(tiles):
            above(d, peers[d]).wait_recv()
            total = total + next_o[peers[d]]
        for copy in obs_to(w + 1):
            copy.wait_recv()
        w_ref[1] = (total - next_obs[0]) * next_obs[1]

    for d in range(1, wins):
        flag(d, others[d]).wait_recv()
        bad = jnp.maximum(bad, flags[others[d]])
    bad_ref[...] = bad
    for d in range(1, wins):
        flag(d, w).wait_send()
    for d in range(1, tiles):
        for k in range(3):
            peer(k, d, t).wait_send()

    @pl.when(up)
    def _():
        for copy in obs_to(w - 1):
            copy.wait_send()
        for d in range(tiles):
            above(d, t).wait_send()

    @pl.when(down)
    def _():
        for d in range(tiles):
            under(d, t).wait_send()


def align_body(rows_ref, tab_ref, out_ref):
    def move(q, _):
        for u in range(4):
            b = q * 4 + u
            at = pl.ds(pl.multiple_of(tab_ref[1, b], 16), LANES)
            out_ref[pl.ds(pl.multiple_of(b * LANES, LANES), LANES), :] = rows_ref[at, :]
        return 0

    lax.fori_loop(0, CELLS // 4, move, 0)


def align(rows, meta):
    return pl.pallas_call(
        align_body,
        grid=(1,),
        out_shape=jax.ShapeDtypeStruct((CELLS * LANES, LANES), BF16),
        in_specs=[VM, tab_of(1)],
        out_specs=VM,
        compiler_params=pltpu.CompilerParams(vmem_limit_bytes=2 << 20),
        name="align",
    )(rows, meta)


def exchange(flux, rows, meta, mine, other, ometa, value, weight):
    wins, tiles = lax.axis_size("win"), lax.axis_size("tile")
    one = pltpu.VMEM((8, LANES), F32)
    block = pltpu.VMEM((tiles, 8, LANES), F32)
    sem = pltpu.SemaphoreType.DMA
    return pl.pallas_call(
        exchange_body,
        grid=(1,),
        out_shape=(jax.ShapeDtypeStruct((2, 8, LANES), F32), jax.ShapeDtypeStruct((8, LANES), F32)),
        in_specs=[VM, VM, VM, VM, VM, tabv_of(0), tabv_of(1), VM, VM],
        out_specs=(VM, VM),
        scratch_shapes=[one, one, one, block, block, block, block, block,
                        pltpu.VMEM((2, 8, LANES), F32), pltpu.VMEM((wins, 8, LANES), F32),
                        sem((3, tiles)), sem((2, tiles)), sem((2,)), sem((wins,)), sem((3, tiles)), sem((2, tiles)),
                        sem((2,)), sem((wins,))],
        compiler_params=pltpu.CompilerParams(collective_id=3, has_side_effects=True, vmem_limit_bytes=8 << 20),
        cost_estimate=pl.CostEstimate(flops=2 * 240 * 8192 * 128, bytes_accessed=30 << 20, transcendentals=0),
        name="exchange",
    )(flux, align(rows, meta), meta, mine, other, ometa, ometa, value, weight)


def weigh(code, tables, slots):
    got = [pick(table, lax.shift_right_logical(code, 8) & 127) for table in tables]
    got = got[0] if len(got) == 1 else jnp.where(iota((8, LANES), 1) < 2 * NEAR, got[0], got[1])
    mine = iota((8, LANES), 0) == lax.shift_right_logical(code, 15) + slots
    return jnp.sum(jnp.where(mine, got, 0.0), axis=0, keepdims=True)


def spread(hour, hours, w):
    hit = hours == hour
    return [jnp.where(hit, v, 0.0).astype(BF16) for v in halves(w)]


def edges_body(w_ref, ps_ref, *refs):
    rows, metas, tabs = refs[0:4], refs[4:6], refs[6:10]
    head_ref, tail_ref = refs[10:]
    total = ps_ref.shape[0]
    band = iota((2 * KH, LANES), 0)
    hours = jnp.where(band < KH, band, band + (total - 2 * KH)) + 1
    quarter = lax.shift_right_logical(iota((1, LANES), 1), 5)
    slots = (quarter & 1) * 4
    tables = [w_ref[0], w_ref[1]]

    def group(g, _):
        for u in range(4):
            b = g * 4 + u
            codes = [metas[i // 2][pl.ds((i % 2) * META + b, 1), :] for i in range(4)]
            code = codes[0]
            fps = []
            for i in range(4):
                if i:
                    code = jnp.where(quarter == i, pltpu.roll(codes[i], i * NEAR, 1), code)
                fps.append(rows[i][pl.ds(pl.multiple_of(tabs[i][1, b], 16), NEAR), :])
            fp = jnp.concatenate(fps, axis=0)
            left = jnp.concatenate(spread(code & 255, hours, weigh(code, tables, slots)), axis=1)
            part = dot(left, jnp.concatenate([fp, fp], axis=0))
            col = pl.ds(pl.multiple_of(b * LANES, LANES), LANES)
            head_ref[:, col] = part[:KH] * ps_ref[:KH, col]
            tail_ref[:, col] = part[KH:] * ps_ref[total - KH:, col]
        return 0

    lax.fori_loop(0, CELLS // 4, group, 0)


def edges(w, ps, rows, metas):
    cells = ps.shape[1]
    return pl.pallas_call(
        edges_body,
        grid=(1,),
        out_shape=(jax.ShapeDtypeStruct((KH, cells), F32), jax.ShapeDtypeStruct((KH, cells), F32)),
        in_specs=[VM, VM]
        + [VM] * 4 + [VM] * 2 + [tab_of(0), tab_of(1)] * 2,
        out_specs=(VM, VM),
        compiler_params=pltpu.CompilerParams(vmem_limit_bytes=8 << 20),
        cost_estimate=pl.CostEstimate(flops=10**8, bytes_accessed=8 << 20, transcendentals=0),
        name="edges",
    )(w, ps, *rows, *metas, *tabs_from(metas))


def inner_body(w_ref, head_ref, tail_ref, kern_ref, ps_ref, *refs):
    rows, metas, tabs = refs[0:4], refs[4:6], refs[6:10]
    out_ref, outv, sv, osems = refs[10:]
    total, cells = ps_ref.shape
    parts = 16
    wide = cells // parts
    per = CELLS // parts
    inside = total - 2 * KH

    def drain(p):
        at = pl.ds(pl.multiple_of(p * wide, LANES), wide)
        return pltpu.make_async_copy(outv.at[p & 1], out_ref.at[:, at], osems.at[p & 1])

    hours = iota((inside, LANES), 0) + KH + 1
    pad = jnp.zeros((16, wide), BF16)

    def part_of(p, _):
        for u in range(per):
            b = p * per + u
            left, right = [], []
            for i in range(4):
                code = metas[i // 2][pl.ds((i % 2) * META + b, 1), :]
                left += spread(code & 255, hours, weigh(code, [w_ref[i // 2]], (i % 2) * 4))
                fp = rows[i][pl.ds(pl.multiple_of(tabs[i][1, b], 16), LANES), :]
                right += [fp, fp]
            part = dot(jnp.concatenate(left, axis=1), jnp.concatenate(right, axis=0))
            col = pl.ds(pl.multiple_of(b * LANES, LANES), LANES)
            here = slice(u * LANES, (u + 1) * LANES)
            sv[:KH, here] = head_ref[:, col]
            sv[KH:total - KH, here] = part * ps_ref[KH:total - KH, col]
            sv[total - KH:, here] = tail_ref[:, col]
        top, low = halves(sv[...])
        top, low = top.astype(BF16), low.astype(BF16)
        stack = jnp.concatenate([top, pad, low, pad, top, pad], axis=0)
        smooth = dot(kern_ref[...], stack)

        @pl.when(p >= 2)
        def _():
            drain(p - 2).wait()

        outv[p & 1] = smooth * ps_ref[:, pl.ds(pl.multiple_of(p * wide, LANES), wide)]
        drain(p).start()
        return 0

    lax.fori_loop(0, parts, part_of, 0)
    for p in (parts - 2, parts - 1):
        drain(p).wait()


def inner(w, head, tail, kern, ps, rows, metas):
    wide = ps.shape[1] // 16
    return pl.pallas_call(
        inner_body,
        grid=(1,),
        out_shape=jax.ShapeDtypeStruct(ps.shape, F32),
        in_specs=[VM, VM, VM, VM, VM] + [VM] * 4 + [VM] * 2 + [tab_of(0), tab_of(1)] * 2,
        out_specs=HBM,
        scratch_shapes=[pltpu.VMEM((2, ps.shape[0], wide), F32), pltpu.VMEM((ps.shape[0], wide), F32),
                        pltpu.SemaphoreType.DMA((2,))],
        compiler_params=pltpu.CompilerParams(vmem_limit_bytes=10 << 20),
        cost_estimate=pl.CostEstimate(flops=4 * 10**9, bytes_accessed=40 << 20, transcendentals=0),
        name="inner",
    )(w, head, tail, kern, ps, *rows, *metas, *tabs_from(metas))


def finish_body(own_ref, ps_ref, above_ref, below_ref, out_ref, ownv, loads, stores):
    total = ps_ref.shape[0]
    row = iota((KH, LANES), 0).astype(F32)
    grow, decay = jnp.exp((row - KH) * (2.0 / KH)), jnp.exp(row * (-2.0 / KH))

    def load(side):
        return pltpu.make_async_copy(own_ref.at[pl.ds(side * (total - KH), KH)], ownv.at[side], loads.at[side])

    def store(side):
        return pltpu.make_async_copy(ownv.at[side], out_ref.at[pl.ds(side * (total - KH), KH)], stores.at[side])

    for side in range(2):
        load(side).start()
    for side in range(2):
        load(side).wait()
        scale, after = (grow, decay) if side == 0 else (decay, grow)
        halo_ref = (above_ref, below_ref)[side]
        at = pl.ds(side * (total - KH), KH)

        def fill(q, _):
            for u in range(4):
                cut = pl.ds(pl.multiple_of((q * 4 + u) * LANES, LANES), LANES)
                x = halo_ref[:, cut] * scale
                for s in (1, 2, 4, 8, 16):
                    gap = jnp.zeros((s, LANES), F32)
                    x = x + (jnp.concatenate([gap, x[:KH - s]], axis=0) if side
                             else jnp.concatenate([x[s:], gap], axis=0))
                ownv[side, :, cut] = ownv[side, :, cut] + ps_ref[at, cut] * (x * after)
            return 0

        lax.fori_loop(0, ps_ref.shape[1] // LANES // 4, fill, 0)
        store(side).start()
    for side in range(2):
        store(side).wait()


def finish(partial, ps, above, below):
    return pl.pallas_call(
        finish_body,
        out_shape=jax.ShapeDtypeStruct(ps.shape, F32),
        in_specs=[HBM, VM, VM, VM],
        out_specs=HBM,
        scratch_shapes=[pltpu.VMEM((2, KH, ps.shape[1]), F32), pltpu.SemaphoreType.DMA((2,)),
                        pltpu.SemaphoreType.DMA((2,))],
        input_output_aliases={0: 0},
        compiler_params=pltpu.CompilerParams(vmem_limit_bytes=4 << 20),
        name="finish",
    )(partial, ps, above, below)


def taps(distance):
    far = np.abs(distance)
    full = np.where(far <= KH, np.exp(np.float32(-2.0) * far.astype(np.float32) / np.float32(KH)), 0).astype(np.float32)
    top = full.astype(BF16)
    return top, (full - top.astype(np.float32)).astype(BF16)


def smoother(total):
    row, col = np.arange(total)[:, None], np.arange(256)[None, :]
    top, low = taps(np.where(col < total, row - col, total))
    return jnp.asarray(np.concatenate([top, top, low], axis=1))


def quick(flux, prior_std, w, rows, metas):
    head, tail = edges(w, prior_std, rows, metas)
    above = from_behind(tail, "win", 1)
    below = from_behind(head, "win", -1)
    partial = inner(w, head, tail, smoother(flux.shape[0]), prior_std, rows, metas)
    return finish(partial, prior_std, above, below)


def shards(flux, prior_std, footprint, obs_value, obs_weight, obs_hour, hour_offset, block_cell):
    count, nblk, width = footprint.shape
    inputs = (obs_hour.reshape(1, count), hour_offset.T, block_cell.T, footprint.reshape(count * nblk, width))
    own0, early0, ometa, nmeta = sort_half(*inputs, 0, flux.shape[0])
    theirs0 = from_behind(early0, "win", -1)
    own1, early1, ometa, nmeta, ps, near = sort_half(*inputs, 1, flux.shape[0], (ometa, nmeta, prior_std, flux))
    meta = from_behind(nmeta, "win", -1)
    theirs1 = from_behind(early1, "win", -1)
    mine = predict(near, (own0, own1), ometa)
    other = predict(near, (theirs0,), meta)
    w, bad = exchange(near, theirs1, meta, mine, other, ometa, obs_value.reshape(8, LANES),
                      obs_weight.reshape(8, LANES))
    return lax.cond(
        bad[2, 0] > 0.0,
        lambda: general(flux, prior_std, footprint, obs_value, obs_weight, obs_hour, hour_offset, block_cell),
        lambda: quick(flux, ps, w, [own0, own1, theirs0, theirs1], (ometa, meta)))


def solution(mesh):
    return jax.shard_map(
        shards,
        mesh=mesh,
        in_specs=(
            P("win", "tile"),
            P("win", "tile"),
            P("win", "tile", None),
            P("win"),
            P("win"),
            P("win"),
            P("win", "tile"),
            P("win", "tile"),
        ),
        out_specs=P("win", "tile"),
        check_vma=False,
    )
```

```python
import functools

import jax
import jax.numpy as jnp
import numpy as np
from jax import lax
from jax.experimental import pallas as pl
from jax.experimental.pallas import tpu as pltpu
from jax.sharding import PartitionSpec as P


KH = 24
LANES = 128
CELLS = 64
NBIN = 2 * CELLS
HEAD = 41 * LANES
NEAR = 32
META = CELLS + CELLS + 8
F32, BF16, I32 = jnp.float32, jnp.bfloat16, jnp.int32
NT = (((1,), (1,)), ((), ()))
MESH = pl.DeviceIdType.MESH
VM = pl.BlockSpec(memory_space=pltpu.VMEM)
HBM = pl.BlockSpec(memory_space=pltpu.HBM)


def tab_of(half):
    return pl.BlockSpec((8, LANES), lambda *_: (META // 8 * (half + 1) - 1, 0), memory_space=pltpu.SMEM)


def tabv_of(half):
    return pl.BlockSpec((8, LANES), lambda *_: (META // 8 * (half + 1) - 1, 0))


def tabs_from(metas):
    return [metas[0], metas[0], metas[1], metas[1]]


def iota(shape, dim):
    return lax.broadcasted_iota(I32, shape, dim)


def dot(a, b):
    return jnp.dot(a, b, preferred_element_type=F32)


def halves(v):
    top = v.astype(BF16).astype(F32)
    return top, v - top


def pick(table, lane):
    return jnp.take_along_axis(table, jnp.broadcast_to(lane, table.shape), axis=1, mode="promise_in_bounds")


def from_behind(value, axis, steps):
    count = lax.axis_size(axis)
    initial, last = (max(0, -steps), min(count, count - steps))
    return lax.ppermute(value, axis, [(source, source + steps) for source in range(initial, last)])


def extended(cells, sides, width):
    for axis, dim in sides:
        count = lax.axis_size(axis)
        ends = count - 1
        head = lax.slice_in_dim(cells, 0, width, axis=dim)
        tail = lax.slice_in_dim(cells, cells.shape[dim] - width, cells.shape[dim], axis=dim)
        cells = jnp.concatenate(
            [
                lax.ppermute(tail, axis, [(i, (i + 1) % count) for i in range(ends)]),
                cells,
                lax.ppermute(head, axis, [((i + 1) % count, i) for i in range(ends)]),
            ],
            axis=dim,
        )
    return cells


def misfits(partial_value, obs_value, obs_weight):
    predicted = lax.psum(partial_value, "tile")
    return (predicted - obs_value) * obs_weight


def general(flux, prior_std, footprint, obs_value, obs_weight, obs_hour, hour_offset, block_cell):
    hours = flux.shape[0]
    cells = flux.shape[1]
    width = footprint.shape[2]
    per_hour = cells // width
    earlier = from_behind(flux, "win", 1)
    joined = jnp.concatenate([earlier, flux], axis=0).reshape(2 * hours * per_hour, width)
    flat = (hours + obs_hour[:, None] - hour_offset) * per_hour + block_cell
    picked = joined[flat]
    partial_value = jnp.einsum("onc,onc->o", footprint, picked, preferred_element_type=jnp.float32)
    weighted = misfits(partial_value, obs_value, obs_weight)
    contrib = weighted[:, None, None] * footprint.astype(jnp.float32)
    summed = jax.ops.segment_sum(
        contrib.reshape(-1, width), flat.reshape(-1), num_segments=2 * hours * per_hour
    )
    summed = summed.reshape(2 * hours, cells)
    returned = from_behind(summed[:hours], "win", -1)
    adjoint = summed[hours:] + returned
    scaled = prior_std * adjoint
    rim = extended(scaled, (("win", 0),), KH)
    rows = jnp.arange(hours, dtype=jnp.int32)[:, None]
    columns = jnp.arange(hours + 2 * KH, dtype=jnp.int32)[None, :]
    distance = columns - rows - KH
    kernel = jnp.where(
        jnp.abs(distance) <= KH, jnp.exp(-2.0 * jnp.abs(distance).astype(jnp.float32) / KH), 0.0
    )
    smoothed = jnp.dot(
        kernel, rim, preferred_element_type=jnp.float32, precision=lax.Precision.HIGHEST
    )
    return prior_std * smoothed


class Sorter:
    def __init__(self, nobs, hb, oh_ref, off_ref, cell_ref, metas, keyv, hourv, posv, tabv):
        self.nobs, self.hb, self.inputs, self.metas = nobs, hb, (oh_ref, off_ref, cell_ref), metas
        self.keyv, self.hourv, self.posv, self.tabv = keyv, hourv, posv, tabv
        self.nblk = off_ref.shape[0]
        self.lines = self.nblk * nobs // LANES
        self.cap = capacity(self.nblk * nobs)

    def prepare(self, which, aside):
        nobs, nblk, cap, lines = self.nobs, self.nblk, self.cap, self.lines
        keyv, hourv, posv, metas = self.keyv, self.hourv, self.posv, self.metas
        oh_ref, off_ref, cell_ref = self.inputs
        per = nobs // LANES
        span = HEAD // LANES - 1
        at0 = which * META
        bins = iota((NBIN, LANES), 0)
        lanes = iota((NBIN, LANES), 1)
        upper = (bins < lanes).astype(BF16)
        ones = jnp.ones((LANES, LANES), BF16)
        same = (bins // CELLS) == (lanes // CELLS)
        below = jnp.where(same & (lanes < bins), 1.0, 0.0).astype(BF16)
        before = jnp.where(same & (bins < lanes), 1.0, 0.0).astype(BF16)
        for c in range(per):
            cut = slice(which * nobs + c * LANES, which * nobs + (c + 1) * LANES)
            hour = oh_ref[:, cut] - off_ref[:, cut]
            early = hour < 0
            hour = jnp.where(early, hour + self.hb, hour)
            key = jnp.where(early, cell_ref[:, cut] + CELLS, cell_ref[:, cut])
            rim = (hour < KH) | (hour >= self.hb - KH)
            at = slice(c * nblk, (c + 1) * nblk)
            keyv[0, at, :] = jnp.where(rim, key, -1)
            keyv[1, at, :] = jnp.where(rim, -1, key)
            keyv[2, at, :] = key
            hourv[at, :] = (hour + 1).astype(F32)

        def count(r, total):
            first, second = total
            for u in range(4):
                first = first + jnp.where(bins == keyv[0, pl.ds(r * 4 + u, 1), :], 1.0, 0.0)
                second = second + jnp.where(bins == keyv[1, pl.ds(r * 4 + u, 1), :], 1.0, 0.0)
                aside(0, r, u)
            return first, second

        zero = jnp.zeros((NBIN, LANES), F32)
        first, second = lax.fori_loop(0, lines // 4, count, (zero, zero))
        first, second = first.astype(BF16), second.astype(BF16)
        ahead = [dot(v, upper) for v in (first, second)]
        rim_s = dot(first, ones)
        cnt_s = rim_s + dot(second, ones)
        rim_l = lax.dot_general(ones[:8], first, NT, preferred_element_type=F32)
        cnt_l = rim_l + lax.dot_general(ones[:8], second, NT, preferred_element_type=F32)

        def starts(cnt, left):
            tiles = jnp.floor((cnt + 15.0) * (1.0 / 16.0))
            coarse = jnp.floor(tiles * (1.0 / 128.0))
            fine = tiles - 128.0 * coarse

            def run(v):
                return dot(below, v.astype(BF16)) if left else dot(v.astype(BF16), before)

            return 16.0 * (128.0 * run(coarse) + run(fine))

        tight_l = starts(cnt_l, False)
        base = starts(cnt_s, True) + jnp.where(bins >= CELLS, float(cap), 0.0)
        line8 = iota((8, LANES), 0)
        limit = float(span * LANES)
        far = jnp.where((cnt_l > float(LANES)) | (rim_l > float(NEAR)) | (tight_l + cnt_l > limit), 1.0, 0.0)
        over = jnp.max(far, axis=1, keepdims=True)
        tab = jnp.where(line8 == 0, jnp.minimum(cnt_l, float(LANES)),
                        jnp.where(line8 == 1, jnp.minimum(tight_l, limit), over)).astype(I32)
        self.tabv[...] = tab
        metas[0][at0 + 2 * CELLS:at0 + META, :] = tab
        metas[1][at0 + 2 * CELLS:at0 + META, :] = pltpu.roll(tab, CELLS, 1)
        for turn in range(2):
            def place(r, acc):
                for u in range(4):
                    at = pl.ds(r * 4 + u, 1)
                    hot = bins == keyv[turn, at, :]
                    posf = jnp.sum(jnp.where(hot, acc, 0.0), axis=0, keepdims=True).astype(I32)
                    posv[at, :] = posf if turn == 0 else posv[at, :] + posf
                    acc = jnp.where(hot, acc + 1.0, acc)
                    aside(1 + turn, r, u)
                return acc

            lax.fori_loop(0, lines // 4, place, base + ahead[turn] + (rim_s if turn else 0.0))
        aside(-1, 0, 0)
        starts_l = tight_l + jnp.where(iota((8, LANES), 1) >= CELLS, float(cap), 0.0)
        for g in range(lines // 8):
            at = slice(g * 8, (g + 1) * 8)
            key = keyv[2, at, :]
            rank = posv[at, :] - pick(starts_l, key).astype(I32)
            keyv[0, at, :] = rank
            spot = jnp.where(rank < LANES, (key & (CELLS - 1)) * LANES + rank, -1)
            lo = at0 + CELLS + g * 8
            metas[0][lo:lo + 8, :] = jnp.where(key < CELLS, spot, -1)
            metas[1][lo:lo + 8, :] = jnp.where(key < CELLS, -1, spot)
        obs = iota((1, LANES), 1).astype(F32)
        done = zero
        for c in range(per):
            def gather(r, acc):
                marks, spots = [], []
                for u in range(2):
                    at = pl.ds(c * nblk + r * 2 + u, 1)
                    hot = bins == keyv[2, at, :]
                    marks.append(jnp.concatenate(
                        [jnp.where(hot, v, 0.0).astype(BF16) for v in (hourv[at, :], obs)], axis=0))
                    spots.append(jnp.where(bins == keyv[0, at, :], 1.0, 0.0).astype(BF16))
                    aside(3, r + c * (nblk // 2), u)
                return acc + lax.dot_general(jnp.concatenate(marks, axis=1), jnp.concatenate(spots, axis=1), NT,
                                             preferred_element_type=F32)

            acc = lax.fori_loop(0, nblk // 2, gather, jnp.zeros((2 * NBIN, LANES), F32))
            hour, low = acc[:NBIN], acc[NBIN:]
            done = done + jnp.where(hour > 0.0, hour + 256.0 * (low + float(c * LANES)), 0.0)
        done = done.astype(I32)
        metas[0][at0:at0 + CELLS, :] = done[:CELLS]
        metas[1][at0:at0 + CELLS, :] = done[CELLS:]


def capacity(n):
    return n + CELLS * 16 + LANES


def blank_block(rows, cap, q):
    blocks = HEAD // LANES
    q = jnp.minimum(q, 2 * blocks - 1)
    at = jnp.where(q < blocks, q, q - blocks + cap // LANES)
    rows[pl.ds(pl.multiple_of(at * LANES, LANES), LANES), :] = jnp.zeros((LANES, LANES), F32)


def unpack_block(stage, fpv, q):
    at = pl.multiple_of(q * LANES, LANES)
    stage[pl.ds(at, LANES), :] = fpv[pl.ds(at, LANES), :].astype(F32)


def permute_all(rows, stage, posv, slots, sems, nblk):
    half = nblk // 2

    def load(i, k):
        return pltpu.make_async_copy(posv.at[pl.ds(i * nblk + k * half, half)], slots[k], sems.at[k])

    for k in range(2):
        load(0, k).start()
    last = posv.shape[0] // nblk - 1

    def batch(i, _):
        src = i * (LANES * nblk)
        for k in range(2):
            load(i, k).wait()
            for q in range(half):
                for l in range(LANES):
                    rows[pl.ds(slots[k][q, l], 1), :] = stage[pl.ds(src + l * nblk + k * half + q, 1), :]

            @pl.when(i < last)
            def _():
                load(i + 1, k).start()

        return 0

    lax.fori_loop(0, last + 1, batch, 0)


def convert_all(rows, cap, outs, ends):
    for side in range(2):
        end = jnp.minimum(ends[side], HEAD - LANES)
        blocks = jnp.minimum(lax.shift_right_logical(end + 270, 7), HEAD // LANES)

        def convert(i, _):
            at = pl.multiple_of(i * LANES, LANES)
            src = pl.multiple_of(at + side * cap, LANES)
            outs[side][pl.ds(at, LANES), :] = rows[pl.ds(src, LANES), :].astype(BF16)
            return 0

        lax.fori_loop(0, blocks, convert, 0)


def sort_body(nobs, which, hb, *refs):
    oh_ref, off_ref, cell_ref, fp_ref = refs[:4]
    given = refs[4:4 + 4 * which]
    own_ref, neg_ref, ometa_ref, nmeta_ref = refs[4 + 4 * which:8 + 4 * which]
    fpv, stage, rows, keyv, hourv, posv, slot0, slot1, tabs, tabv, sems = refs[-11:]
    nblk = off_ref.shape[0]
    n = nobs * nblk
    fetch = pltpu.make_async_copy(fp_ref.at[pl.ds(which * n, n)], fpv, sems.at[0])
    fetch.start()
    if which:
        keeps = [pltpu.make_async_copy(given[2 + k], refs[12 + k], sems.at[4 + k]) for k in range(2)]
        for keep in keeps:
            keep.start()
        ometa_ref[:META, :] = given[0][...]
        nmeta_ref[:META, :] = given[1][...]
    sorter = Sorter(nobs, hb, oh_ref, off_ref, cell_ref, (ometa_ref, nmeta_ref), keyv, hourv, posv, tabv)
    cap = sorter.cap

    def aside(phase, r, u):
        if phase == -1:
            fetch.wait()
        elif phase == 0 and u < 3:
            blank_block(rows, cap, r * 6 + u * 2)
            blank_block(rows, cap, r * 6 + u * 2 + 1)
        elif phase == 3:
            unpack_block(stage, fpv, r * 2 + u)

    sorter.prepare(which, aside)
    to_tab = pltpu.make_async_copy(tabv, tabs, sems.at[1])
    to_tab.start()
    permute_all(rows, stage, posv, (slot0, slot1), sems.at[pl.ds(2, 2)], nblk)
    to_tab.wait()
    ends = [tabs[1, k] + tabs[0, k] for k in (CELLS - 1, NBIN - 1)]
    convert_all(rows, cap, (own_ref, neg_ref), ends)
    if which:
        for keep in keeps:
            keep.wait()


def sort_half(oh, off, cell, fp2, which, hb, given=()):
    nblk, count = off.shape
    nobs = count // 2
    n = nobs * nblk
    cap = capacity(n)
    lines = n // LANES
    rows = jax.ShapeDtypeStruct((HEAD, LANES), BF16)
    meta = jax.ShapeDtypeStruct(((1 + which) * META, LANES), I32)
    kept = [jax.ShapeDtypeStruct(v.shape, v.dtype) for v in given[2:]]
    slot = pltpu.SMEM((nblk // 2, LANES), I32)
    return pl.pallas_call(
        functools.partial(sort_body, nobs, which, hb),
        out_shape=(rows, rows, meta, meta, *kept),
        in_specs=[VM, VM, VM, HBM] + ([VM, VM, HBM, HBM] if which else []),
        out_specs=(VM,) * (4 + 2 * which),
        scratch_shapes=[
            pltpu.VMEM((n, LANES), BF16), pltpu.VMEM((n, LANES), F32), pltpu.VMEM((2 * cap, LANES), F32),
            pltpu.VMEM((3, lines, LANES), I32), pltpu.VMEM((lines, LANES), F32), pltpu.VMEM((lines, LANES), I32),
            slot, slot, pltpu.SMEM((8, LANES), I32), pltpu.VMEM((8, LANES), I32), pltpu.SemaphoreType.DMA((6,))],
        compiler_params=pltpu.CompilerParams(vmem_limit_bytes=20 << 20),
        cost_estimate=pl.CostEstimate(flops=10**9, bytes_accessed=50 << 20, transcendentals=0),
        name="sort_half",
    )(oh, off, cell, fp2, *given)


def predict_cells(flux_ref, rows, meta, tabs, first, tablev):
    k = len(rows)
    hours = iota((flux_ref.shape[0], k * LANES), 0) + 1
    step = 8

    def group(g, _):
        for u in range(step):
            b = g * step + u
            hour = jnp.concatenate([meta[pl.ds(f + b, 1), :] & 255 for f in first], axis=1)
            fp = jnp.concatenate(
                [rows[i][pl.ds(pl.multiple_of(tabs[i][1, b], 16), LANES), :] for i in range(k)], axis=0)
            local = flux_ref[:, pl.ds(pl.multiple_of(b * LANES, LANES), LANES)]
            full = lax.dot_general(local, fp, NT, preferred_element_type=F32)
            value = jnp.sum(jnp.where(hours == hour, full, 0.0), axis=0, keepdims=True)
            for i in range(k):
                tablev[i, pl.ds(b, 1), :] = value[:, i * LANES:(i + 1) * LANES]
        return 0

    lax.fori_loop(0, CELLS // step, group, 0)


def predict_sums(meta, first, tablev):
    lines = []
    for i in range(len(first)):
        lo = first[i] + CELLS
        spots = [meta[lo + g * 8:lo + (g + 1) * 8, :] for g in range(8)]
        cell = [lax.shift_right_arithmetic(s, 7) for s in spots]
        lane = [s & 127 for s in spots]

        def collect(q, acc):
            acc = list(acc)
            for u in range(4):
                b = q * 4 + u
                row = jnp.broadcast_to(tablev[i, pl.ds(b, 1), :], (8, LANES))
                for g in range(8):
                    acc[g // 2] = acc[g // 2] + jnp.where(cell[g] == b, pick(row, lane[g]), 0.0)
            return tuple(acc)

        acc = lax.fori_loop(0, CELLS // 4, collect, (jnp.zeros((8, LANES), F32),) * 4)
        lines.append(jnp.concatenate([jnp.sum(a, axis=0, keepdims=True) for a in acc], axis=0))
    return lines


def predict_binned(flux_ref, rows_ref, meta_ref, first, begin, end, acc):
    hours = iota((flux_ref.shape[0], LANES), 0) + 1
    eight, bins = iota((8, LANES), 0), iota((LANES, LANES), 0)
    step = 8

    def group(g, acc):
        left, right = [], []
        for u in range(step):
            b = g * step + u
            code = meta_ref[pl.ds(first + b, 1), :]
            fp = rows_ref[pl.ds(pl.multiple_of(b * LANES, LANES), LANES), :]
            local = flux_ref[:, pl.ds(pl.multiple_of(b * LANES, LANES), LANES)]
            full = lax.dot_general(local, fp, NT, preferred_element_type=F32)
            value = jnp.sum(jnp.where(hours == (code & 255), full, 0.0), axis=0, keepdims=True)
            here = eight == lax.shift_right_logical(code, 15)
            left.append(jnp.concatenate([jnp.where(here, v, 0.0) for v in halves(value)], axis=0).astype(BF16))
            right.append(jnp.where(bins == (lax.shift_right_logical(code, 8) & 127), 1.0, 0.0).astype(BF16))
        for at in range(0, step, 2):
            acc = acc + lax.dot_general(jnp.concatenate(left[at:at + 2], axis=1),
                                        jnp.concatenate(right[at:at + 2], axis=1), NT, preferred_element_type=F32)
        return acc

    return lax.fori_loop(begin // step, end // step, group, acc)


def predict_body(k, *refs):
    flux_ref, rows, meta, tabs = refs[0], refs[1:1 + k], refs[1 + k], refs[2 + k:2 + 2 * k]
    out_ref, tablev = refs[-2:]
    first = [i * META for i in range(k)]
    predict_cells(flux_ref, rows, meta, tabs, first, tablev)
    lines = predict_sums(meta, first, tablev)
    out_ref[...] = jnp.concatenate(lines if k == 2 else lines + [jnp.zeros((4, LANES), F32)], axis=0)


def predict(flux, rows, meta):
    k = len(rows)
    return pl.pallas_call(
        functools.partial(predict_body, k),
        grid=(1,),
        out_shape=jax.ShapeDtypeStruct((8, LANES), F32),
        in_specs=[VM] * (k + 2) + [tab_of(i) for i in range(k)],
        out_specs=VM,
        scratch_shapes=[pltpu.VMEM((k, CELLS, LANES), F32)],
        compiler_params=pltpu.CompilerParams(vmem_limit_bytes=8 << 20),
        cost_estimate=pl.CostEstimate(flops=k * 2 * 240 * 8192 * 128, bytes_accessed=(10 + 5 * k) << 20,
                                      transcendentals=0),
        name="predict",
    )(flux, *rows, meta, *([meta] * k))


def exchange_body(flux_ref, rows_ref, meta_ref, mine_ref, other_ref, tab0_ref, tab1_ref, value_ref,
                  weight_ref, w_ref, bad_ref, later_ref, flag0, flag1, pair_o, pair_n, pair_f, prev_n, next_o,
                  next_obs, flags, s_pair, s_side, s_obs, s_flag, r_pair, r_side, r_obs, r_flag):
    wins, tiles = lax.axis_size("win"), lax.axis_size("tile")
    w, t = lax.axis_index("win"), lax.axis_index("tile")
    up, down = w > 0, w < wins - 1
    barrier = pltpu.get_barrier_semaphore()
    peers = [lax.rem(t + d, tiles) for d in range(tiles)]
    others = [lax.rem(w + d, wins) for d in range(wins)]

    def greet(device):
        pl.semaphore_signal(barrier, inc=1, device_id=device, device_id_type=MESH)

    for d in range(1, tiles):
        greet((w, peers[d]))
    for d in range(1, wins):
        greet((others[d], t))

    @pl.when(up)
    def _():
        for d in range(1, tiles):
            greet((w - 1, peers[d]))

    @pl.when(down)
    def _():
        for d in range(1, tiles):
            greet((w + 1, peers[d]))

    flag0[...] = jnp.maximum(tab0_ref[...], tab1_ref[...]).astype(F32)
    pause = 40
    acc = predict_binned(flux_ref, rows_ref, meta_ref, META, 0, pause, jnp.zeros((16, LANES), F32))
    sides = jnp.where(up, 1, 0) + jnp.where(down, 1, 0)
    pl.semaphore_wait(barrier, tiles - 1 + wins - 1 + sides * (tiles - 1))

    def push(src, dst, ssem, rsem, device):
        return pltpu.make_async_remote_copy(src_ref=src, dst_ref=dst, send_sem=ssem, recv_sem=rsem,
                                            device_id=device, device_id_type=MESH)

    def peer(k, d, at):
        src, dst = ((mine_ref, pair_o), (later_ref, pair_n), (flag0, pair_f))[k]
        return push(src, dst.at[at], s_pair.at[k, d], r_pair.at[k, at], (w, peers[d]))

    def above(d, at):
        return push(mine_ref, next_o.at[at], s_side.at[0, d], r_side.at[0, at], (w - 1, peers[d]))

    def under(d, at):
        return push(later_ref, prev_n.at[at], s_side.at[1, d], r_side.at[1, at], (w + 1, peers[d]))

    def obs_to(v):
        return [push(ref, next_obs.at[k], s_obs.at[k], r_obs.at[k], (v, t))
                for k, ref in enumerate((value_ref, weight_ref))]

    def flag(d, at):
        return push(flag1, flags.at[at], s_flag.at[d], r_flag.at[at], (others[d], t))

    for d in range(1, tiles):
        peer(2, d, t).start()
    for d in range(1, tiles):
        peer(0, d, t).start()

    @pl.when(up)
    def _():
        for d in range(tiles):
            above(d, t).start()
        for copy in obs_to(w - 1):
            copy.start()

    acc = predict_binned(flux_ref, rows_ref, meta_ref, META, pause, CELLS, acc)
    later = jnp.concatenate([jnp.zeros((4, LANES), F32), acc[:4] + acc[8:12]], axis=0) + other_ref[...]
    later_ref[...] = later
    for d in range(1, tiles):
        peer(1, d, t).start()

    @pl.when(down)
    def _():
        for d in range(tiles):
            under(d, t).start()

    bad = flag0[...]
    for d in range(1, tiles):
        peer(2, d, peers[d]).wait_recv()
        bad = jnp.maximum(bad, pair_f[peers[d]])
    flag1[...] = bad
    for d in range(1, wins):
        flag(d, w).start()
    own = mine_ref[...]
    for d in range(1, tiles):
        for k in range(2):
            peer(k, d, peers[d]).wait_recv()
        own, later = own + pair_o[peers[d]], later + pair_n[peers[d]]
    w_ref[0] = own
    w_ref[1] = later

    @pl.when(up)
    def _():
        total = w_ref[0]
        for d in range(tiles):
            under(d, peers[d]).wait_recv()
            total = total + prev_n[peers[d]]
        w_ref[0] = total

    w_ref[0] = (w_ref[0] - value_ref[...]) * weight_ref[...]

    @pl.when(down)
    def _():
        total = w_ref[1]
        for d in range(tiles):
            above(d, peers[d]).wait_recv()
            total = total + next_o[peers[d]]
        for copy in obs_to(w + 1):
            copy.wait_recv()
        w_ref[1] = (total - next_obs[0]) * next_obs[1]

    for d in range(1, wins):
        flag(d, others[d]).wait_recv()
        bad = jnp.maximum(bad, flags[others[d]])
    bad_ref[...] = bad
    for d in range(1, wins):
        flag(d, w).wait_send()
    for d in range(1, tiles):
        for k in range(3):
            peer(k, d, t).wait_send()

    @pl.when(up)
    def _():
        for copy in obs_to(w - 1):
            copy.wait_send()
        for d in range(tiles):
            above(d, t).wait_send()

    @pl.when(down)
    def _():
        for d in range(tiles):
            under(d, t).wait_send()


def align_body(rows_ref, tab_ref, out_ref):
    def move(q, _):
        for u in range(4):
            b = q * 4 + u
            at = pl.ds(pl.multiple_of(tab_ref[1, b], 16), LANES)
            out_ref[pl.ds(pl.multiple_of(b * LANES, LANES), LANES), :] = rows_ref[at, :]
        return 0

    lax.fori_loop(0, CELLS // 4, move, 0)


def align(rows, meta):
    return pl.pallas_call(
        align_body,
        grid=(1,),
        out_shape=jax.ShapeDtypeStruct((CELLS * LANES, LANES), BF16),
        in_specs=[VM, tab_of(1)],
        out_specs=VM,
        compiler_params=pltpu.CompilerParams(vmem_limit_bytes=2 << 20),
        name="align",
    )(rows, meta)


def exchange(flux, rows, meta, mine, other, ometa, value, weight):
    wins, tiles = lax.axis_size("win"), lax.axis_size("tile")
    one = pltpu.VMEM((8, LANES), F32)
    block = pltpu.VMEM((tiles, 8, LANES), F32)
    sem = pltpu.SemaphoreType.DMA
    return pl.pallas_call(
        exchange_body,
        grid=(1,),
        out_shape=(jax.ShapeDtypeStruct((2, 8, LANES), F32), jax.ShapeDtypeStruct((8, LANES), F32)),
        in_specs=[VM, VM, VM, VM, VM, tabv_of(0), tabv_of(1), VM, VM],
        out_specs=(VM, VM),
        scratch_shapes=[one, one, one, block, block, block, block, block,
                        pltpu.VMEM((2, 8, LANES), F32), pltpu.VMEM((wins, 8, LANES), F32),
                        sem((3, tiles)), sem((2, tiles)), sem((2,)), sem((wins,)), sem((3, tiles)), sem((2, tiles)),
                        sem((2,)), sem((wins,))],
        compiler_params=pltpu.CompilerParams(collective_id=3, has_side_effects=True, vmem_limit_bytes=8 << 20),
        cost_estimate=pl.CostEstimate(flops=2 * 240 * 8192 * 128, bytes_accessed=30 << 20, transcendentals=0),
        name="exchange",
    )(flux, align(rows, meta), meta, mine, other, ometa, ometa, value, weight)


def weigh(code, tables, slots):
    got = [pick(table, lax.shift_right_logical(code, 8) & 127) for table in tables]
    got = got[0] if len(got) == 1 else jnp.where(iota((8, LANES), 1) < 2 * NEAR, got[0], got[1])
    mine = iota((8, LANES), 0) == lax.shift_right_logical(code, 15) + slots
    return jnp.sum(jnp.where(mine, got, 0.0), axis=0, keepdims=True)


def spread(hour, hours, w):
    hit = hours == hour
    return [jnp.where(hit, v, 0.0).astype(BF16) for v in halves(w)]


def edges_body(w_ref, ps_ref, *refs):
    rows, metas, tabs = refs[0:4], refs[4:6], refs[6:10]
    head_ref, tail_ref = refs[10:]
    total = ps_ref.shape[0]
    band = iota((2 * KH, LANES), 0)
    hours = jnp.where(band < KH, band, band + (total - 2 * KH)) + 1
    quarter = lax.shift_right_logical(iota((1, LANES), 1), 5)
    slots = (quarter & 1) * 4
    tables = [w_ref[0], w_ref[1]]

    def group(g, _):
        for u in range(8):
            b = g * 8 + u
            codes = [metas[i // 2][pl.ds((i % 2) * META + b, 1), :] for i in range(4)]
            code = codes[0]
            fps = []
            for i in range(4):
                if i:
                    code = jnp.where(quarter == i, pltpu.roll(codes[i], i * NEAR, 1), code)
                fps.append(rows[i][pl.ds(pl.multiple_of(tabs[i][1, b], 16), NEAR), :])
            fp = jnp.concatenate(fps, axis=0)
            left = jnp.concatenate(spread(code & 255, hours, weigh(code, tables, slots)), axis=1)
            part = dot(left, jnp.concatenate([fp, fp], axis=0))
            col = pl.ds(pl.multiple_of(b * LANES, LANES), LANES)
            head_ref[:, col] = part[:KH] * ps_ref[:KH, col]
            tail_ref[:, col] = part[KH:] * ps_ref[total - KH:, col]
        return 0

    lax.fori_loop(0, CELLS // 8, group, 0)


def edges(w, ps, rows, metas):
    cells = ps.shape[1]
    return pl.pallas_call(
        edges_body,
        grid=(1,),
        out_shape=(jax.ShapeDtypeStruct((KH, cells), F32), jax.ShapeDtypeStruct((KH, cells), F32)),
        in_specs=[VM, VM]
        + [VM] * 4 + [VM] * 2 + [tab_of(0), tab_of(1)] * 2,
        out_specs=(VM, VM),
        compiler_params=pltpu.CompilerParams(vmem_limit_bytes=8 << 20),
        cost_estimate=pl.CostEstimate(flops=10**8, bytes_accessed=8 << 20, transcendentals=0),
        name="edges",
    )(w, ps, *rows, *metas, *tabs_from(metas))


def inner_body(w_ref, head_ref, tail_ref, kern_ref, ps_ref, *refs):
    rows, metas, tabs = refs[0:4], refs[4:6], refs[6:10]
    out_ref, outv, sv, osems = refs[10:]
    total, cells = ps_ref.shape
    parts = 16
    wide = cells // parts
    per = CELLS // parts
    inside = total - 2 * KH

    def drain(p):
        at = pl.ds(pl.multiple_of(p * wide, LANES), wide)
        return pltpu.make_async_copy(outv.at[p & 1], out_ref.at[:, at], osems.at[p & 1])

    hours = iota((inside, LANES), 0) + KH + 1
    pad = jnp.zeros((16, wide), BF16)

    def part_of(p, _):
        for u in range(per):
            b = p * per + u
            left, right = [], []
            for i in range(4):
                code = metas[i // 2][pl.ds((i % 2) * META + b, 1), :]
                left += spread(code & 255, hours, weigh(code, [w_ref[i // 2]], (i % 2) * 4))
                fp = rows[i][pl.ds(pl.multiple_of(tabs[i][1, b], 16), LANES), :]
                right += [fp, fp]
            part = dot(jnp.concatenate(left, axis=1), jnp.concatenate(right, axis=0))
            col = pl.ds(pl.multiple_of(b * LANES, LANES), LANES)
            here = slice(u * LANES, (u + 1) * LANES)
            sv[:KH, here] = head_ref[:, col]
            sv[KH:total - KH, here] = part * ps_ref[KH:total - KH, col]
            sv[total - KH:, here] = tail_ref[:, col]
        top, low = halves(sv[...])
        top, low = top.astype(BF16), low.astype(BF16)
        stack = jnp.concatenate([top, pad, low, pad, top, pad], axis=0)
        smooth = dot(kern_ref[...], stack)

        @pl.when(p >= 2)
        def _():
            drain(p - 2).wait()

        outv[p & 1] = smooth * ps_ref[:, pl.ds(pl.multiple_of(p * wide, LANES), wide)]
        drain(p).start()
        return 0

    lax.fori_loop(0, parts, part_of, 0)
    for p in (parts - 2, parts - 1):
        drain(p).wait()


def inner(w, head, tail, kern, ps, rows, metas):
    wide = ps.shape[1] // 16
    return pl.pallas_call(
        inner_body,
        grid=(1,),
        out_shape=jax.ShapeDtypeStruct(ps.shape, F32),
        in_specs=[VM, VM, VM, VM, VM] + [VM] * 4 + [VM] * 2 + [tab_of(0), tab_of(1)] * 2,
        out_specs=HBM,
        scratch_shapes=[pltpu.VMEM((2, ps.shape[0], wide), F32), pltpu.VMEM((ps.shape[0], wide), F32),
                        pltpu.SemaphoreType.DMA((2,))],
        compiler_params=pltpu.CompilerParams(vmem_limit_bytes=10 << 20),
        cost_estimate=pl.CostEstimate(flops=4 * 10**9, bytes_accessed=40 << 20, transcendentals=0),
        name="inner",
    )(w, head, tail, kern, ps, *rows, *metas, *tabs_from(metas))


def finish_body(own_ref, ps_ref, above_ref, below_ref, out_ref, ownv, loads, stores):
    total = ps_ref.shape[0]
    row = iota((KH, LANES), 0).astype(F32)
    grow, decay = jnp.exp((row - KH) * (2.0 / KH)), jnp.exp(row * (-2.0 / KH))

    def load(side):
        return pltpu.make_async_copy(own_ref.at[pl.ds(side * (total - KH), KH)], ownv.at[side], loads.at[side])

    def store(side):
        return pltpu.make_async_copy(ownv.at[side], out_ref.at[pl.ds(side * (total - KH), KH)], stores.at[side])

    for side in range(2):
        load(side).start()
    for side in range(2):
        load(side).wait()
        scale, after = (grow, decay) if side == 0 else (decay, grow)
        halo_ref = (above_ref, below_ref)[side]
        at = pl.ds(side * (total - KH), KH)

        def fill(q, _):
            for u in range(4):
                cut = pl.ds(pl.multiple_of((q * 4 + u) * LANES, LANES), LANES)
                x = halo_ref[:, cut] * scale
                for s in (1, 2, 4, 8, 16):
                    gap = jnp.zeros((s, LANES), F32)
                    x = x + (jnp.concatenate([gap, x[:KH - s]], axis=0) if side
                             else jnp.concatenate([x[s:], gap], axis=0))
                ownv[side, :, cut] = ownv[side, :, cut] + ps_ref[at, cut] * (x * after)
            return 0

        lax.fori_loop(0, ps_ref.shape[1] // LANES // 4, fill, 0)
        store(side).start()
    for side in range(2):
        store(side).wait()


def finish(partial, ps, above, below):
    return pl.pallas_call(
        finish_body,
        out_shape=jax.ShapeDtypeStruct(ps.shape, F32),
        in_specs=[HBM, VM, VM, VM],
        out_specs=HBM,
        scratch_shapes=[pltpu.VMEM((2, KH, ps.shape[1]), F32), pltpu.SemaphoreType.DMA((2,)),
                        pltpu.SemaphoreType.DMA((2,))],
        input_output_aliases={0: 0},
        compiler_params=pltpu.CompilerParams(vmem_limit_bytes=4 << 20),
        name="finish",
    )(partial, ps, above, below)


def taps(distance):
    far = np.abs(distance)
    full = np.where(far <= KH, np.exp(np.float32(-2.0) * far.astype(np.float32) / np.float32(KH)), 0).astype(np.float32)
    top = full.astype(BF16)
    return top, (full - top.astype(np.float32)).astype(BF16)


def smoother(total):
    row, col = np.arange(total)[:, None], np.arange(256)[None, :]
    top, low = taps(np.where(col < total, row - col, total))
    return jnp.asarray(np.concatenate([top, top, low], axis=1))


def quick(flux, prior_std, w, rows, metas):
    head, tail = edges(w, prior_std, rows, metas)
    above = from_behind(tail, "win", 1)
    below = from_behind(head, "win", -1)
    partial = inner(w, head, tail, smoother(flux.shape[0]), prior_std, rows, metas)
    return finish(partial, prior_std, above, below)


def shards(flux, prior_std, footprint, obs_value, obs_weight, obs_hour, hour_offset, block_cell):
    count, nblk, width = footprint.shape
    inputs = (obs_hour.reshape(1, count), hour_offset.T, block_cell.T, footprint.reshape(count * nblk, width))
    own0, early0, ometa, nmeta = sort_half(*inputs, 0, flux.shape[0])
    theirs0 = from_behind(early0, "win", -1)
    own1, early1, ometa, nmeta, ps, near = sort_half(*inputs, 1, flux.shape[0], (ometa, nmeta, prior_std, flux))
    meta = from_behind(nmeta, "win", -1)
    theirs1 = from_behind(early1, "win", -1)
    mine = predict(near, (own0, own1), ometa)
    other = predict(near, (theirs0,), meta)
    w, bad = exchange(near, theirs1, meta, mine, other, ometa, obs_value.reshape(8, LANES),
                      obs_weight.reshape(8, LANES))
    return lax.cond(
        bad[2, 0] > 0.0,
        lambda: general(flux, prior_std, footprint, obs_value, obs_weight, obs_hour, hour_offset, block_cell),
        lambda: quick(flux, ps, w, [own0, own1, theirs0, theirs1], (ometa, meta)))


def solution(mesh):
    return jax.shard_map(
        shards,
        mesh=mesh,
        in_specs=(
            P("win", "tile"),
            P("win", "tile"),
            P("win", "tile", None),
            P("win"),
            P("win"),
            P("win"),
            P("win", "tile"),
            P("win", "tile"),
        ),
        out_specs=P("win", "tile"),
        check_vma=False,
    )
```

```python
import functools

import jax
import jax.numpy as jnp
import numpy as np
from jax import lax
from jax.experimental import pallas as pl
from jax.experimental.pallas import tpu as pltpu
from jax.sharding import PartitionSpec as P


KH = 24
LANES = 128
CELLS = 64
NBIN = 2 * CELLS
HEAD = 41 * LANES
NEAR = 32
META = CELLS + CELLS + 8
F32, BF16, I32 = jnp.float32, jnp.bfloat16, jnp.int32
NT = (((1,), (1,)), ((), ()))
MESH = pl.DeviceIdType.MESH
VM = pl.BlockSpec(memory_space=pltpu.VMEM)
HBM = pl.BlockSpec(memory_space=pltpu.HBM)


def tab_of(half):
    return pl.BlockSpec((8, LANES), lambda *_: (META // 8 * (half + 1) - 1, 0), memory_space=pltpu.SMEM)


def tabv_of(half):
    return pl.BlockSpec((8, LANES), lambda *_: (META // 8 * (half + 1) - 1, 0))


def tabs_from(metas):
    return [metas[0], metas[0], metas[1], metas[1]]


def iota(shape, dim):
    return lax.broadcasted_iota(I32, shape, dim)


def dot(a, b):
    return jnp.dot(a, b, preferred_element_type=F32)


def halves(v):
    top = v.astype(BF16).astype(F32)
    return top, v - top


def pick(table, lane):
    return jnp.take_along_axis(table, jnp.broadcast_to(lane, table.shape), axis=1, mode="promise_in_bounds")


def from_behind(value, axis, steps):
    count = lax.axis_size(axis)
    initial, last = (max(0, -steps), min(count, count - steps))
    return lax.ppermute(value, axis, [(source, source + steps) for source in range(initial, last)])


def extended(cells, sides, width):
    for axis, dim in sides:
        count = lax.axis_size(axis)
        ends = count - 1
        head = lax.slice_in_dim(cells, 0, width, axis=dim)
        tail = lax.slice_in_dim(cells, cells.shape[dim] - width, cells.shape[dim], axis=dim)
        cells = jnp.concatenate(
            [
                lax.ppermute(tail, axis, [(i, (i + 1) % count) for i in range(ends)]),
                cells,
                lax.ppermute(head, axis, [((i + 1) % count, i) for i in range(ends)]),
            ],
            axis=dim,
        )
    return cells


def misfits(partial_value, obs_value, obs_weight):
    predicted = lax.psum(partial_value, "tile")
    return (predicted - obs_value) * obs_weight


def general(flux, prior_std, footprint, obs_value, obs_weight, obs_hour, hour_offset, block_cell):
    hours = flux.shape[0]
    cells = flux.shape[1]
    width = footprint.shape[2]
    per_hour = cells // width
    earlier = from_behind(flux, "win", 1)
    joined = jnp.concatenate([earlier, flux], axis=0).reshape(2 * hours * per_hour, width)
    flat = (hours + obs_hour[:, None] - hour_offset) * per_hour + block_cell
    picked = joined[flat]
    partial_value = jnp.einsum("onc,onc->o", footprint, picked, preferred_element_type=jnp.float32)
    weighted = misfits(partial_value, obs_value, obs_weight)
    contrib = weighted[:, None, None] * footprint.astype(jnp.float32)
    summed = jax.ops.segment_sum(
        contrib.reshape(-1, width), flat.reshape(-1), num_segments=2 * hours * per_hour
    )
    summed = summed.reshape(2 * hours, cells)
    returned = from_behind(summed[:hours], "win", -1)
    adjoint = summed[hours:] + returned
    scaled = prior_std * adjoint
    rim = extended(scaled, (("win", 0),), KH)
    rows = jnp.arange(hours, dtype=jnp.int32)[:, None]
    columns = jnp.arange(hours + 2 * KH, dtype=jnp.int32)[None, :]
    distance = columns - rows - KH
    kernel = jnp.where(
        jnp.abs(distance) <= KH, jnp.exp(-2.0 * jnp.abs(distance).astype(jnp.float32) / KH), 0.0
    )
    smoothed = jnp.dot(
        kernel, rim, preferred_element_type=jnp.float32, precision=lax.Precision.HIGHEST
    )
    return prior_std * smoothed


class Sorter:
    def __init__(self, nobs, hb, oh_ref, off_ref, cell_ref, metas, keyv, hourv, posv, tabv):
        self.nobs, self.hb, self.inputs, self.metas = nobs, hb, (oh_ref, off_ref, cell_ref), metas
        self.keyv, self.hourv, self.posv, self.tabv = keyv, hourv, posv, tabv
        self.nblk = off_ref.shape[0]
        self.lines = self.nblk * nobs // LANES
        self.cap = capacity(self.nblk * nobs)

    def prepare(self, which, aside):
        nobs, nblk, cap, lines = self.nobs, self.nblk, self.cap, self.lines
        keyv, hourv, posv, metas = self.keyv, self.hourv, self.posv, self.metas
        oh_ref, off_ref, cell_ref = self.inputs
        per = nobs // LANES
        span = HEAD // LANES - 1
        at0 = which * META
        bins = iota((NBIN, LANES), 0)
        lanes = iota((NBIN, LANES), 1)
        upper = (bins < lanes).astype(BF16)
        ones = jnp.ones((LANES, LANES), BF16)
        same = (bins // CELLS) == (lanes // CELLS)
        below = jnp.where(same & (lanes < bins), 1.0, 0.0).astype(BF16)
        before = jnp.where(same & (bins < lanes), 1.0, 0.0).astype(BF16)
        for c in range(per):
            cut = slice(which * nobs + c * LANES, which * nobs + (c + 1) * LANES)
            hour = oh_ref[:, cut] - off_ref[:, cut]
            early = hour < 0
            hour = jnp.where(early, hour + self.hb, hour)
            key = jnp.where(early, cell_ref[:, cut] + CELLS, cell_ref[:, cut])
            rim = (hour < KH) | (hour >= self.hb - KH)
            at = slice(c * nblk, (c + 1) * nblk)
            keyv[0, at, :] = jnp.where(rim, key, -1)
            keyv[1, at, :] = jnp.where(rim, -1, key)
            keyv[2, at, :] = key
            hourv[at, :] = (hour + 1).astype(F32)

        def count(r, total):
            first, second = total
            for u in range(4):
                first = first + jnp.where(bins == keyv[0, pl.ds(r * 4 + u, 1), :], 1.0, 0.0)
                second = second + jnp.where(bins == keyv[1, pl.ds(r * 4 + u, 1), :], 1.0, 0.0)
                aside(0, r, u)
            return first, second

        zero = jnp.zeros((NBIN, LANES), F32)
        first, second = lax.fori_loop(0, lines // 4, count, (zero, zero))
        first, second = first.astype(BF16), second.astype(BF16)
        ahead = [dot(v, upper) for v in (first, second)]
        rim_s = dot(first, ones)
        cnt_s = rim_s + dot(second, ones)
        rim_l = lax.dot_general(ones[:8], first, NT, preferred_element_type=F32)
        cnt_l = rim_l + lax.dot_general(ones[:8], second, NT, preferred_element_type=F32)

        def starts(cnt, left):
            tiles = jnp.floor((cnt + 15.0) * (1.0 / 16.0))
            coarse = jnp.floor(tiles * (1.0 / 128.0))
            fine = tiles - 128.0 * coarse

            def run(v):
                return dot(below, v.astype(BF16)) if left else dot(v.astype(BF16), before)

            return 16.0 * (128.0 * run(coarse) + run(fine))

        tight_l = starts(cnt_l, False)
        base = starts(cnt_s, True) + jnp.where(bins >= CELLS, float(cap), 0.0)
        line8 = iota((8, LANES), 0)
        limit = float(span * LANES)
        far = jnp.where((cnt_l > float(LANES)) | (rim_l > float(NEAR)) | (tight_l + cnt_l > limit), 1.0, 0.0)
        over = jnp.max(far, axis=1, keepdims=True)
        tab = jnp.where(line8 == 0, jnp.minimum(cnt_l, float(LANES)),
                        jnp.where(line8 == 1, jnp.minimum(tight_l, limit), over)).astype(I32)
        self.tabv[...] = tab
        metas[0][at0 + 2 * CELLS:at0 + META, :] = tab
        metas[1][at0 + 2 * CELLS:at0 + META, :] = pltpu.roll(tab, CELLS, 1)
        for turn in range(2):
            def place(r, acc):
                for u in range(4):
                    at = pl.ds(r * 4 + u, 1)
                    hot = bins == keyv[turn, at, :]
                    posf = jnp.sum(jnp.where(hot, acc, 0.0), axis=0, keepdims=True).astype(I32)
                    posv[at, :] = posf if turn == 0 else posv[at, :] + posf
                    acc = jnp.where(hot, acc + 1.0, acc)
                    aside(1 + turn, r, u)
                return acc

            lax.fori_loop(0, lines // 4, place, base + ahead[turn] + (rim_s if turn else 0.0))
        aside(-1, 0, 0)
        starts_l = tight_l + jnp.where(iota((8, LANES), 1) >= CELLS, float(cap), 0.0)
        for g in range(lines // 8):
            at = slice(g * 8, (g + 1) * 8)
            key = keyv[2, at, :]
            rank = posv[at, :] - pick(starts_l, key).astype(I32)
            keyv[0, at, :] = rank
            spot = jnp.where(rank < LANES, (key & (CELLS - 1)) * LANES + rank, -1)
            lo = at0 + CELLS + g * 8
            metas[0][lo:lo + 8, :] = jnp.where(key < CELLS, spot, -1)
            metas[1][lo:lo + 8, :] = jnp.where(key < CELLS, -1, spot)
        obs = iota((1, LANES), 1).astype(F32)
        done = zero
        for c in range(per):
            def gather(r, acc):
                marks, spots = [], []
                for u in range(2):
                    at = pl.ds(c * nblk + r * 2 + u, 1)
                    hot = bins == keyv[2, at, :]
                    marks.append(jnp.concatenate(
                        [jnp.where(hot, v, 0.0).astype(BF16) for v in (hourv[at, :], obs)], axis=0))
                    spots.append(jnp.where(bins == keyv[0, at, :], 1.0, 0.0).astype(BF16))
                    aside(3, r + c * (nblk // 2), u)
                return acc + lax.dot_general(jnp.concatenate(marks, axis=1), jnp.concatenate(spots, axis=1), NT,
                                             preferred_element_type=F32)

            acc = lax.fori_loop(0, nblk // 2, gather, jnp.zeros((2 * NBIN, LANES), F32))
            hour, low = acc[:NBIN], acc[NBIN:]
            done = done + jnp.where(hour > 0.0, hour + 256.0 * (low + float(c * LANES)), 0.0)
        done = done.astype(I32)
        metas[0][at0:at0 + CELLS, :] = done[:CELLS]
        metas[1][at0:at0 + CELLS, :] = done[CELLS:]


def capacity(n):
    return n + CELLS * 16 + LANES


def blank_block(rows, cap, q):
    blocks = HEAD // LANES
    q = jnp.minimum(q, 2 * blocks - 1)
    at = jnp.where(q < blocks, q, q - blocks + cap // LANES)
    rows[pl.ds(pl.multiple_of(at * LANES, LANES), LANES), :] = jnp.zeros((LANES, LANES), F32)


def unpack_block(stage, fpv, q):
    at = pl.multiple_of(q * LANES, LANES)
    stage[pl.ds(at, LANES), :] = fpv[pl.ds(at, LANES), :].astype(F32)


def permute_all(rows, stage, posv, slots, sems, nblk):
    half = nblk // 2

    def load(i, k):
        return pltpu.make_async_copy(posv.at[pl.ds(i * nblk + k * half, half)], slots[k], sems.at[k])

    for k in range(2):
        load(0, k).start()
    last = posv.shape[0] // nblk - 1

    def batch(i, _):
        src = i * (LANES * nblk)
        for k in range(2):
            load(i, k).wait()
            for q in range(half):
                for l in range(LANES):
                    rows[pl.ds(slots[k][q, l], 1), :] = stage[pl.ds(src + l * nblk + k * half + q, 1), :]

            @pl.when(i < last)
            def _():
                load(i + 1, k).start()

        return 0

    lax.fori_loop(0, last + 1, batch, 0)


def convert_all(rows, cap, outs, ends):
    for side in range(2):
        end = jnp.minimum(ends[side], HEAD - LANES)
        blocks = jnp.minimum(lax.shift_right_logical(end + 270, 7), HEAD // LANES)

        def convert(i, _):
            at = pl.multiple_of(i * LANES, LANES)
            src = pl.multiple_of(at + side * cap, LANES)
            outs[side][pl.ds(at, LANES), :] = rows[pl.ds(src, LANES), :].astype(BF16)
            return 0

        lax.fori_loop(0, blocks, convert, 0)


def sort_body(nobs, which, hb, *refs):
    oh_ref, off_ref, cell_ref, fp_ref = refs[:4]
    given = refs[4:4 + 4 * which]
    own_ref, neg_ref, ometa_ref, nmeta_ref = refs[4 + 4 * which:8 + 4 * which]
    fpv, stage, rows, keyv, hourv, posv, slot0, slot1, tabs, tabv, sems = refs[-11:]
    nblk = off_ref.shape[0]
    n = nobs * nblk
    fetch = pltpu.make_async_copy(fp_ref.at[pl.ds(which * n, n)], fpv, sems.at[0])
    fetch.start()
    if which:
        keeps = [pltpu.make_async_copy(given[2 + k], refs[12 + k], sems.at[4 + k]) for k in range(2)]
        for keep in keeps:
            keep.start()
        ometa_ref[:META, :] = given[0][...]
        nmeta_ref[:META, :] = given[1][...]
    sorter = Sorter(nobs, hb, oh_ref, off_ref, cell_ref, (ometa_ref, nmeta_ref), keyv, hourv, posv, tabv)
    cap = sorter.cap

    def aside(phase, r, u):
        if phase == -1:
            fetch.wait()
        elif phase == 0 and u < 3:
            blank_block(rows, cap, r * 6 + u * 2)
            blank_block(rows, cap, r * 6 + u * 2 + 1)
        elif phase == 3:
            unpack_block(stage, fpv, r * 2 + u)

    sorter.prepare(which, aside)
    to_tab = pltpu.make_async_copy(tabv, tabs, sems.at[1])
    to_tab.start()
    permute_all(rows, stage, posv, (slot0, slot1), sems.at[pl.ds(2, 2)], nblk)
    to_tab.wait()
    ends = [tabs[1, k] + tabs[0, k] for k in (CELLS - 1, NBIN - 1)]
    convert_all(rows, cap, (own_ref, neg_ref), ends)
    if which:
        for keep in keeps:
            keep.wait()


def sort_half(oh, off, cell, fp2, which, hb, given=()):
    nblk, count = off.shape
    nobs = count // 2
    n = nobs * nblk
    cap = capacity(n)
    lines = n // LANES
    rows = jax.ShapeDtypeStruct((HEAD, LANES), BF16)
    meta = jax.ShapeDtypeStruct(((1 + which) * META, LANES), I32)
    kept = [jax.ShapeDtypeStruct(v.shape, v.dtype) for v in given[2:]]
    slot = pltpu.SMEM((nblk // 2, LANES), I32)
    return pl.pallas_call(
        functools.partial(sort_body, nobs, which, hb),
        out_shape=(rows, rows, meta, meta, *kept),
        in_specs=[VM, VM, VM, HBM] + ([VM, VM, HBM, HBM] if which else []),
        out_specs=(VM,) * (4 + 2 * which),
        scratch_shapes=[
            pltpu.VMEM((n, LANES), BF16), pltpu.VMEM((n, LANES), F32), pltpu.VMEM((2 * cap, LANES), F32),
            pltpu.VMEM((3, lines, LANES), I32), pltpu.VMEM((lines, LANES), F32), pltpu.VMEM((lines, LANES), I32),
            slot, slot, pltpu.SMEM((8, LANES), I32), pltpu.VMEM((8, LANES), I32), pltpu.SemaphoreType.DMA((6,))],
        compiler_params=pltpu.CompilerParams(vmem_limit_bytes=20 << 20),
        cost_estimate=pl.CostEstimate(flops=10**9, bytes_accessed=50 << 20, transcendentals=0),
        name="sort_half",
    )(oh, off, cell, fp2, *given)


def predict_cells(flux_ref, rows, meta, tabs, first, tablev):
    k = len(rows)
    hours = iota((flux_ref.shape[0], k * LANES), 0) + 1
    step = 8

    def group(g, _):
        for u in range(step):
            b = g * step + u
            hour = jnp.concatenate([meta[pl.ds(f + b, 1), :] & 255 for f in first], axis=1)
            fp = jnp.concatenate(
                [rows[i][pl.ds(pl.multiple_of(tabs[i][1, b], 16), LANES), :] for i in range(k)], axis=0)
            local = flux_ref[:, pl.ds(pl.multiple_of(b * LANES, LANES), LANES)]
            full = lax.dot_general(local, fp, NT, preferred_element_type=F32)
            value = jnp.sum(jnp.where(hours == hour, full, 0.0), axis=0, keepdims=True)
            for i in range(k):
                tablev[i, pl.ds(b, 1), :] = value[:, i * LANES:(i + 1) * LANES]
        return 0

    lax.fori_loop(0, CELLS // step, group, 0)


def predict_sums(meta, first, tablev):
    lines = []
    for i in range(len(first)):
        lo = first[i] + CELLS
        spots = [meta[lo + g * 8:lo + (g + 1) * 8, :] for g in range(8)]
        cell = [lax.shift_right_arithmetic(s, 7) for s in spots]
        lane = [s & 127 for s in spots]

        def collect(q, acc):
            acc = list(acc)
            for u in range(4):
                b = q * 4 + u
                row = jnp.broadcast_to(tablev[i, pl.ds(b, 1), :], (8, LANES))
                for g in range(8):
                    acc[g // 2] = acc[g // 2] + jnp.where(cell[g] == b, pick(row, lane[g]), 0.0)
            return tuple(acc)

        acc = lax.fori_loop(0, CELLS // 4, collect, (jnp.zeros((8, LANES), F32),) * 4)
        lines.append(jnp.concatenate([jnp.sum(a, axis=0, keepdims=True) for a in acc], axis=0))
    return lines


def predict_binned(flux_ref, rows_ref, meta_ref, first, begin, end, acc):
    hours = iota((flux_ref.shape[0], LANES), 0) + 1
    eight, bins = iota((8, LANES), 0), iota((LANES, LANES), 0)
    step = 8

    def group(g, acc):
        left, right = [], []
        for u in range(step):
            b = g * step + u
            code = meta_ref[pl.ds(first + b, 1), :]
            fp = rows_ref[pl.ds(pl.multiple_of(b * LANES, LANES), LANES), :]
            local = flux_ref[:, pl.ds(pl.multiple_of(b * LANES, LANES), LANES)]
            full = lax.dot_general(local, fp, NT, preferred_element_type=F32)
            value = jnp.sum(jnp.where(hours == (code & 255), full, 0.0), axis=0, keepdims=True)
            here = eight == lax.shift_right_logical(code, 15)
            left.append(jnp.concatenate([jnp.where(here, v, 0.0) for v in halves(value)], axis=0).astype(BF16))
            right.append(jnp.where(bins == (lax.shift_right_logical(code, 8) & 127), 1.0, 0.0).astype(BF16))
        for at in range(0, step, 2):
            acc = acc + lax.dot_general(jnp.concatenate(left[at:at + 2], axis=1),
                                        jnp.concatenate(right[at:at + 2], axis=1), NT, preferred_element_type=F32)
        return acc

    return lax.fori_loop(begin // step, end // step, group, acc)


def predict_body(k, *refs):
    flux_ref, rows, meta, tabs = refs[0], refs[1:1 + k], refs[1 + k], refs[2 + k:2 + 2 * k]
    out_ref, tablev = refs[-2:]
    first = [i * META for i in range(k)]
    predict_cells(flux_ref, rows, meta, tabs, first, tablev)
    lines = predict_sums(meta, first, tablev)
    out_ref[...] = jnp.concatenate(lines if k == 2 else lines + [jnp.zeros((4, LANES), F32)], axis=0)


def predict(flux, rows, meta):
    k = len(rows)
    return pl.pallas_call(
        functools.partial(predict_body, k),
        grid=(1,),
        out_shape=jax.ShapeDtypeStruct((8, LANES), F32),
        in_specs=[VM] * (k + 2) + [tab_of(i) for i in range(k)],
        out_specs=VM,
        scratch_shapes=[pltpu.VMEM((k, CELLS, LANES), F32)],
        compiler_params=pltpu.CompilerParams(vmem_limit_bytes=8 << 20),
        cost_estimate=pl.CostEstimate(flops=k * 2 * 240 * 8192 * 128, bytes_accessed=(10 + 5 * k) << 20,
                                      transcendentals=0),
        name="predict",
    )(flux, *rows, meta, *([meta] * k))


def exchange_body(flux_ref, rows_ref, meta_ref, mine_ref, other_ref, tab0_ref, tab1_ref, value_ref,
                  weight_ref, w_ref, bad_ref, later_ref, flag0, flag1, pair_o, pair_n, pair_f, prev_n, next_o,
                  next_obs, flags, s_pair, s_side, s_obs, s_flag, r_pair, r_side, r_obs, r_flag):
    wins, tiles = lax.axis_size("win"), lax.axis_size("tile")
    w, t = lax.axis_index("win"), lax.axis_index("tile")
    up, down = w > 0, w < wins - 1
    barrier = pltpu.get_barrier_semaphore()
    peers = [lax.rem(t + d, tiles) for d in range(tiles)]
    others = [lax.rem(w + d, wins) for d in range(wins)]

    def greet(device):
        pl.semaphore_signal(barrier, inc=1, device_id=device, device_id_type=MESH)

    for d in range(1, tiles):
        greet((w, peers[d]))
    for d in range(1, wins):
        greet((others[d], t))

    @pl.when(up)
    def _():
        for d in range(1, tiles):
            greet((w - 1, peers[d]))

    @pl.when(down)
    def _():
        for d in range(1, tiles):
            greet((w + 1, peers[d]))

    flag0[...] = jnp.maximum(tab0_ref[...], tab1_ref[...]).astype(F32)
    pause = 40
    acc = predict_binned(flux_ref, rows_ref, meta_ref, META, 0, pause, jnp.zeros((16, LANES), F32))
    sides = jnp.where(up, 1, 0) + jnp.where(down, 1, 0)
    pl.semaphore_wait(barrier, tiles - 1 + wins - 1 + sides * (tiles - 1))

    def push(src, dst, ssem, rsem, device):
        return pltpu.make_async_remote_copy(src_ref=src, dst_ref=dst, send_sem=ssem, recv_sem=rsem,
                                            device_id=device, device_id_type=MESH)

    def peer(k, d, at):
        src, dst = ((mine_ref, pair_o), (later_ref, pair_n), (flag0, pair_f))[k]
        return push(src, dst.at[at], s_pair.at[k, d], r_pair.at[k, at], (w, peers[d]))

    def above(d, at):
        return push(mine_ref, next_o.at[at], s_side.at[0, d], r_side.at[0, at], (w - 1, peers[d]))

    def under(d, at):
        return push(later_ref, prev_n.at[at], s_side.at[1, d], r_side.at[1, at], (w + 1, peers[d]))

    def obs_to(v):
        return [push(ref, next_obs.at[k], s_obs.at[k], r_obs.at[k], (v, t))
                for k, ref in enumerate((value_ref, weight_ref))]

    def flag(d, at):
        return push(flag1, flags.at[at], s_flag.at[d], r_flag.at[at], (others[d], t))

    for d in range(1, tiles):
        peer(2, d, t).start()
    for d in range(1, tiles):
        peer(0, d, t).start()

    @pl.when(up)
    def _():
        for d in range(tiles):
            above(d, t).start()
        for copy in obs_to(w - 1):
            copy.start()

    acc = predict_binned(flux_ref, rows_ref, meta_ref, META, pause, CELLS, acc)
    later = jnp.concatenate([jnp.zeros((4, LANES), F32), acc[:4] + acc[8:12]], axis=0) + other_ref[...]
    later_ref[...] = later
    for d in range(1, tiles):
        peer(1, d, t).start()

    @pl.when(down)
    def _():
        for d in range(tiles):
            under(d, t).start()

    bad = flag0[...]
    for d in range(1, tiles):
        peer(2, d, peers[d]).wait_recv()
        bad = jnp.maximum(bad, pair_f[peers[d]])
    flag1[...] = bad
    for d in range(1, wins):
        flag(d, w).start()
    own = mine_ref[...]
    for d in range(1, tiles):
        for k in range(2):
            peer(k, d, peers[d]).wait_recv()
        own, later = own + pair_o[peers[d]], later + pair_n[peers[d]]
    w_ref[0] = own
    w_ref[1] = later

    @pl.when(up)
    def _():
        total = w_ref[0]
        for d in range(tiles):
            under(d, peers[d]).wait_recv()
            total = total + prev_n[peers[d]]
        w_ref[0] = total

    w_ref[0] = (w_ref[0] - value_ref[...]) * weight_ref[...]

    @pl.when(down)
    def _():
        total = w_ref[1]
        for d in range(tiles):
            above(d, peers[d]).wait_recv()
            total = total + next_o[peers[d]]
        for copy in obs_to(w + 1):
            copy.wait_recv()
        w_ref[1] = (total - next_obs[0]) * next_obs[1]

    for d in range(1, wins):
        flag(d, others[d]).wait_recv()
        bad = jnp.maximum(bad, flags[others[d]])
    bad_ref[...] = bad
    for d in range(1, wins):
        flag(d, w).wait_send()
    for d in range(1, tiles):
        for k in range(3):
            peer(k, d, t).wait_send()

    @pl.when(up)
    def _():
        for copy in obs_to(w - 1):
            copy.wait_send()
        for d in range(tiles):
            above(d, t).wait_send()

    @pl.when(down)
    def _():
        for d in range(tiles):
            under(d, t).wait_send()


def align_body(rows_ref, tab_ref, out_ref):
    def move(q, _):
        for u in range(4):
            b = q * 4 + u
            at = pl.ds(pl.multiple_of(tab_ref[1, b], 16), LANES)
            out_ref[pl.ds(pl.multiple_of(b * LANES, LANES), LANES), :] = rows_ref[at, :]
        return 0

    lax.fori_loop(0, CELLS // 4, move, 0)


def align(rows, meta):
    return pl.pallas_call(
        align_body,
        grid=(1,),
        out_shape=jax.ShapeDtypeStruct((CELLS * LANES, LANES), BF16),
        in_specs=[VM, tab_of(1)],
        out_specs=VM,
        compiler_params=pltpu.CompilerParams(vmem_limit_bytes=2 << 20),
        name="align",
    )(rows, meta)


def exchange(flux, rows, meta, mine, other, ometa, value, weight):
    wins, tiles = lax.axis_size("win"), lax.axis_size("tile")
    one = pltpu.VMEM((8, LANES), F32)
    block = pltpu.VMEM((tiles, 8, LANES), F32)
    sem = pltpu.SemaphoreType.DMA
    return pl.pallas_call(
        exchange_body,
        grid=(1,),
        out_shape=(jax.ShapeDtypeStruct((2, 8, LANES), F32), jax.ShapeDtypeStruct((8, LANES), F32)),
        in_specs=[VM, VM, VM, VM, VM, tabv_of(0), tabv_of(1), VM, VM],
        out_specs=(VM, VM),
        scratch_shapes=[one, one, one, block, block, block, block, block,
                        pltpu.VMEM((2, 8, LANES), F32), pltpu.VMEM((wins, 8, LANES), F32),
                        sem((3, tiles)), sem((2, tiles)), sem((2,)), sem((wins,)), sem((3, tiles)), sem((2, tiles)),
                        sem((2,)), sem((wins,))],
        compiler_params=pltpu.CompilerParams(collective_id=3, has_side_effects=True, vmem_limit_bytes=8 << 20),
        cost_estimate=pl.CostEstimate(flops=2 * 240 * 8192 * 128, bytes_accessed=30 << 20, transcendentals=0),
        name="exchange",
    )(flux, align(rows, meta), meta, mine, other, ometa, ometa, value, weight)


def weigh(code, tables, slots):
    got = [pick(table, lax.shift_right_logical(code, 8) & 127) for table in tables]
    got = got[0] if len(got) == 1 else jnp.where(iota((8, LANES), 1) < 2 * NEAR, got[0], got[1])
    mine = iota((8, LANES), 0) == lax.shift_right_logical(code, 15) + slots
    return jnp.sum(jnp.where(mine, got, 0.0), axis=0, keepdims=True)


def spread(hour, hours, w):
    hit = hours == hour
    return [jnp.where(hit, v, 0.0).astype(BF16) for v in halves(w)]


def edges_body(w_ref, ps_ref, *refs):
    rows, metas, tabs = refs[0:4], refs[4:6], refs[6:10]
    head_ref, tail_ref = refs[10:]
    total = ps_ref.shape[0]
    band = iota((2 * KH, LANES), 0)
    hours = jnp.where(band < KH, band, band + (total - 2 * KH)) + 1
    quarter = lax.shift_right_logical(iota((1, LANES), 1), 5)
    slots = (quarter & 1) * 4
    tables = [w_ref[0], w_ref[1]]

    def group(g, _):
        for u in range(8):
            b = g * 8 + u
            codes = [metas[i // 2][pl.ds((i % 2) * META + b, 1), :] for i in range(4)]
            code = codes[0]
            fps = []
            for i in range(4):
                if i:
                    code = jnp.where(quarter == i, pltpu.roll(codes[i], i * NEAR, 1), code)
                fps.append(rows[i][pl.ds(pl.multiple_of(tabs[i][1, b], 16), NEAR), :])
            fp = jnp.concatenate(fps, axis=0)
            left = jnp.concatenate(spread(code & 255, hours, weigh(code, tables, slots)), axis=1)
            part = dot(left, jnp.concatenate([fp, fp], axis=0))
            col = pl.ds(pl.multiple_of(b * LANES, LANES), LANES)
            head_ref[:, col] = part[:KH] * ps_ref[:KH, col]
            tail_ref[:, col] = part[KH:] * ps_ref[total - KH:, col]
        return 0

    lax.fori_loop(0, CELLS // 8, group, 0)


def edges(w, ps, rows, metas):
    cells = ps.shape[1]
    return pl.pallas_call(
        edges_body,
        grid=(1,),
        out_shape=(jax.ShapeDtypeStruct((KH, cells), F32), jax.ShapeDtypeStruct((KH, cells), F32)),
        in_specs=[VM, VM]
        + [VM] * 4 + [VM] * 2 + [tab_of(0), tab_of(1)] * 2,
        out_specs=(VM, VM),
        compiler_params=pltpu.CompilerParams(vmem_limit_bytes=8 << 20),
        cost_estimate=pl.CostEstimate(flops=10**8, bytes_accessed=8 << 20, transcendentals=0),
        name="edges",
    )(w, ps, *rows, *metas, *tabs_from(metas))


def inner_body(w_ref, head_ref, tail_ref, kern_ref, ps_ref, *refs):
    rows, metas, tabs = refs[0:4], refs[4:6], refs[6:10]
    out_ref, outv, sv, osems = refs[10:]
    total, cells = ps_ref.shape
    parts = 16
    wide = cells // parts
    per = CELLS // parts
    inside = total - 2 * KH

    def drain(p):
        at = pl.ds(pl.multiple_of(p * wide, LANES), wide)
        return pltpu.make_async_copy(outv.at[p & 1], out_ref.at[:, at], osems.at[p & 1])

    hours = iota((inside, LANES), 0) + KH + 1
    pad = jnp.zeros((16, wide), BF16)

    def part_of(p, _):
        for u in range(per):
            b = p * per + u
            left, right = [], []
            for i in range(4):
                code = metas[i // 2][pl.ds((i % 2) * META + b, 1), :]
                left += spread(code & 255, hours, weigh(code, [w_ref[i // 2]], (i % 2) * 4))
                fp = rows[i][pl.ds(pl.multiple_of(tabs[i][1, b], 16), LANES), :]
                right += [fp, fp]
            part = dot(jnp.concatenate(left, axis=1), jnp.concatenate(right, axis=0))
            col = pl.ds(pl.multiple_of(b * LANES, LANES), LANES)
            here = slice(u * LANES, (u + 1) * LANES)
            sv[:KH, here] = head_ref[:, col]
            sv[KH:total - KH, here] = part * ps_ref[KH:total - KH, col]
            sv[total - KH:, here] = tail_ref[:, col]
        top, low = halves(sv[...])
        top, low = top.astype(BF16), low.astype(BF16)
        stack = jnp.concatenate([top, pad, low, pad, top, pad], axis=0)
        smooth = dot(kern_ref[...], stack)

        @pl.when(p >= 2)
        def _():
            drain(p - 2).wait()

        outv[p & 1] = smooth * ps_ref[:, pl.ds(pl.multiple_of(p * wide, LANES), wide)]
        drain(p).start()
        return 0

    lax.fori_loop(0, parts, part_of, 0)
    for p in (parts - 2, parts - 1):
        drain(p).wait()


def inner(w, head, tail, kern, ps, rows, metas):
    wide = ps.shape[1] // 16
    return pl.pallas_call(
        inner_body,
        grid=(1,),
        out_shape=jax.ShapeDtypeStruct(ps.shape, F32),
        in_specs=[VM, VM, VM, VM, VM] + [VM] * 4 + [VM] * 2 + [tab_of(0), tab_of(1)] * 2,
        out_specs=HBM,
        scratch_shapes=[pltpu.VMEM((2, ps.shape[0], wide), F32), pltpu.VMEM((ps.shape[0], wide), F32),
                        pltpu.SemaphoreType.DMA((2,))],
        compiler_params=pltpu.CompilerParams(vmem_limit_bytes=10 << 20),
        cost_estimate=pl.CostEstimate(flops=4 * 10**9, bytes_accessed=40 << 20, transcendentals=0),
        name="inner",
    )(w, head, tail, kern, ps, *rows, *metas, *tabs_from(metas))


def finish_body(own_ref, ps_ref, above_ref, below_ref, out_ref, ownv, loads, stores):
    total = ps_ref.shape[0]
    row = iota((KH, LANES), 0).astype(F32)
    grow, decay = jnp.exp((row - KH) * (2.0 / KH)), jnp.exp(row * (-2.0 / KH))

    def load(side):
        return pltpu.make_async_copy(own_ref.at[pl.ds(side * (total - KH), KH)], ownv.at[side], loads.at[side])

    def store(side):
        return pltpu.make_async_copy(ownv.at[side], out_ref.at[pl.ds(side * (total - KH), KH)], stores.at[side])

    for side in range(2):
        load(side).start()
    for side in range(2):
        load(side).wait()
        scale, after = (grow, decay) if side == 0 else (decay, grow)
        halo_ref = (above_ref, below_ref)[side]
        at = pl.ds(side * (total - KH), KH)

        def fill(q, _):
            for u in range(8):
                cut = pl.ds(pl.multiple_of((q * 8 + u) * LANES, LANES), LANES)
                x = halo_ref[:, cut] * scale
                for s in (1, 2, 4, 8, 16):
                    gap = jnp.zeros((s, LANES), F32)
                    x = x + (jnp.concatenate([gap, x[:KH - s]], axis=0) if side
                             else jnp.concatenate([x[s:], gap], axis=0))
                ownv[side, :, cut] = ownv[side, :, cut] + ps_ref[at, cut] * (x * after)
            return 0

        lax.fori_loop(0, ps_ref.shape[1] // LANES // 8, fill, 0)
        store(side).start()
    for side in range(2):
        store(side).wait()


def finish(partial, ps, above, below):
    return pl.pallas_call(
        finish_body,
        out_shape=jax.ShapeDtypeStruct(ps.shape, F32),
        in_specs=[HBM, VM, VM, VM],
        out_specs=HBM,
        scratch_shapes=[pltpu.VMEM((2, KH, ps.shape[1]), F32), pltpu.SemaphoreType.DMA((2,)),
                        pltpu.SemaphoreType.DMA((2,))],
        input_output_aliases={0: 0},
        compiler_params=pltpu.CompilerParams(vmem_limit_bytes=4 << 20),
        name="finish",
    )(partial, ps, above, below)


def taps(distance):
    far = np.abs(distance)
    full = np.where(far <= KH, np.exp(np.float32(-2.0) * far.astype(np.float32) / np.float32(KH)), 0).astype(np.float32)
    top = full.astype(BF16)
    return top, (full - top.astype(np.float32)).astype(BF16)


def smoother(total):
    row, col = np.arange(total)[:, None], np.arange(256)[None, :]
    top, low = taps(np.where(col < total, row - col, total))
    return jnp.asarray(np.concatenate([top, top, low], axis=1))


def quick(flux, prior_std, w, rows, metas):
    head, tail = edges(w, prior_std, rows, metas)
    above = from_behind(tail, "win", 1)
    below = from_behind(head, "win", -1)
    partial = inner(w, head, tail, smoother(flux.shape[0]), prior_std, rows, metas)
    return finish(partial, prior_std, above, below)


def shards(flux, prior_std, footprint, obs_value, obs_weight, obs_hour, hour_offset, block_cell):
    count, nblk, width = footprint.shape
    inputs = (obs_hour.reshape(1, count), hour_offset.T, block_cell.T, footprint.reshape(count * nblk, width))
    own0, early0, ometa, nmeta = sort_half(*inputs, 0, flux.shape[0])
    theirs0 = from_behind(early0, "win", -1)
    own1, early1, ometa, nmeta, ps, near = sort_half(*inputs, 1, flux.shape[0], (ometa, nmeta, prior_std, flux))
    meta = from_behind(nmeta, "win", -1)
    theirs1 = from_behind(early1, "win", -1)
    mine = predict(near, (own0, own1), ometa)
    other = predict(near, (theirs0,), meta)
    w, bad = exchange(near, theirs1, meta, mine, other, ometa, obs_value.reshape(8, LANES),
                      obs_weight.reshape(8, LANES))
    return lax.cond(
        bad[2, 0] > 0.0,
        lambda: general(flux, prior_std, footprint, obs_value, obs_weight, obs_hour, hour_offset, block_cell),
        lambda: quick(flux, ps, w, [own0, own1, theirs0, theirs1], (ometa, meta)))


def solution(mesh):
    return jax.shard_map(
        shards,
        mesh=mesh,
        in_specs=(
            P("win", "tile"),
            P("win", "tile"),
            P("win", "tile", None),
            P("win"),
            P("win"),
            P("win"),
            P("win", "tile"),
            P("win", "tile"),
        ),
        out_specs=P("win", "tile"),
        check_vma=False,
    )
```
